256 devices in a mesh: wide: 32 (over z_hi, x, core), narrow: 8 (over z_lo, y).
Axes of the slice: x: 4, y: 4, z: 8 (z_hi: 4, z_lo: 2; z = z_hi * 2 + z_lo), core: 2. Of those that a mesh axis runs over, the one named last changes fastest.
Arguments:
- resid: bfloat16 [1024, 5120], P('wide'), may hold values from -6 to 6
- final_gain: float32 [5120], replicated, may hold values from 0.25 to 1.75
- unembed: bfloat16 [16384, 5120], P('narrow', 'wide'), may hold values from -12 to 12
- labels: int32 [1024, 4], replicated, may hold values from 0 to 16383
- layer_in: bfloat16 [1024, 5120], P('wide'), may hold values from -6 to 6
- gate_value: bfloat16 [1024, 13824], P('wide', 'narrow'), may hold values from -0.29882812 to 2
- down_weight: bfloat16 [13824, 5120], P('narrow', 'wide'), may hold values from -0.078125 to 0.078125
- basis_in: bfloat16 [5120, 5120], P('wide', 'narrow'), may hold values from -0.078125 to 0.078125
- basis_out: bfloat16 [13824, 13824], P('narrow', 'wide'), may hold values from -0.0546875 to 0.0546875
Outputs:
- corrected: float32 [13824, 5120], P('wide', 'narrow')
The draws below stay inside these ranges and needn't reach their ends.
All inputs are finite; a program needn't handle non-finite values.
Results may differ from the reference program's by a relative error of at most 0.002.
The reference program's roundings to bfloat16 on the way (of `normed`, `probs`, `back`, `gated`, `rotated` and `inputs_rot`) count: a program that leaves them out, or rounds other values in their place, can miss the bound.
Values may be sent and summed in bfloat16 or wider, within the bound.
A program may use at most 128 MiB of HBM per device.

```python
import math
import jax
import jax.numpy as jnp
from jax import lax

D = 5120
FW = 13824
VOCAB = 16384
SEQ = 256
SAMPLES = 4
EXAMPLES = 4
TOKENS = 1024


def draw_unembed(key, part):
    base = jax.random.normal(key, (VOCAB, D), jnp.float32) * (4.0 / math.sqrt(D))
    return jnp.clip(base, -12.0, 12.0).astype(jnp.bfloat16)


def with_ends(array, key, low, high):
    dims = array.shape
    index_at = [jax.random.randint(jax.random.fold_in(key, axis), (), 0, dims[axis]) for axis in range(len(dims))]
    array = array.at[tuple(index_at)].set(low)
    longest = dims.index(max(dims))
    index_at[longest] = (index_at[longest] + 1) % dims[longest]
    return array.at[tuple(index_at)].set(high)


def steps_of(key, extent, split, least, top_value):
    def one(dim, blocks):
        heights = jax.random.uniform(jax.random.fold_in(jax.random.fold_in(key, 6), dim), (blocks,), jnp.float32, least / len(split), top_value / len(split))
        return jnp.repeat(jnp.exp(heights), extent[dim] // blocks).reshape((-1,) + (1,) * (len(extent) - dim - 1))

    gain = one(*split[0])
    for cut in split[1:]:
        gain = gain * one(*cut)
    return gain


def normal_values(key, extent, deviation, most, split=(), kind=jnp.bfloat16):
    gain = steps_of(key, extent, split, -0.22, 0.18) if split else 1.0
    entries = jax.random.normal(key, extent, jnp.float32) * deviation * gain
    return jnp.minimum(jnp.maximum(entries, -most), most).astype(kind)


def setup_inputs(seed: int = 0) -> dict:
    key_list = jax.random.split(jax.random.key(seed), 10)
    resid = normal_values(key_list[0], (TOKENS, D), 1.0, 6.0, ((0, 32),))
    final_gain = jnp.clip(1.0 + 0.15 * jax.random.normal(key_list[1], (D,), jnp.float32), 0.25, 1.75)
    unembed = draw_unembed(jax.random.fold_in(key_list[9], 71), 0)
    labels = with_ends(jax.random.randint(key_list[3], (TOKENS, SAMPLES), 0, VOCAB), jax.random.fold_in(key_list[3], 1), 0, VOCAB - 1).astype(jnp.int32)
    layer_in = normal_values(key_list[4], (TOKENS, D), 1.0, 6.0, ((0, 32),))
    gate_value = jnp.clip(-0.29882812 + 2.2988281 * jax.random.uniform(key_list[5], (TOKENS, FW), jnp.float32) ** steps_of(key_list[5], (TOKENS, FW), ((0, 32), (1, 8)), -0.2, 0.2), -0.29882812, 2.0).astype(jnp.bfloat16)
    down_weight = normal_values(key_list[6], (FW, D), D ** -0.5, 0.078125, ((0, 8), (1, 32)))
    basis_in = normal_values(key_list[7], (D, D), D ** -0.5, 0.078125, ((0, 32), (1, 8)))
    basis_out = normal_values(key_list[8], (FW, FW), FW ** -0.5, 0.0546875, ((0, 8), (1, 32)))
    return {"resid": resid, "final_gain": final_gain, "unembed": unembed, "labels": labels, "layer_in": layer_in, "gate_value": gate_value, "down_weight": down_weight, "basis_in": basis_in, "basis_out": basis_out}


EPSILON = 1e-05

def reference(resid, final_gain, unembed, labels, layer_in, gate_value, down_weight, basis_in, basis_out):
    resid_float = resid.astype(jnp.float32)
    inverse = lax.rsqrt(lax.optimization_barrier(jnp.mean(resid_float * resid_float, axis=1)) + EPSILON)
    normed = (resid_float * inverse[:, None] * final_gain).astype(jnp.bfloat16)
    logits = lax.dot_general(normed, unembed, (((1,), (1,)), ((), ())), preferred_element_type=jnp.float32)
    largest = lax.optimization_barrier(jnp.max(logits, axis=1, keepdims=True))
    scaled = jnp.exp(logits - largest)
    probs = (scaled / lax.optimization_barrier(jnp.sum(scaled, axis=1, keepdims=True))).astype(jnp.bfloat16)
    common = jnp.dot(probs, unembed, preferred_element_type=jnp.float32)
    picked = jnp.take(unembed, labels.astype(jnp.int32), axis=0).astype(jnp.float32)
    label_grads = common[:, None, :] - picked
    inner = lax.optimization_barrier(jnp.sum(final_gain * label_grads * resid_float[:, None, :], axis=2))
    back = inverse[:, None, None] * final_gain * label_grads - resid_float[:, None, :] * (inverse ** 3)[:, None, None] * inner[:, :, None] / D
    back = back.astype(jnp.bfloat16).reshape(TOKENS * SAMPLES, D)
    hidden_grads = lax.dot_general(back, down_weight, (((1,), (1,)), ((), ())), preferred_element_type=jnp.float32)
    gated = (hidden_grads.reshape(TOKENS, SAMPLES, FW) * gate_value.astype(jnp.float32)[:, None, :]).astype(jnp.bfloat16)
    rotated = jnp.dot(gated.reshape(TOKENS * SAMPLES, FW), basis_out, preferred_element_type=jnp.float32).astype(jnp.bfloat16)
    rotated = rotated.reshape(EXAMPLES, SEQ, SAMPLES, FW)
    inputs_rot = jnp.dot(layer_in, basis_in, preferred_element_type=jnp.float32).astype(jnp.bfloat16).reshape(EXAMPLES, SEQ, D)

    def accumulate(total, pair):
        rot_example, input_example = pair
        for sample in range(SAMPLES):
            block = lax.dot_general(rot_example[:, sample, :], input_example, (((0,), (0,)), ((), ())), preferred_element_type=jnp.float32)
            total = total + block * block
        return (total, None)
    total, _ = lax.scan(accumulate, jnp.zeros((FW, D), jnp.float32), (rotated, inputs_rot))
    return total / (EXAMPLES * SAMPLES)
```

```python
import functools

import jax
import jax.numpy as jnp
from jax import lax
from jax.experimental import pallas as pl
from jax.experimental.pallas import tpu as pltpu
from jax.sharding import PartitionSpec as P

EPSILON = 1e-05
MESH = pl.DeviceIdType.MESH
F32 = jnp.float32
BF16 = jnp.bfloat16
ANY = pl.BlockSpec(memory_space=pl.ANY)
VMEM = pl.BlockSpec(memory_space=pltpu.VMEM)


class Net:
    def __init__(self, send_sem, recv_sem):
        self.send_sem, self.recv_sem = send_sem, recv_sem
        self.started = []
        wide, narrow = lax.axis_index("wide"), lax.axis_index("narrow")
        self.wide, self.narrow = wide, narrow
        self.core = lax.rem(wide, 2)
        self.x = lax.rem(lax.div(wide, 2), 4)
        self.z = lax.div(wide, 8)
        self.y = lax.rem(narrow, 4)
        self.zl = lax.div(narrow, 4)

    def on_x(self, step):
        return {"wide": self.z * 8 + lax.rem(self.x + step, 4) * 2 + self.core}

    def on_z(self, step):
        return {"wide": lax.rem(self.z + step, 4) * 8 + self.x * 2 + self.core}

    def on_y(self, step):
        return {"narrow": self.zl * 4 + lax.rem(self.y + step, 4)}

    def on_zl(self, step):
        return {"narrow": (1 - self.zl) * 4 + self.y}

    def on_core(self):
        return {"wide": self.wide + 1 - 2 * self.core}

    def greet(self, devices):
        barrier = pltpu.get_barrier_semaphore()
        for device in devices:
            pl.semaphore_signal(barrier, inc=1, device_id=device, device_id_type=MESH)
        pl.semaphore_wait(barrier, len(devices))

    def copy(self, slot, src, dst, device):
        return pltpu.make_async_remote_copy(
            src_ref=src,
            dst_ref=dst,
            send_sem=self.send_sem.at[slot],
            recv_sem=self.recv_sem.at[slot],
            device_id=device,
            device_id_type=MESH,
        )

    def send(self, slot, src, dst, device):
        copy = self.copy(slot, src, dst, device)
        copy.start()
        self.started.append(copy)

    def recv(self, slot, dst):
        self.copy(slot, dst, dst, self.on_core()).wait_recv()

    def finish(self):
        for copy in self.started:
            copy.wait_send()


def turn(place, step, size):
    return lax.rem(place + step, size)


def gather_stage(net, base, own, slot, outer_size, me_o, me_i, on_o, on_i):
    ip, im, i2 = (turn(me_i, s, 4) for s in (1, 3, 2))
    inner = lambda row: base + 6 + 6 * row

    def along(row, o, first):
        b = inner(row)
        src = own if first else (lambda h: slot(o, me_i, h))
        net.send(b, src(0), slot(o, me_i, 0), on_i(1))
        net.send(b + 2, src(1), slot(o, me_i, 1), on_i(3))
        net.send(b + 1, src(1), slot(o, me_i, 1), on_i(1))
        net.send(b + 3, src(0), slot(o, me_i, 0), on_i(3))

    def forward(row, o):
        b = inner(row)
        net.recv(b, slot(o, im, 0))
        net.send(b + 4, slot(o, im, 0), slot(o, im, 0), on_i(1))
        net.recv(b + 2, slot(o, ip, 1))
        net.send(b + 5, slot(o, ip, 1), slot(o, ip, 1), on_i(3))

    def rest(row, o):
        b = inner(row)
        net.recv(b + 1, slot(o, im, 1))
        net.recv(b + 3, slot(o, ip, 0))
        net.recv(b + 4, slot(o, i2, 0))
        net.recv(b + 5, slot(o, i2, 1))

    if outer_size == 4:
        op, om, o2 = (turn(me_o, s, 4) for s in (1, 3, 2))
        net.send(base, own(0), slot(me_o, me_i, 0), on_o(1))
        net.send(base + 2, own(1), slot(me_o, me_i, 1), on_o(3))
        net.send(base + 1, own(1), slot(me_o, me_i, 1), on_o(1))
        net.send(base + 3, own(0), slot(me_o, me_i, 0), on_o(3))
        along(0, me_o, True)
        net.recv(base, slot(om, me_i, 0))
        net.send(base + 4, slot(om, me_i, 0), slot(om, me_i, 0), on_o(1))
        net.recv(base + 2, slot(op, me_i, 1))
        net.send(base + 5, slot(op, me_i, 1), slot(op, me_i, 1), on_o(3))
        forward(0, me_o)
        net.recv(base + 1, slot(om, me_i, 1))
        along(1, om, False)
        net.recv(base + 3, slot(op, me_i, 0))
        along(2, op, False)
        forward(1, om)
        net.recv(base + 4, slot(o2, me_i, 0))
        net.recv(base + 5, slot(o2, me_i, 1))
        along(3, o2, False)
        forward(2, op)
        forward(3, o2)
        for row, o in enumerate((me_o, om, op, o2)):
            rest(row, o)
    else:
        oq = 1 - me_o
        for h in range(2):
            net.send(base + h, own(h), slot(me_o, me_i, h), on_o(1))
        along(0, me_o, True)
        forward(0, me_o)
        for h in range(2):
            net.recv(base + h, slot(oq, me_i, h))
        along(1, oq, False)
        forward(1, oq)
        rest(0, me_o)
        rest(1, oq)


def gather_slots(outer_size):
    return 6 + 6 * outer_size


class Sum:
    def __init__(self, part, fwd, mid, got, tot, zfwd, zgot):
        self.part, self.fwd, self.mid, self.got = part, fwd, mid, got
        self.tot, self.zfwd, self.zgot = tot, zfwd, zgot
        self.half = part.shape[2] // 2

    @staticmethod
    def scratch(outer, rows, columns, dtype):
        half = rows // 2
        return [
            pltpu.VMEM((outer, 2, half, columns), dtype),
            pltpu.VMEM((outer, 2, half, columns), dtype),
            pltpu.VMEM((outer, 2, rows, columns), dtype),
            pltpu.VMEM((outer, rows, columns), dtype),
            pltpu.VMEM((2, half, columns), dtype),
            pltpu.VMEM((2, rows, columns), dtype),
        ]

    def h(self, k):
        return pl.ds(k * self.half, self.half)


def reduce_slots(outer_size):
    return 6 * outer_size + 6


def reduce_stage(net, base, sums, outer_size, me_o, me_i, on_o, on_i):
    ip, im, i2 = (turn(me_i, s, 4) for s in (1, 3, 2))
    offsets = (2, 1, 3, 0) if outer_size == 4 else (1, 0)
    rows = [turn(me_o, off, outer_size) for off in offsets]
    count = reduce_slots(outer_size)

    def at(a, k, j):
        return base + a * count + 6 * k + j

    def start_far(k):
        for a, s in enumerate(sums):
            net.send(at(a, k, 0), s.part.at[rows[k], i2, s.h(0)], s.fwd.at[k, 0], on_i(1))
            net.send(at(a, k, 1), s.part.at[rows[k], i2, s.h(1)], s.fwd.at[k, 1], on_i(3))

    def start_near(k):
        for a, s in enumerate(sums):
            net.send(at(a, k, 2), s.part.at[rows[k], ip, s.h(1)], s.got.at[k, 0, s.h(1)], on_i(1))
            net.send(at(a, k, 3), s.part.at[rows[k], im, s.h(0)], s.got.at[k, 1, s.h(0)], on_i(3))

    def middle(k):
        for a, s in enumerate(sums):
            net.recv(at(a, k, 0), s.fwd.at[k, 0])
            s.mid[k, 0] = s.part[rows[k], ip, s.h(0)] + s.fwd[k, 0]
            net.send(at(a, k, 4), s.mid.at[k, 0], s.got.at[k, 0, s.h(0)], on_i(1))
            net.recv(at(a, k, 1), s.fwd.at[k, 1])
            s.mid[k, 1] = s.part[rows[k], im, s.h(1)] + s.fwd[k, 1]
            net.send(at(a, k, 5), s.mid.at[k, 1], s.got.at[k, 1, s.h(1)], on_i(3))

    def total(k):
        for a, s in enumerate(sums):
            z = base + a * count + 6 * outer_size
            net.recv(at(a, k, 2), s.got.at[k, 0, s.h(1)])
            net.recv(at(a, k, 3), s.got.at[k, 1, s.h(0)])
            net.recv(at(a, k, 4), s.got.at[k, 0, s.h(0)])
            net.recv(at(a, k, 5), s.got.at[k, 1, s.h(1)])
            for h in range(2):
                s.tot[k, s.h(h)] = (
                    s.part[rows[k], me_i, s.h(h)] + s.got[k, 0, s.h(h)] + s.got[k, 1, s.h(h)]
                )
            if outer_size == 2:
                if k == 0:
                    for h in range(2):
                        net.send(z + h, s.tot.at[0, s.h(h)], s.zgot.at[0, s.h(h)], on_o(1))
            elif k == 0:
                net.send(z, s.tot.at[0, s.h(0)], s.zfwd.at[0], on_o(1))
                net.send(z + 1, s.tot.at[0, s.h(1)], s.zfwd.at[1], on_o(3))
            elif k == 1:
                net.send(z + 2, s.tot.at[1, s.h(1)], s.zgot.at[0, s.h(1)], on_o(1))
                net.recv(z, s.zfwd.at[0])
                s.tot[1, s.h(0)] += s.zfwd[0]
                net.send(z + 3, s.tot.at[1, s.h(0)], s.zgot.at[0, s.h(0)], on_o(1))
            elif k == 2:
                net.send(z + 4, s.tot.at[2, s.h(0)], s.zgot.at[1, s.h(0)], on_o(3))
                net.recv(z + 1, s.zfwd.at[1])
                s.tot[2, s.h(1)] += s.zfwd[1]
                net.send(z + 5, s.tot.at[2, s.h(1)], s.zgot.at[1, s.h(1)], on_o(3))

    start_far(0)
    start_far(1)
    start_near(0)
    for k in range(outer_size):
        if k + 2 < outer_size:
            start_far(k + 2)
        if k + 1 < outer_size:
            start_near(k + 1)
        middle(k)
        if k >= 1:
            total(k - 1)
    total(outer_size - 1)

    def final(a):
        s = sums[a]
        z = base + a * count + 6 * outer_size
        last = outer_size - 1

        def value(h):
            if outer_size == 2:
                net.recv(z + h, s.zgot.at[0, s.h(h)])
                return s.tot[last, s.h(h)] + s.zgot[0, s.h(h)]
            first, second = ((z + 3, z + 4), (z + 2, z + 5))[h]
            net.recv(first, s.zgot.at[0, s.h(h)])
            net.recv(second, s.zgot.at[1, s.h(h)])
            return s.tot[last, s.h(h)] + s.zgot[0, s.h(h)] + s.zgot[1, s.h(h)]

        return value

    return [final(a) for a in range(len(sums))]


def sems(slots):
    return [pltpu.SemaphoreType.DMA((slots,)), pltpu.SemaphoreType.DMA((slots,))]


def call(kernel, collective_id, outs, in_specs, out_specs, scratch, args, name):
    return pl.pallas_call(
        kernel,
        out_shape=outs,
        in_specs=in_specs,
        out_specs=out_specs,
        scratch_shapes=scratch,
        compiler_params=pltpu.CompilerParams(
            collective_id=collective_id, has_side_effects=True, vmem_limit_bytes=60 << 20
        ),
        name=name,
    )(*args)


def like(shape, dtype):
    return jax.ShapeDtypeStruct(shape, dtype)


def exchange(arrays, pairs, collective_id, name):
    na, np_ = len(arrays), len(pairs)

    def kernel(*refs):
        ins, shared = refs[:na], refs[na : na + np_]
        outs, both = refs[na + np_ : 2 * na + np_], refs[2 * na + np_ : 2 * (na + np_)]
        local, send_sem, recv_sem = refs[2 * (na + np_) :]
        net = Net(send_sem, recv_sem)
        steps = [(dz, dx) for dz in range(4) for dx in range(4) if (dz, dx) != (0, 0)]
        steps.sort(key=lambda s: -(min(s[0], 4 - s[0]) * 2 + min(s[1], 4 - s[1])))

        def to(dz, dx):
            return turn(net.z, dz, 4) * 4 + turn(net.x, dx, 4)

        me = net.z * 4 + net.x
        peers = [{"wide": to(*s) * 2 + net.core} for s in steps]
        net.greet(peers + ([net.on_core()] if np_ else []))
        copies = []
        for j, s in enumerate(steps):
            for a in range(na):
                net.send(j * na + a, ins[a].at[to(*s)], outs[a].at[me], peers[j])
        for a in range(na):
            copies.append(pltpu.make_async_copy(ins[a].at[me], outs[a].at[me], local.at[a]))
        for b in range(np_):
            net.send(15 * na + b, shared[b], both[b].at[net.core], net.on_core())
            copies.append(
                pltpu.make_async_copy(shared[b], both[b].at[net.core], local.at[na + b])
            )
        for copy in copies:
            copy.start()
        for j, (dz, dx) in enumerate(steps):
            source = to((4 - dz) % 4, (4 - dx) % 4)
            for a in range(na):
                net.recv(j * na + a, outs[a].at[source])
        for b in range(np_):
            net.recv(15 * na + b, both[b].at[1 - net.core])
        for copy in copies:
            copy.wait()
        net.finish()

    outs = [like(a.shape, a.dtype) for a in arrays] + [like((2, *p.shape), p.dtype) for p in pairs]
    return call(
        kernel,
        collective_id,
        outs,
        [ANY] * (na + np_),
        [ANY] * (na + np_),
        [pltpu.SemaphoreType.DMA((na + np_,)), *sems(15 * na + max(np_, 1))],
        (*arrays, *pairs),
        name,
    )


def gather_wide(shard, spread, collective_id, name):
    half = shard.shape[0] // 2
    shape = (4, shard.shape[0], 4, *shard.shape[1:]) if spread else (4, 4, *shard.shape)

    def kernel(x_ref, o_ref, local, send_sem, recv_sem):
        net = Net(send_sem, recv_sem)

        def slot(o, i, h):
            part = pl.ds(h * half, half)
            return o_ref.at[o, part, i] if spread else o_ref.at[o, i, part]

        net.greet([net.on_x(1), net.on_x(3), net.on_z(1), net.on_z(3)])
        own = lambda h: x_ref.at[pl.ds(h * half, half)]
        copies = [
            pltpu.make_async_copy(own(h), slot(net.z, net.x, h), local.at[h]) for h in range(2)
        ]
        for copy in copies:
            copy.start()
        gather_stage(net, 0, own, slot, 4, net.z, net.x, net.on_z, net.on_x)
        for copy in copies:
            copy.wait()
        net.finish()

    return call(
        kernel,
        collective_id,
        like(shape, shard.dtype),
        [ANY],
        ANY,
        [pltpu.SemaphoreType.DMA((2,)), *sems(gather_slots(4))],
        (shard,),
        name,
    )


def gather_narrow(shard, collective_id, name):
    half = shard.shape[0] // 2

    def kernel(x_ref, o_ref, local, send_sem, recv_sem):
        net = Net(send_sem, recv_sem)
        slot = lambda o, i, h: o_ref.at[o, i, pl.ds(h * half, half)]
        net.greet([net.on_y(1), net.on_y(3), net.on_zl(1)])
        own = lambda h: x_ref.at[pl.ds(h * half, half)]
        copies = [
            pltpu.make_async_copy(own(h), slot(net.zl, net.y, h), local.at[h]) for h in range(2)
        ]
        for copy in copies:
            copy.start()
        gather_stage(net, 0, own, slot, 2, net.zl, net.y, net.on_zl, net.on_y)
        for copy in copies:
            copy.wait()
        net.finish()

    return call(
        kernel,
        collective_id,
        like((2, 4, *shard.shape), shard.dtype),
        [ANY],
        ANY,
        [pltpu.SemaphoreType.DMA((2,)), *sems(gather_slots(2))],
        (shard,),
        name,
    )


def reduce_over(axis, parts, dtypes, collective_id, name):
    n = len(parts)
    outer = parts[0].shape[0]

    def kernel(*refs):
        ins, outs = refs[:n], refs[n : 2 * n]
        buffers, (send_sem, recv_sem) = refs[2 * n : -2], refs[-2:]
        net = Net(send_sem, recv_sem)
        sums = [Sum(ins[a], *buffers[6 * a : 6 * a + 6]) for a in range(n)]
        if axis == "wide":
            net.greet([net.on_x(1), net.on_x(3), net.on_z(1), net.on_z(3)])
            ends = reduce_stage(net, 0, sums, 4, net.z, net.x, net.on_z, net.on_x)
        else:
            net.greet([net.on_y(1), net.on_y(3), net.on_zl(1)])
            ends = reduce_stage(net, 0, sums, 2, net.zl, net.y, net.on_zl, net.on_y)
        for a in range(n):
            for h in range(2):
                outs[a][sums[a].h(h), :] = ends[a](h).astype(outs[a].dtype)
        net.finish()

    scratch = []
    for p in parts:
        scratch += Sum.scratch(outer, p.shape[2], p.shape[3], p.dtype)
    return call(
        kernel,
        collective_id,
        [like(p.shape[2:], d) for p, d in zip(parts, dtypes)],
        [VMEM] * n,
        [VMEM] * n,
        [*scratch, *sems(n * reduce_slots(outer))],
        tuple(parts),
        name,
    )


def softmax_narrow(logits, collective_id, name):
    rows, columns = logits.shape

    def kernel(l_ref, p_ref, mine, got, send_sem, recv_sem):
        net = Net(send_sem, recv_sem)
        peers = [{"narrow": turn(net.narrow, k, 8)} for k in range(1, 8)]
        top = jnp.max(l_ref[...], axis=1, keepdims=True)
        mine[0] = jnp.broadcast_to(top, (rows, 128))
        mine[1] = jnp.broadcast_to(
            jnp.sum(jnp.exp(l_ref[...] - top), axis=1, keepdims=True), (rows, 128)
        )
        net.greet(peers)
        for k in range(7):
            net.send(k, mine, got.at[k], peers[k])
        for k in range(7):
            net.recv(k, got.at[k])
        largest = mine[0]
        for k in range(7):
            largest = jnp.maximum(largest, got[k, 0])
        total = mine[1] * jnp.exp(mine[0] - largest)
        for k in range(7):
            total += got[k, 1] * jnp.exp(got[k, 0] - largest)
        p_ref[...] = (jnp.exp(l_ref[...] - largest[:, :1]) / total[:, :1]).astype(BF16)
        net.finish()

    return call(
        kernel,
        collective_id,
        like((rows, columns), BF16),
        [VMEM],
        VMEM,
        [pltpu.VMEM((2, rows, 128), F32), pltpu.VMEM((7, 2, rows, 128), F32), *sems(7)],
        (logits,),
        name,
    )


def rotate(gated, basis):
    chunks, rows, depth = gated.shape
    columns = basis.shape[0]

    def kernel(g_ref, b_ref, o_ref):
        o_ref[0] = lax.dot_general(
            b_ref[...], g_ref[0], (((1,), (1,)), ((), ())), preferred_element_type=F32
        )

    return pl.pallas_call(
        kernel,
        grid=(chunks,),
        out_shape=like((chunks, columns, rows), F32),
        in_specs=[
            pl.BlockSpec((1, rows, depth), lambda i: (i, 0, 0)),
            pl.BlockSpec((columns, depth), lambda i: (0, 0)),
        ],
        out_specs=pl.BlockSpec((1, columns, rows), lambda i: (i, 0, 0)),
        name="rotate",
    )(gated, basis)


def total_narrow(part, inputs, collective_id, name):
    rows, columns = part.shape[2] // 2, part.shape[3]

    def kernel(p_ref, i_ref, o_ref, j_ref, *refs):
        buffers, (mine, local, send_sem, recv_sem) = refs[:6], refs[6:]
        net = Net(send_sem, recv_sem)
        net.greet([net.on_y(1), net.on_y(3), net.on_zl(1), net.on_core()])
        base = reduce_slots(2)
        net.send(base, i_ref, j_ref, net.on_core())
        sums = [Sum(p_ref, *buffers)]
        (end,) = reduce_stage(net, 0, sums, 2, net.zl, net.y, net.on_zl, net.on_y)
        for h in range(2):
            mine[h] = end(h).astype(BF16)
        net.send(base + 1, mine.at[1 - net.core], mine.at[2], net.on_core())
        net.recv(base + 1, mine.at[2])
        slot = lambda o, i, h: o_ref.at[o, i, h]
        own = lambda h: mine.at[2 if h else net.core]
        copies = [
            pltpu.make_async_copy(own(h), slot(net.zl, net.y, h), local.at[h]) for h in range(2)
        ]
        for copy in copies:
            copy.start()
        gather_stage(net, base + 2, own, slot, 2, net.zl, net.y, net.on_zl, net.on_y)
        net.recv(base, j_ref)
        for copy in copies:
            copy.wait()
        net.finish()

    return call(
        kernel,
        collective_id,
        [like((2, 4, 2, rows, columns), BF16), like(inputs.shape, BF16)],
        [VMEM, ANY],
        [ANY, ANY],
        [
            *Sum.scratch(2, 2 * rows, columns, F32),
            pltpu.VMEM((3, rows, columns), BF16),
            pltpu.SemaphoreType.DMA((2,)),
            *sems(reduce_slots(2) + 2 + gather_slots(2)),
        ],
        (part, inputs),
        name,
    )


def squares(rotated, own_inputs, other_inputs):
    rows, width = rotated.shape[2], own_inputs.shape[2]

    def kernel(r_ref, a_ref, b_ref, o_ref):
        step = pl.program_id(0)

        @pl.when(step == 0)
        def _():
            o_ref[...] = jnp.zeros_like(o_ref)

        for s in range(2):
            cut = pl.ds(s * 128, 128)
            block = jnp.dot(r_ref[0, 0, :, cut], a_ref[0], preferred_element_type=F32)
            block += jnp.dot(r_ref[0, 1, :, cut], b_ref[0], preferred_element_type=F32)
            o_ref[...] += block * block * (1.0 / 16.0)

    return pl.pallas_call(
        kernel,
        grid=(8,),
        out_shape=like((rows, width), F32),
        in_specs=[
            pl.BlockSpec((1, 2, rows, 256), lambda i: (i, 0, 0, 0)),
            pl.BlockSpec((1, 128, width), lambda i: (i // 2, 0, 0)),
            pl.BlockSpec((1, 128, width), lambda i: (i // 2, 0, 0)),
        ],
        out_specs=pl.BlockSpec((rows, width), lambda i: (0, 0)),
        name="squares",
    )(rotated, own_inputs, other_inputs)


def contract_last(left, right):
    return lax.dot_general(left, right, (((1,), (1,)), ((), ())), preferred_element_type=F32)


def per_device(
    resid, final_gain, unembed, labels, layer_in, gate_value, down_weight, basis_in, basis_out
):
    wide, narrow = lax.axis_index("wide"), lax.axis_index("narrow")
    core = lax.rem(wide, 2)
    tokens, width = resid.shape
    samples = labels.shape[1]
    vocab, part = unembed.shape
    hidden = down_weight.shape[0]
    columns = basis_out.shape[1]
    width_in = basis_in.shape[1]
    pair = 2 * part
    core_tokens = 16 * tokens
    few = tokens // 8

    down_rows = lax.all_gather(down_weight.T, "wide", axis=0, tiled=True)

    resid_float = resid.astype(F32)
    inverse = lax.rsqrt(jnp.mean(resid_float * resid_float, axis=1) + EPSILON)
    normed = (resid_float * inverse[:, None] * final_gain).astype(BF16)

    def blocks(rows):
        return rows.reshape(tokens, 16, pair).transpose(1, 0, 2)

    normed_cols, inputs_cols, unembed_rows, basis_in_rows, basis_rows = exchange(
        [blocks(normed), blocks(layer_in)],
        [unembed.T, basis_in, basis_out.T],
        0,
        "exchange",
    )
    unembed_rows = unembed_rows.reshape(pair, vocab)
    basis_in_rows = basis_in_rows.reshape(pair, width_in)
    logits_part = jnp.dot(
        normed_cols.reshape(core_tokens, pair), unembed_rows, preferred_element_type=F32
    )
    inputs_part = jnp.dot(
        inputs_cols.reshape(core_tokens, pair), basis_in_rows, preferred_element_type=F32
    )
    logits, inputs_rot = reduce_over(
        "wide",
        [logits_part.reshape(4, 4, tokens, vocab), inputs_part.reshape(4, 4, tokens, width_in)],
        [F32, BF16],
        1,
        "reduce_logits",
    )
    probs = softmax_narrow(logits, 2, "softmax")
    both = jnp.concatenate([probs, inputs_rot], axis=1)
    both = gather_wide(both.reshape(2, tokens // 2, vocab + width_in), False, 3, "gather_probs")
    both = both.reshape(core_tokens, vocab + width_in)
    inputs_all = both[:, vocab:].reshape(4, 4 * tokens, width_in)
    common = contract_last(both[:, :vocab], unembed_rows)
    common = common.reshape(16, 8, few, pair).transpose(1, 0, 2, 3).reshape(2, 4, 16 * few, pair)

    mine = lax.dynamic_index_in_dim(
        labels.reshape(16, 2, 8, few, samples), core, 1, keepdims=False
    )
    shifted = mine.transpose(1, 0, 2, 3).reshape(core_tokens * samples) - narrow * vocab
    chosen = (shifted[:, None] == lax.broadcasted_iota(jnp.int32, (1, vocab), 1)).astype(BF16)
    picked = contract_last(chosen, unembed_rows).astype(BF16)
    picked = picked.reshape(2, 4, 16 * few * samples, pair)
    common, picked = reduce_over("narrow", [common, picked], [F32, BF16], 4, "reduce_grads")
    grads = common.reshape(16, few, 1, pair) - picked.astype(F32).reshape(16, few, samples, pair)
    (grads,) = exchange([grads.reshape(16, few * samples, pair)], [], 5, "exchange_grads")
    grads = grads.transpose(1, 0, 2).reshape(few, samples, width)
    resid_few = lax.dynamic_slice_in_dim(resid_float, narrow * few, few, 0)
    inverse_few = lax.dynamic_slice_in_dim(inverse, narrow * few, few, 0)
    inner = jnp.sum(final_gain * grads * resid_few[:, None, :], axis=2)
    back = (
        inverse_few[:, None, None] * final_gain * grads
        - resid_few[:, None, :] * (inverse_few**3)[:, None, None] * inner[:, :, None] / width
    )
    back = back.astype(BF16).reshape(2, few * samples // 2, width)
    back = gather_narrow(back, 6, "gather_back").reshape(tokens * samples, width)
    hidden_grads = jnp.dot(back, down_rows, preferred_element_type=F32)
    gated = hidden_grads.reshape(tokens, samples, hidden) * gate_value.astype(F32)[:, None, :]
    gated = gated.astype(BF16).transpose(1, 0, 2)
    gated = gather_wide(gated, True, 7, "gather_gated")
    part_rot = rotate(
        gated.reshape(8, 8 * tokens, hidden), basis_rows.reshape(2 * columns, hidden)
    )
    rotated, inputs_other = total_narrow(
        part_rot.reshape(2, 4, 2 * columns, 8 * tokens), inputs_all, 8, "total"
    )
    return squares(rotated.reshape(8, 2, columns, 8 * tokens), inputs_all, inputs_other)


def solution(mesh):
    in_specs = (
        P("wide", None),
        P(),
        P("narrow", "wide"),
        P(),
        P("wide", None),
        P("wide", "narrow"),
        P("narrow", "wide"),
        P("wide", "narrow"),
        P("narrow", "wide"),
    )
    out_specs = P("wide", "narrow")
    return jax.shard_map(
        per_device, mesh=mesh, in_specs=in_specs, out_specs=out_specs, check_vma=False
    )
```

```python
import functools

import jax
import jax.numpy as jnp
from jax import lax
from jax.experimental import pallas as pl
from jax.experimental.pallas import tpu as pltpu
from jax.sharding import PartitionSpec as P

EPSILON = 1e-05
MESH = pl.DeviceIdType.MESH
F32 = jnp.float32
BF16 = jnp.bfloat16
ANY = pl.BlockSpec(memory_space=pl.ANY)
VMEM = pl.BlockSpec(memory_space=pltpu.VMEM)


class Net:
    def __init__(self, send_sem, recv_sem):
        self.send_sem, self.recv_sem = send_sem, recv_sem
        self.started = []
        wide, narrow = lax.axis_index("wide"), lax.axis_index("narrow")
        self.wide, self.narrow = wide, narrow
        self.core = lax.rem(wide, 2)
        self.x = lax.rem(lax.div(wide, 2), 4)
        self.z = lax.div(wide, 8)
        self.y = lax.rem(narrow, 4)
        self.zl = lax.div(narrow, 4)

    def on_x(self, step):
        return {"wide": self.z * 8 + lax.rem(self.x + step, 4) * 2 + self.core}

    def on_z(self, step):
        return {"wide": lax.rem(self.z + step, 4) * 8 + self.x * 2 + self.core}

    def on_y(self, step):
        return {"narrow": self.zl * 4 + lax.rem(self.y + step, 4)}

    def on_zl(self, step):
        return {"narrow": (1 - self.zl) * 4 + self.y}

    def on_core(self):
        return {"wide": self.wide + 1 - 2 * self.core}

    def greet(self, devices):
        barrier = pltpu.get_barrier_semaphore()
        for device in devices:
            pl.semaphore_signal(barrier, inc=1, device_id=device, device_id_type=MESH)
        pl.semaphore_wait(barrier, len(devices))

    def copy(self, slot, src, dst, device):
        return pltpu.make_async_remote_copy(
            src_ref=src,
            dst_ref=dst,
            send_sem=self.send_sem.at[slot],
            recv_sem=self.recv_sem.at[slot],
            device_id=device,
            device_id_type=MESH,
        )

    def send(self, slot, src, dst, device):
        copy = self.copy(slot, src, dst, device)
        copy.start()
        self.started.append(copy)

    def recv(self, slot, dst):
        self.copy(slot, dst, dst, self.on_core()).wait_recv()

    def finish(self):
        for copy in self.started:
            copy.wait_send()


def turn(place, step, size):
    return lax.rem(place + step, size)


def gather_stage(net, base, own, slot, outer_size, me_o, me_i, on_o, on_i):
    ip, im, i2 = (turn(me_i, s, 4) for s in (1, 3, 2))
    inner = lambda row: base + 6 + 6 * row

    def along(row, o, first):
        b = inner(row)
        src = own if first else (lambda h: slot(o, me_i, h))
        net.send(b, src(0), slot(o, me_i, 0), on_i(1))
        net.send(b + 2, src(1), slot(o, me_i, 1), on_i(3))
        net.send(b + 1, src(1), slot(o, me_i, 1), on_i(1))
        net.send(b + 3, src(0), slot(o, me_i, 0), on_i(3))

    def forward(row, o):
        b = inner(row)
        net.recv(b, slot(o, im, 0))
        net.send(b + 4, slot(o, im, 0), slot(o, im, 0), on_i(1))
        net.recv(b + 2, slot(o, ip, 1))
        net.send(b + 5, slot(o, ip, 1), slot(o, ip, 1), on_i(3))

    def rest(row, o):
        b = inner(row)
        net.recv(b + 1, slot(o, im, 1))
        net.recv(b + 3, slot(o, ip, 0))
        net.recv(b + 4, slot(o, i2, 0))
        net.recv(b + 5, slot(o, i2, 1))

    if outer_size == 4:
        op, om, o2 = (turn(me_o, s, 4) for s in (1, 3, 2))
        net.send(base, own(0), slot(me_o, me_i, 0), on_o(1))
        net.send(base + 2, own(1), slot(me_o, me_i, 1), on_o(3))
        net.send(base + 1, own(1), slot(me_o, me_i, 1), on_o(1))
        net.send(base + 3, own(0), slot(me_o, me_i, 0), on_o(3))
        along(0, me_o, True)
        net.recv(base, slot(om, me_i, 0))
        net.send(base + 4, slot(om, me_i, 0), slot(om, me_i, 0), on_o(1))
        net.recv(base + 2, slot(op, me_i, 1))
        net.send(base + 5, slot(op, me_i, 1), slot(op, me_i, 1), on_o(3))
        forward(0, me_o)
        net.recv(base + 1, slot(om, me_i, 1))
        along(1, om, False)
        net.recv(base + 3, slot(op, me_i, 0))
        along(2, op, False)
        forward(1, om)
        net.recv(base + 4, slot(o2, me_i, 0))
        net.recv(base + 5, slot(o2, me_i, 1))
        along(3, o2, False)
        forward(2, op)
        forward(3, o2)
        for row, o in enumerate((me_o, om, op, o2)):
            rest(row, o)
    else:
        oq = 1 - me_o
        for h in range(2):
            net.send(base + h, own(h), slot(me_o, me_i, h), on_o(1))
        along(0, me_o, True)
        yield
        forward(0, me_o)
        for h in range(2):
            net.recv(base + h, slot(oq, me_i, h))
        along(1, oq, False)
        yield
        forward(1, oq)
        yield
        rest(0, me_o)
        rest(1, oq)


def gather_slots(outer_size):
    return 6 + 6 * outer_size


class Sum:
    def __init__(self, part, fwd, mid, got, tot, zfwd, zgot):
        self.part, self.fwd, self.mid, self.got = part, fwd, mid, got
        self.tot, self.zfwd, self.zgot = tot, zfwd, zgot
        self.half = part.shape[2] // 2

    @staticmethod
    def scratch(outer, rows, columns, dtype):
        half = rows // 2
        return [
            pltpu.VMEM((outer, 2, half, columns), dtype),
            pltpu.VMEM((outer, 2, half, columns), dtype),
            pltpu.VMEM((outer, 2, rows, columns), dtype),
            pltpu.VMEM((outer, rows, columns), dtype),
            pltpu.VMEM((2, half, columns), dtype),
            pltpu.VMEM((2, rows, columns), dtype),
        ]

    def h(self, k):
        return pl.ds(k * self.half, self.half)


def reduce_slots(outer_size):
    return 6 * outer_size + 6


def reduce_stage(net, base, sums, outer_size, me_o, me_i, on_o, on_i):
    ip, im, i2 = (turn(me_i, s, 4) for s in (1, 3, 2))
    offsets = (2, 1, 3, 0) if outer_size == 4 else (1, 0)
    rows = [turn(me_o, off, outer_size) for off in offsets]
    count = reduce_slots(outer_size)

    def at(a, k, j):
        return base + a * count + 6 * k + j

    def start_far(k):
        for a, s in enumerate(sums):
            net.send(at(a, k, 0), s.part.at[rows[k], i2, s.h(0)], s.fwd.at[k, 0], on_i(1))
            net.send(at(a, k, 1), s.part.at[rows[k], i2, s.h(1)], s.fwd.at[k, 1], on_i(3))

    def start_near(k):
        for a, s in enumerate(sums):
            net.send(at(a, k, 2), s.part.at[rows[k], ip, s.h(1)], s.got.at[k, 0, s.h(1)], on_i(1))
            net.send(at(a, k, 3), s.part.at[rows[k], im, s.h(0)], s.got.at[k, 1, s.h(0)], on_i(3))

    def middle(k):
        for a, s in enumerate(sums):
            net.recv(at(a, k, 0), s.fwd.at[k, 0])
            s.mid[k, 0] = s.part[rows[k], ip, s.h(0)] + s.fwd[k, 0]
            net.send(at(a, k, 4), s.mid.at[k, 0], s.got.at[k, 0, s.h(0)], on_i(1))
            net.recv(at(a, k, 1), s.fwd.at[k, 1])
            s.mid[k, 1] = s.part[rows[k], im, s.h(1)] + s.fwd[k, 1]
            net.send(at(a, k, 5), s.mid.at[k, 1], s.got.at[k, 1, s.h(1)], on_i(3))

    def total(k):
        for a, s in enumerate(sums):
            z = base + a * count + 6 * outer_size
            net.recv(at(a, k, 2), s.got.at[k, 0, s.h(1)])
            net.recv(at(a, k, 3), s.got.at[k, 1, s.h(0)])
            net.recv(at(a, k, 4), s.got.at[k, 0, s.h(0)])
            net.recv(at(a, k, 5), s.got.at[k, 1, s.h(1)])
            for h in range(2):
                s.tot[k, s.h(h)] = (
                    s.part[rows[k], me_i, s.h(h)] + s.got[k, 0, s.h(h)] + s.got[k, 1, s.h(h)]
                )
            if outer_size == 2:
                if k == 0:
                    for h in range(2):
                        net.send(z + h, s.tot.at[0, s.h(h)], s.zgot.at[0, s.h(h)], on_o(1))
            elif k == 0:
                net.send(z, s.tot.at[0, s.h(0)], s.zfwd.at[0], on_o(1))
                net.send(z + 1, s.tot.at[0, s.h(1)], s.zfwd.at[1], on_o(3))
            elif k == 1:
                net.send(z + 2, s.tot.at[1, s.h(1)], s.zgot.at[0, s.h(1)], on_o(1))
                net.recv(z, s.zfwd.at[0])
                s.tot[1, s.h(0)] += s.zfwd[0]
                net.send(z + 3, s.tot.at[1, s.h(0)], s.zgot.at[0, s.h(0)], on_o(1))
            elif k == 2:
                net.send(z + 4, s.tot.at[2, s.h(0)], s.zgot.at[1, s.h(0)], on_o(3))
                net.recv(z + 1, s.zfwd.at[1])
                s.tot[2, s.h(1)] += s.zfwd[1]
                net.send(z + 5, s.tot.at[2, s.h(1)], s.zgot.at[1, s.h(1)], on_o(3))

    def steps():
        start_far(0)
        start_far(1)
        start_near(0)
        yield
        for k in range(outer_size):
            if k + 2 < outer_size:
                start_far(k + 2)
            if k + 1 < outer_size:
                start_near(k + 1)
            middle(k)
            if k >= 1:
                total(k - 1)
            yield
        total(outer_size - 1)

    def final(a):
        s = sums[a]
        z = base + a * count + 6 * outer_size
        last = outer_size - 1

        def value(h):
            if outer_size == 2:
                net.recv(z + h, s.zgot.at[0, s.h(h)])
                return s.tot[last, s.h(h)] + s.zgot[0, s.h(h)]
            first, second = ((z + 3, z + 4), (z + 2, z + 5))[h]
            net.recv(first, s.zgot.at[0, s.h(h)])
            net.recv(second, s.zgot.at[1, s.h(h)])
            return s.tot[last, s.h(h)] + s.zgot[0, s.h(h)] + s.zgot[1, s.h(h)]

        return value

    return steps(), [final(a) for a in range(len(sums))]


def drive(*stages):
    stages = list(stages)
    while stages:
        stages = [stage for stage in stages if next(stage, 0) is None]


def sems(slots):
    return [pltpu.SemaphoreType.DMA((slots,)), pltpu.SemaphoreType.DMA((slots,))]


def call(kernel, collective_id, outs, in_specs, out_specs, scratch, args, name, cost):
    return pl.pallas_call(
        kernel,
        out_shape=outs,
        in_specs=in_specs,
        out_specs=out_specs,
        scratch_shapes=scratch,
        compiler_params=pltpu.CompilerParams(
            collective_id=collective_id, has_side_effects=True, vmem_limit_bytes=60 << 20
        ),
        cost_estimate=pl.CostEstimate(flops=cost * 10**9, bytes_accessed=0, transcendentals=0),
        name=name,
    )(*args)


def like(shape, dtype):
    return jax.ShapeDtypeStruct(shape, dtype)


def exchange(arrays, pairs, collective_id, name, cost):
    na, np_ = len(arrays), len(pairs)

    def kernel(*refs):
        ins, shared = refs[:na], refs[na : na + np_]
        outs, both = refs[na + np_ : 2 * na + np_], refs[2 * na + np_ : 2 * (na + np_)]
        local, send_sem, recv_sem = refs[2 * (na + np_) :]
        net = Net(send_sem, recv_sem)
        steps = [(dz, dx) for dz in range(4) for dx in range(4) if (dz, dx) != (0, 0)]
        steps.sort(key=lambda s: -(min(s[0], 4 - s[0]) * 2 + min(s[1], 4 - s[1])))

        def to(dz, dx):
            return turn(net.z, dz, 4) * 4 + turn(net.x, dx, 4)

        me = net.z * 4 + net.x
        peers = [{"wide": to(*s) * 2 + net.core} for s in steps]
        net.greet(peers + ([net.on_core()] if np_ else []))
        copies = []
        for j, s in enumerate(steps):
            for a in range(na):
                net.send(j * na + a, ins[a].at[to(*s)], outs[a].at[me], peers[j])
        for a in range(na):
            copies.append(pltpu.make_async_copy(ins[a].at[me], outs[a].at[me], local.at[a]))
        for b in range(np_):
            net.send(15 * na + b, shared[b], both[b].at[net.core], net.on_core())
            copies.append(
                pltpu.make_async_copy(shared[b], both[b].at[net.core], local.at[na + b])
            )
        for copy in copies:
            copy.start()
        for j, (dz, dx) in enumerate(steps):
            source = to((4 - dz) % 4, (4 - dx) % 4)
            for a in range(na):
                net.recv(j * na + a, outs[a].at[source])
        for b in range(np_):
            net.recv(15 * na + b, both[b].at[1 - net.core])
        for copy in copies:
            copy.wait()
        net.finish()

    outs = [like(a.shape, a.dtype) for a in arrays] + [like((2, *p.shape), p.dtype) for p in pairs]
    return call(
        kernel,
        collective_id,
        outs,
        [ANY] * (na + np_),
        [ANY] * (na + np_),
        [pltpu.SemaphoreType.DMA((na + np_,)), *sems(15 * na + max(np_, 1))],
        (*arrays, *pairs),
        name,
        cost,
    )


def gather_wide(shard, collective_id, name, cost):
    half = shard.shape[0] // 2
    shape = (4, 4, *shard.shape)

    def kernel(x_ref, o_ref, local, send_sem, recv_sem):
        net = Net(send_sem, recv_sem)

        slot = lambda o, i, h: o_ref.at[o, i, pl.ds(h * half, half)]
        net.greet([net.on_x(1), net.on_x(3), net.on_z(1), net.on_z(3)])
        own = lambda h: x_ref.at[pl.ds(h * half, half)]
        copies = [
            pltpu.make_async_copy(own(h), slot(net.z, net.x, h), local.at[h]) for h in range(2)
        ]
        for copy in copies:
            copy.start()
        drive(gather_stage(net, 0, own, slot, 4, net.z, net.x, net.on_z, net.on_x))
        for copy in copies:
            copy.wait()
        net.finish()

    return call(
        kernel,
        collective_id,
        like(shape, shard.dtype),
        [ANY],
        ANY,
        [pltpu.SemaphoreType.DMA((2,)), *sems(gather_slots(4))],
        (shard,),
        name,
        cost,
    )


def reduce_over(wide_parts, narrow_parts, dtypes, collective_id, name, cost):
    parts = [*wide_parts, *narrow_parts]
    n, split = len(parts), len(wide_parts)

    def kernel(*refs):
        ins, outs = refs[:n], refs[n : 2 * n]
        buffers, (send_sem, recv_sem) = refs[2 * n : -2], refs[-2:]
        net = Net(send_sem, recv_sem)
        sums = [Sum(ins[a], *buffers[6 * a : 6 * a + 6]) for a in range(n)]
        stages, ends, peers = [], [], []
        if split:
            peers += [net.on_x(1), net.on_x(3), net.on_z(1), net.on_z(3)]
            stage, end = reduce_stage(net, 0, sums[:split], 4, net.z, net.x, net.on_z, net.on_x)
            stages.append(stage)
            ends += end
        if n > split:
            peers += [net.on_y(1), net.on_y(3), net.on_zl(1)]
            base = split * reduce_slots(4)
            stage, end = reduce_stage(
                net, base, sums[split:], 2, net.zl, net.y, net.on_zl, net.on_y
            )
            stages.append(stage)
            ends += end
        net.greet(peers)
        drive(*stages)
        for a in range(n):
            for h in range(2):
                outs[a][sums[a].h(h), :] = ends[a](h).astype(outs[a].dtype)
        net.finish()

    scratch = []
    for p in parts:
        scratch += Sum.scratch(p.shape[0], p.shape[2], p.shape[3], p.dtype)
    slots = split * reduce_slots(4) + (n - split) * reduce_slots(2)
    return call(
        kernel,
        collective_id,
        [like(p.shape[2:], d) for p, d in zip(parts, dtypes)],
        [VMEM] * n,
        [VMEM] * n,
        [*scratch, *sems(slots)],
        tuple(parts),
        name,
        cost,
    )


def softmax_narrow(logits, collective_id, name, cost):
    rows, columns = logits.shape

    def kernel(l_ref, p_ref, mine, got, send_sem, recv_sem):
        net = Net(send_sem, recv_sem)
        peers = [{"narrow": turn(net.narrow, k, 8)} for k in range(1, 8)]
        top = jnp.max(l_ref[...], axis=1, keepdims=True)
        mine[0] = jnp.broadcast_to(top, (rows, 128))
        mine[1] = jnp.broadcast_to(
            jnp.sum(jnp.exp(l_ref[...] - top), axis=1, keepdims=True), (rows, 128)
        )
        net.greet(peers)
        for k in range(7):
            net.send(k, mine, got.at[k], peers[k])
        for k in range(7):
            net.recv(k, got.at[k])
        largest = mine[0]
        for k in range(7):
            largest = jnp.maximum(largest, got[k, 0])
        total = mine[1] * jnp.exp(mine[0] - largest)
        for k in range(7):
            total += got[k, 1] * jnp.exp(got[k, 0] - largest)
        p_ref[...] = (jnp.exp(l_ref[...] - largest[:, :1]) / total[:, :1]).astype(BF16)
        net.finish()

    return call(
        kernel,
        collective_id,
        like((rows, columns), BF16),
        [VMEM],
        VMEM,
        [pltpu.VMEM((2, rows, 128), F32), pltpu.VMEM((7, 2, rows, 128), F32), *sems(7)],
        (logits,),
        name,
        cost,
    )


def gather_back(shard, collective_id, name, cost):
    _, rows, features = shard.shape

    def kernel(x_ref, o_ref, mine, local, send_sem, recv_sem):
        net = Net(send_sem, recv_sem)
        net.greet([net.on_y(1), net.on_y(3), net.on_zl(1), net.on_core()])
        net.send(0, x_ref.at[1 - net.core], mine, net.on_core())
        slot = lambda o, i, h: o_ref.at[o, i, lax.rem(net.core + h, 2)]
        own = lambda h: mine if h else x_ref.at[net.core]
        net.recv(0, mine)
        copies = [
            pltpu.make_async_copy(own(h), slot(net.zl, net.y, h), local.at[h]) for h in range(2)
        ]
        for copy in copies:
            copy.start()
        drive(gather_stage(net, 1, own, slot, 2, net.zl, net.y, net.on_zl, net.on_y))
        for copy in copies:
            copy.wait()
        net.finish()

    return call(
        kernel,
        collective_id,
        like((2, 4, 2, rows, features), shard.dtype),
        [ANY],
        ANY,
        [
            pltpu.VMEM((rows, features), shard.dtype),
            pltpu.SemaphoreType.DMA((2,)),
            *sems(1 + gather_slots(2)),
        ],
        (shard,),
        name,
        cost,
    )


def rotate_all(hidden, gate, bases, inputs, collective_id, name, cost):
    tokens, depth = gate.shape
    columns = bases[0].shape[0]
    rows = 2 * tokens

    def kernel(*refs):
        h_ref, g_ref = refs[:2]
        b_refs, i_ref, o_ref, j_ref = refs[2:6], refs[6], refs[7], refs[8]
        half_in, gated, other, every, part, fwd, mid, got, mine = refs[9:18]
        local, send_sem, recv_sem = refs[18:]
        net = Net(send_sem, recv_sem)
        ones = [net.on_x(1), net.on_x(3), net.on_z(1), net.on_z(3)]
        net.greet(ones + [net.on_y(1), net.on_y(3), net.on_zl(1), net.on_core()])
        c, z, x, zl, y = net.core, net.z, net.x, net.zl, net.y
        base_z, base_r, base_n = 8, 40, 64

        net.send(0, h_ref.at[1 - c], half_in, net.on_core())
        net.send(1, i_ref, j_ref, net.on_core())
        net.recv(0, half_in)

        def gate_rows(s):
            cut = pl.ds(pl.multiple_of(s * tokens, tokens), tokens)
            value = (h_ref[c, cut] + half_in[cut]) * g_ref[...].astype(F32)
            gated[s] = value.astype(BF16)

        for s in range(2):
            gate_rows(2 * (1 - zl) + s)
        net.send(2, gated.at[pl.ds(2 * (1 - zl), 2)], other, net.on_zl(1))
        for s in range(2):
            gate_rows(2 * zl + s)

        own = lambda h: other if h else gated.at[pl.ds(2 * zl, 2)]
        slot = lambda o, i, h: every.at[o, h, i]
        zp, zm, z2 = (turn(z, s, 4) for s in (1, 3, 2))
        xp, xm, x2 = (turn(x, s, 4) for s in (1, 3, 2))
        yp, ym, y2 = (turn(y, s, 4) for s in (1, 3, 2))
        order = (z, zm, zp, z2)
        inner = lambda row: base_z + 6 + 6 * row

        def along(row, h):
            o, b = order[row], inner(row)
            src = own(h) if row == 0 else slot(o, x, h)
            net.send(b + (0, 1)[h], src, slot(o, x, h), net.on_x(1))
            net.send(b + (3, 2)[h], src, slot(o, x, h), net.on_x(3))

        def forward(row):
            o, b = order[row], inner(row)
            net.recv(b, slot(o, xm, 0))
            net.send(b + 4, slot(o, xm, 0), slot(o, xm, 0), net.on_x(1))
            net.recv(b + 2, slot(o, xp, 1))
            net.send(b + 5, slot(o, xp, 1), slot(o, xp, 1), net.on_x(3))

        def rest(row):
            o, b = order[row], inner(row)
            net.recv(b + 1, slot(o, xm, 1))
            net.recv(b + 3, slot(o, xp, 0))
            net.recv(b + 4, slot(o, x2, 0))
            net.recv(b + 5, slot(o, x2, 1))

        def multiply(row):
            o = order[row]
            for m in range(2):
                block = None
                for h in range(2):
                    left = every[o, h].reshape(4 * rows, depth)
                    term = contract_last(left, b_refs[2 * h + m][...])
                    block = term if block is None else block + term
                part[row, :, m] = block.reshape(4, rows, columns)

        def reduce_start(k):
            b = base_r + 6 * k
            net.send(b, part.at[k, y2, 0], fwd.at[k, 0], net.on_y(1))
            net.send(b + 1, part.at[k, y2, 1], fwd.at[k, 1], net.on_y(3))
            net.send(b + 2, part.at[k, yp, 1], got.at[k, 0, 1], net.on_y(1))
            net.send(b + 3, part.at[k, ym, 0], got.at[k, 1, 0], net.on_y(3))

        def reduce_middle(k):
            b = base_r + 6 * k
            net.recv(b, fwd.at[k, 0])
            mid[k, 0] = part[k, yp, 0] + fwd[k, 0]
            net.send(b + 4, mid.at[k, 0], got.at[k, 0, 0], net.on_y(1))
            net.recv(b + 1, fwd.at[k, 1])
            mid[k, 1] = part[k, ym, 1] + fwd[k, 1]
            net.send(b + 5, mid.at[k, 1], got.at[k, 1, 1], net.on_y(3))

        def reduce_end(k):
            b = base_r + 6 * k
            net.recv(b + 2, got.at[k, 0, 1])
            net.recv(b + 5, got.at[k, 1, 1])
            value = part[k, y, 1] + got[k, 0, 1] + got[k, 1, 1]
            mine[k, 1] = value.astype(BF16).reshape(2, tokens, columns)
            net.send(3 + k, mine.at[k, 1], mine.at[k, 2], net.on_core())
            net.recv(b + 3, got.at[k, 1, 0])
            net.recv(b + 4, got.at[k, 0, 0])
            value = part[k, y, 0] + got[k, 0, 0] + got[k, 1, 0]
            mine[k, 0] = value.astype(BF16).reshape(2, tokens, columns)

        last = []

        def spread(k):
            mine_k = lambda h: mine.at[k, 2 * h]
            place = lambda o, i, h: o_ref.at[order[k], o, :, h, i]
            net.recv(3 + k, mine.at[k, 2])
            for h in range(2):
                copy = pltpu.make_async_copy(mine_k(h), place(zl, y, h), local.at[2 + 2 * k + h])
                copy.start()
                last.append(copy)
            base = base_n + gather_slots(2) * k
            return gather_stage(net, base, mine_k, place, 2, zl, y, net.on_zl, net.on_y)

        net.send(base_z, own(0), slot(z, x, 0), net.on_z(1))
        net.send(base_z + 3, own(0), slot(z, x, 0), net.on_z(3))
        along(0, 0)
        net.recv(2, other)
        net.send(base_z + 2, own(1), slot(z, x, 1), net.on_z(3))
        net.send(base_z + 1, own(1), slot(z, x, 1), net.on_z(1))
        along(0, 1)
        copies = [pltpu.make_async_copy(own(h), slot(z, x, h), local.at[h]) for h in range(2)]
        for copy in copies:
            copy.start()
        net.recv(base_z, slot(zm, x, 0))
        net.send(base_z + 4, slot(zm, x, 0), slot(zm, x, 0), net.on_z(1))
        net.recv(base_z + 2, slot(zp, x, 1))
        net.send(base_z + 5, slot(zp, x, 1), slot(zp, x, 1), net.on_z(3))
        forward(0)
        net.recv(base_z + 1, slot(zm, x, 1))
        for h in range(2):
            along(1, h)
        rest(0)
        for copy in copies:
            copy.wait()
        multiply(0)
        reduce_start(0)
        net.recv(base_z + 3, slot(zp, x, 0))
        for h in range(2):
            along(2, h)
        forward(1)
        reduce_middle(0)
        rest(1)
        multiply(1)
        reduce_start(1)
        net.recv(base_z + 4, slot(z2, x, 0))
        net.recv(base_z + 5, slot(z2, x, 1))
        for h in range(2):
            along(3, h)
        forward(2)
        reduce_end(0)
        reduce_middle(1)
        spread_0 = spread(0)
        next(spread_0)
        rest(2)
        multiply(2)
        reduce_start(2)
        forward(3)
        next(spread_0)
        reduce_end(1)
        reduce_middle(2)
        spread_1 = spread(1)
        next(spread_1)
        next(spread_0)
        rest(3)
        multiply(3)
        reduce_start(3)
        next(spread_1)
        reduce_end(2)
        reduce_middle(3)
        spread_2 = spread(2)
        next(spread_2)
        next(spread_1)
        reduce_end(3)
        spread_3 = spread(3)
        next(spread_3)
        drive(spread_0)
        for stage in (spread_2, spread_3, spread_2, spread_3):
            next(stage)
        drive(spread_1)
        drive(spread_2)
        drive(spread_3)
        for copy in last:
            copy.wait()
        net.recv(1, j_ref)
        net.finish()

    return call(
        kernel,
        collective_id,
        [like((4, 2, 2, 2, 4, tokens, columns), BF16), like(inputs.shape, BF16)],
        [VMEM] * 6 + [ANY],
        [ANY, ANY],
        [
            pltpu.VMEM((4 * tokens, depth), F32),
            pltpu.VMEM((4, tokens, depth), BF16),
            pltpu.VMEM((2, tokens, depth), BF16),
            pltpu.VMEM((4, 2, 4, 2, tokens, depth), BF16),
            pltpu.VMEM((4, 4, 2, rows, columns), F32),
            pltpu.VMEM((4, 2, rows, columns), F32),
            pltpu.VMEM((4, 2, rows, columns), F32),
            pltpu.VMEM((4, 2, 2, rows, columns), F32),
            pltpu.VMEM((4, 3, 2, tokens, columns), BF16),
            pltpu.SemaphoreType.DMA((10,)),
            *sems(64 + 4 * gather_slots(2)),
        ],
        (hidden, gate, *bases, inputs),
        name,
        cost,
    )


def squares(rotated, own_inputs, other_inputs):
    rows, width = rotated.shape[3], own_inputs.shape[2]
    depth = own_inputs.shape[1]

    def kernel(r_ref, a_ref, b_ref, o_ref, both):
        example, sample = pl.program_id(0), pl.program_id(1)

        @pl.when((example == 0) & (sample == 0))
        def _():
            o_ref[...] = jnp.zeros_like(o_ref)

        @pl.when(sample == 0)
        def _():
            both[:depth] = a_ref[0]
            both[depth:] = b_ref[0]

        block = lax.dot_general(
            r_ref[0, 0], both[...], (((0,), (0,)), ((), ())), preferred_element_type=F32
        )
        o_ref[...] += block * block * (1.0 / 16.0)

    return pl.pallas_call(
        kernel,
        grid=(4, 4),
        out_shape=like((rows, width), F32),
        in_specs=[
            pl.BlockSpec((1, 1, 2 * depth, rows), lambda e, s: (e, s, 0, 0)),
            pl.BlockSpec((1, depth, width), lambda e, s: (e, 0, 0)),
            pl.BlockSpec((1, depth, width), lambda e, s: (e, 0, 0)),
        ],
        out_specs=pl.BlockSpec((rows, width), lambda e, s: (0, 0)),
        scratch_shapes=[pltpu.VMEM((2 * depth, width), BF16)],
        name="squares",
    )(rotated, own_inputs, other_inputs)


def contract_last(left, right):
    return lax.dot_general(left, right, (((1,), (1,)), ((), ())), preferred_element_type=F32)


def per_device(
    resid, final_gain, unembed, labels, layer_in, gate_value, down_weight, basis_in, basis_out
):
    wide, narrow = lax.axis_index("wide"), lax.axis_index("narrow")
    core = lax.rem(wide, 2)
    tokens, width = resid.shape
    samples = labels.shape[1]
    vocab, part = unembed.shape
    hidden = down_weight.shape[0]
    columns = basis_out.shape[1]
    width_in = basis_in.shape[1]
    pair = 2 * part
    core_tokens = 16 * tokens
    few = tokens // 8

    resid_float = resid.astype(F32)
    inverse = lax.rsqrt(jnp.mean(resid_float * resid_float, axis=1) + EPSILON)
    normed = (resid_float * inverse[:, None] * final_gain).astype(BF16)

    def blocks(rows):
        return rows.reshape(tokens, 16, pair).transpose(1, 0, 2)

    normed_cols, inputs_cols, unembed_rows, basis_in_rows = exchange(
        [blocks(normed), blocks(layer_in)], [unembed.T, basis_in], 0, "exchange", 20
    )
    unembed_rows = unembed_rows.reshape(pair, vocab)
    basis_in_rows = basis_in_rows.reshape(pair, width_in)
    logits_part = jnp.dot(
        normed_cols.reshape(core_tokens, pair), unembed_rows, preferred_element_type=F32
    )
    inputs_part = jnp.dot(
        inputs_cols.reshape(core_tokens, pair), basis_in_rows, preferred_element_type=F32
    )
    mine = lax.dynamic_index_in_dim(
        labels.reshape(16, 2, 8, few, samples), core, 1, keepdims=False
    )
    shifted = mine.transpose(1, 0, 2, 3).reshape(core_tokens * samples) - narrow * vocab
    chosen = (shifted[:, None] == lax.broadcasted_iota(jnp.int32, (1, vocab), 1)).astype(BF16)
    picked = contract_last(chosen, unembed_rows).astype(BF16)
    logits, inputs_rot, picked = reduce_over(
        [logits_part.reshape(4, 4, tokens, vocab), inputs_part.reshape(4, 4, tokens, width_in)],
        [picked.reshape(2, 4, 16 * few * samples, pair)],
        [F32, BF16, BF16],
        1,
        "reduce_logits",
        45,
    )

    down_cols, basis_rows, logits = lax.optimization_barrier(
        (down_weight.T, basis_out.T, logits)
    )
    wide_count = lax.axis_size("wide")
    same_core = [list(range(c, wide_count, 2)) for c in range(2)]
    down_rows = lax.all_gather(
        down_cols, "wide", axis=0, tiled=True, axis_index_groups=same_core
    )
    to_core = [(w, w + 1 - 2 * (w % 2)) for w in range(wide_count)]
    to_zl = [(n, (n + 4) % 8) for n in range(8)]
    basis_zl = lax.ppermute(basis_rows, "narrow", to_zl)
    bases = [
        basis_rows,
        lax.ppermute(basis_rows, "wide", to_core),
        basis_zl,
        lax.ppermute(basis_zl, "wide", to_core),
    ]

    probs = softmax_narrow(logits, 2, "softmax", 6)
    both = jnp.concatenate([probs, inputs_rot], axis=1)
    both = gather_wide(both.reshape(2, tokens // 2, vocab + width_in), 3, "gather_probs", 24)
    both = both.reshape(core_tokens, vocab + width_in)
    inputs_all = both[:, vocab:].reshape(4, 4 * tokens, width_in)
    common = contract_last(both[:, :vocab], unembed_rows)
    common = common.reshape(16, 8, few, pair).transpose(1, 0, 2, 3).reshape(2, 4, 16 * few, pair)
    (common,) = reduce_over([], [common], [F32], 4, "reduce_common", 10)
    grads = common.reshape(16, few, 1, pair) - picked.astype(F32).reshape(16, few, samples, pair)
    (grads,) = exchange([grads.reshape(16, few * samples, pair)], [], 5, "exchange_grads", 12)
    grads = grads.transpose(1, 0, 2).reshape(few, samples, width)
    resid_few = lax.dynamic_slice_in_dim(resid_float, narrow * few, few, 0)
    inverse_few = lax.dynamic_slice_in_dim(inverse, narrow * few, few, 0)
    inner = jnp.sum(final_gain * grads * resid_few[:, None, :], axis=2)
    back = (
        inverse_few[:, None, None] * final_gain * grads
        - resid_few[:, None, :] * (inverse_few**3)[:, None, None] * inner[:, :, None] / width
    )
    back = back.astype(BF16).reshape(few * samples, 16, 2, part).transpose(2, 0, 1, 3)
    back = gather_back(back.reshape(2, few * samples, width // 2), 6, "gather_back", 16)
    back = back.reshape(8, 2, few, samples, width // 2).transpose(1, 3, 0, 2, 4)
    hidden_part = jnp.dot(
        back.reshape(2 * tokens * samples, width // 2), down_rows, preferred_element_type=F32
    )
    rotated, inputs_other = rotate_all(
        hidden_part.reshape(2, samples * tokens, hidden),
        gate_value,
        bases,
        inputs_all,
        7,
        "rotate_all",
        90,
    )
    return squares(
        rotated.reshape(4, samples, 8 * tokens, columns), inputs_all, inputs_other
    )


def solution(mesh):
    in_specs = (
        P("wide", None),
        P(),
        P("narrow", "wide"),
        P(),
        P("wide", None),
        P("wide", "narrow"),
        P("narrow", "wide"),
        P("wide", "narrow"),
        P("narrow", "wide"),
    )
    out_specs = P("wide", "narrow")
    return jax.shard_map(
        per_device, mesh=mesh, in_specs=in_specs, out_specs=out_specs, check_vma=False
    )
```

```python
import functools

import jax
import jax.numpy as jnp
from jax import lax
from jax.experimental import pallas as pl
from jax.experimental.pallas import tpu as pltpu
from jax.sharding import PartitionSpec as P

EPSILON = 1e-05
MESH = pl.DeviceIdType.MESH
F32 = jnp.float32
BF16 = jnp.bfloat16
ANY = pl.BlockSpec(memory_space=pl.ANY)
VMEM = pl.BlockSpec(memory_space=pltpu.VMEM)


class Net:
    def __init__(self, send_sem, recv_sem):
        self.send_sem, self.recv_sem = send_sem, recv_sem
        self.started = []
        wide, narrow = lax.axis_index("wide"), lax.axis_index("narrow")
        self.wide, self.narrow = wide, narrow
        self.core = lax.rem(wide, 2)
        self.x = lax.rem(lax.div(wide, 2), 4)
        self.z = lax.div(wide, 8)
        self.y = lax.rem(narrow, 4)
        self.zl = lax.div(narrow, 4)

    def on_x(self, step):
        return {"wide": self.z * 8 + lax.rem(self.x + step, 4) * 2 + self.core}

    def on_z(self, step):
        return {"wide": lax.rem(self.z + step, 4) * 8 + self.x * 2 + self.core}

    def on_y(self, step):
        return {"narrow": self.zl * 4 + lax.rem(self.y + step, 4)}

    def on_zl(self, step):
        return {"narrow": (1 - self.zl) * 4 + self.y}

    def on_core(self):
        return {"wide": self.wide + 1 - 2 * self.core}

    def greet(self, devices):
        barrier = pltpu.get_barrier_semaphore()
        for device in devices:
            pl.semaphore_signal(barrier, inc=1, device_id=device, device_id_type=MESH)
        pl.semaphore_wait(barrier, len(devices))

    def copy(self, slot, src, dst, device):
        return pltpu.make_async_remote_copy(
            src_ref=src,
            dst_ref=dst,
            send_sem=self.send_sem.at[slot],
            recv_sem=self.recv_sem.at[slot],
            device_id=device,
            device_id_type=MESH,
        )

    def send(self, slot, src, dst, device):
        copy = self.copy(slot, src, dst, device)
        copy.start()
        self.started.append(copy)

    def recv(self, slot, dst):
        self.copy(slot, dst, dst, self.on_core()).wait_recv()

    def finish(self):
        for copy in self.started:
            copy.wait_send()


def turn(place, step, size):
    return lax.rem(place + step, size)


def gather_stage(net, base, own, slot, outer_size, me_o, me_i, on_o, on_i):
    ip, im, i2 = (turn(me_i, s, 4) for s in (1, 3, 2))
    inner = lambda row: base + 6 + 6 * row

    def along(row, o, first):
        b = inner(row)
        src = own if first else (lambda h: slot(o, me_i, h))
        net.send(b, src(0), slot(o, me_i, 0), on_i(1))
        net.send(b + 2, src(1), slot(o, me_i, 1), on_i(3))
        net.send(b + 1, src(1), slot(o, me_i, 1), on_i(1))
        net.send(b + 3, src(0), slot(o, me_i, 0), on_i(3))

    def forward(row, o):
        b = inner(row)
        net.recv(b, slot(o, im, 0))
        net.send(b + 4, slot(o, im, 0), slot(o, im, 0), on_i(1))
        net.recv(b + 2, slot(o, ip, 1))
        net.send(b + 5, slot(o, ip, 1), slot(o, ip, 1), on_i(3))

    def rest(row, o):
        b = inner(row)
        net.recv(b + 1, slot(o, im, 1))
        net.recv(b + 3, slot(o, ip, 0))
        net.recv(b + 4, slot(o, i2, 0))
        net.recv(b + 5, slot(o, i2, 1))

    if outer_size == 4:
        op, om, o2 = (turn(me_o, s, 4) for s in (1, 3, 2))
        net.send(base, own(0), slot(me_o, me_i, 0), on_o(1))
        net.send(base + 2, own(1), slot(me_o, me_i, 1), on_o(3))
        net.send(base + 1, own(1), slot(me_o, me_i, 1), on_o(1))
        net.send(base + 3, own(0), slot(me_o, me_i, 0), on_o(3))
        along(0, me_o, True)
        yield
        net.recv(base, slot(om, me_i, 0))
        net.send(base + 4, slot(om, me_i, 0), slot(om, me_i, 0), on_o(1))
        net.recv(base + 2, slot(op, me_i, 1))
        net.send(base + 5, slot(op, me_i, 1), slot(op, me_i, 1), on_o(3))
        forward(0, me_o)
        net.recv(base + 1, slot(om, me_i, 1))
        along(1, om, False)
        yield
        net.recv(base + 3, slot(op, me_i, 0))
        along(2, op, False)
        forward(1, om)
        yield
        net.recv(base + 4, slot(o2, me_i, 0))
        net.recv(base + 5, slot(o2, me_i, 1))
        along(3, o2, False)
        forward(2, op)
        yield
        forward(3, o2)
        for row, o in enumerate((me_o, om, op, o2)):
            rest(row, o)
    else:
        oq = 1 - me_o
        for h in range(2):
            net.send(base + h, own(h), slot(me_o, me_i, h), on_o(1))
        along(0, me_o, True)
        yield
        forward(0, me_o)
        for h in range(2):
            net.recv(base + h, slot(oq, me_i, h))
        along(1, oq, False)
        yield
        forward(1, oq)
        yield
        rest(0, me_o)
        rest(1, oq)


def gather_slots(outer_size):
    return 6 + 6 * outer_size


class Sum:
    def __init__(self, part, fwd, mid, got, tot, zfwd, zgot):
        self.part, self.fwd, self.mid, self.got = part, fwd, mid, got
        self.tot, self.zfwd, self.zgot = tot, zfwd, zgot
        self.half = part.shape[2] // 2

    @staticmethod
    def scratch(outer, rows, columns, dtype):
        half = rows // 2
        return [
            pltpu.VMEM((outer, 2, half, columns), dtype),
            pltpu.VMEM((outer, 2, half, columns), dtype),
            pltpu.VMEM((outer, 2, rows, columns), dtype),
            pltpu.VMEM((outer, rows, columns), dtype),
            pltpu.VMEM((2, half, columns), dtype),
            pltpu.VMEM((2, rows, columns), dtype),
        ]

    def h(self, k):
        return pl.ds(k * self.half, self.half)


def reduce_slots(outer_size):
    return 6 * outer_size + 6


def reduce_stage(net, base, sums, outer_size, me_o, me_i, on_o, on_i):
    ip, im, i2 = (turn(me_i, s, 4) for s in (1, 3, 2))
    offsets = (2, 1, 3, 0) if outer_size == 4 else (1, 0)
    rows = [turn(me_o, off, outer_size) for off in offsets]
    count = reduce_slots(outer_size)

    def at(a, k, j):
        return base + a * count + 6 * k + j

    def start_far(k):
        for a, s in enumerate(sums):
            net.send(at(a, k, 0), s.part.at[rows[k], i2, s.h(0)], s.fwd.at[k, 0], on_i(1))
            net.send(at(a, k, 1), s.part.at[rows[k], i2, s.h(1)], s.fwd.at[k, 1], on_i(3))

    def start_near(k):
        for a, s in enumerate(sums):
            net.send(at(a, k, 2), s.part.at[rows[k], ip, s.h(1)], s.got.at[k, 0, s.h(1)], on_i(1))
            net.send(at(a, k, 3), s.part.at[rows[k], im, s.h(0)], s.got.at[k, 1, s.h(0)], on_i(3))

    def middle(k):
        for a, s in enumerate(sums):
            net.recv(at(a, k, 0), s.fwd.at[k, 0])
            s.mid[k, 0] = s.part[rows[k], ip, s.h(0)] + s.fwd[k, 0]
            net.send(at(a, k, 4), s.mid.at[k, 0], s.got.at[k, 0, s.h(0)], on_i(1))
            net.recv(at(a, k, 1), s.fwd.at[k, 1])
            s.mid[k, 1] = s.part[rows[k], im, s.h(1)] + s.fwd[k, 1]
            net.send(at(a, k, 5), s.mid.at[k, 1], s.got.at[k, 1, s.h(1)], on_i(3))

    def total(k):
        for a, s in enumerate(sums):
            z = base + a * count + 6 * outer_size
            net.recv(at(a, k, 2), s.got.at[k, 0, s.h(1)])
            net.recv(at(a, k, 3), s.got.at[k, 1, s.h(0)])
            net.recv(at(a, k, 4), s.got.at[k, 0, s.h(0)])
            net.recv(at(a, k, 5), s.got.at[k, 1, s.h(1)])
            for h in range(2):
                s.tot[k, s.h(h)] = (
                    s.part[rows[k], me_i, s.h(h)] + s.got[k, 0, s.h(h)] + s.got[k, 1, s.h(h)]
                )
            if outer_size == 2:
                if k == 0:
                    for h in range(2):
                        net.send(z + h, s.tot.at[0, s.h(h)], s.zgot.at[0, s.h(h)], on_o(1))
            elif k == 0:
                net.send(z, s.tot.at[0, s.h(0)], s.zfwd.at[0], on_o(1))
                net.send(z + 1, s.tot.at[0, s.h(1)], s.zfwd.at[1], on_o(3))
            elif k == 1:
                net.send(z + 2, s.tot.at[1, s.h(1)], s.zgot.at[0, s.h(1)], on_o(1))
                net.recv(z, s.zfwd.at[0])
                s.tot[1, s.h(0)] += s.zfwd[0]
                net.send(z + 3, s.tot.at[1, s.h(0)], s.zgot.at[0, s.h(0)], on_o(1))
            elif k == 2:
                net.send(z + 4, s.tot.at[2, s.h(0)], s.zgot.at[1, s.h(0)], on_o(3))
                net.recv(z + 1, s.zfwd.at[1])
                s.tot[2, s.h(1)] += s.zfwd[1]
                net.send(z + 5, s.tot.at[2, s.h(1)], s.zgot.at[1, s.h(1)], on_o(3))

    def steps():
        start_far(0)
        start_far(1)
        start_near(0)
        yield
        for k in range(outer_size):
            if k + 2 < outer_size:
                start_far(k + 2)
            if k + 1 < outer_size:
                start_near(k + 1)
            middle(k)
            if k >= 1:
                total(k - 1)
            yield
        total(outer_size - 1)

    def final(a):
        s = sums[a]
        z = base + a * count + 6 * outer_size
        last = outer_size - 1

        def value(h):
            if outer_size == 2:
                net.recv(z + h, s.zgot.at[0, s.h(h)])
                return s.tot[last, s.h(h)] + s.zgot[0, s.h(h)]
            first, second = ((z + 3, z + 4), (z + 2, z + 5))[h]
            net.recv(first, s.zgot.at[0, s.h(h)])
            net.recv(second, s.zgot.at[1, s.h(h)])
            return s.tot[last, s.h(h)] + s.zgot[0, s.h(h)] + s.zgot[1, s.h(h)]

        return value

    return steps(), [final(a) for a in range(len(sums))]


def drive(*stages):
    stages = list(stages)
    while stages:
        stages = [stage for stage in stages if next(stage, 0) is None]


def ring(net, base, own, slot, me, on):
    plus, minus, far = (turn(me, s, 4) for s in (1, 3, 2))
    net.send(base, own(0), slot(me, 0), on(1))
    net.send(base + 2, own(1), slot(me, 1), on(3))
    yield
    net.send(base + 1, own(1), slot(me, 1), on(1))
    net.send(base + 3, own(0), slot(me, 0), on(3))
    yield
    net.recv(base, slot(minus, 0))
    net.send(base + 4, slot(minus, 0), slot(minus, 0), on(1))
    net.recv(base + 2, slot(plus, 1))
    net.send(base + 5, slot(plus, 1), slot(plus, 1), on(3))
    yield
    net.recv(base + 1, slot(minus, 1))
    net.recv(base + 3, slot(plus, 0))
    net.recv(base + 4, slot(far, 0))
    net.recv(base + 5, slot(far, 1))


class Side:
    def __init__(self, tasks):
        self.tasks = tasks
        self.arrays = [array for _, array, _ in tasks]
        self.outs = []
        for kind, array, _ in tasks:
            rows, depth = array.shape[-2:]
            shape = (2, rows // 3, depth) if kind == "basis" else (4, rows, depth)
            self.outs.append(like(shape, array.dtype))
        self.slots = 6 * len(tasks)

    def local(self):
        return [pltpu.SemaphoreType.DMA((max(len(self.tasks), 1),))]

    def peers(self, net):
        found = []
        for kind, _, _ in self.tasks:
            if kind == "x":
                found += [net.on_x(1), net.on_x(3)]
            elif kind == "z":
                found += [net.on_z(1), net.on_z(3)]
            else:
                found += [net.on_zl(1), net.on_core()]
        return found

    def stages(self, net, base, ins, outs, local):
        return [
            self.stage(net, base + 6 * t, kind, ins[t], outs[t], step, local.at[t])
            for t, (kind, _, step) in enumerate(self.tasks)
        ]

    def stage(self, net, base, kind, src, out, step, local):
        if kind == "basis":
            rows = out.shape[1]
            net.send(base, src.at[pl.ds(rows * step, rows)], out.at[0], net.on_zl(1))
            yield
            yield
            net.recv(base, out.at[0])
            net.send(base + 1, out.at[0], out.at[1], net.on_core())
            yield
            net.recv(base + 1, out.at[1])
            return
        half = out.shape[1] // 2
        cut = lambda h: pl.ds(h * half, half)
        row = src if len(src.shape) == 2 else src.at[turn(net.z, step, 4)]
        own = lambda h: row.at[cut(h)]
        slot = lambda i, h: out.at[i, cut(h)]
        if kind == "z":
            yield from ring(net, base, own, slot, net.z, net.on_z)
        else:
            copy = pltpu.make_async_copy(row, out.at[net.x], local)
            copy.start()
            yield from ring(net, base, own, slot, net.x, net.on_x)
            copy.wait()


def sems(slots):
    return [pltpu.SemaphoreType.DMA((slots,)), pltpu.SemaphoreType.DMA((slots,))]


def call(kernel, collective_id, outs, in_specs, out_specs, scratch, args, name, cost):
    return pl.pallas_call(
        kernel,
        out_shape=outs,
        in_specs=in_specs,
        out_specs=out_specs,
        scratch_shapes=scratch,
        compiler_params=pltpu.CompilerParams(
            collective_id=collective_id, has_side_effects=True, vmem_limit_bytes=60 << 20
        ),
        cost_estimate=pl.CostEstimate(flops=cost * 10**9, bytes_accessed=0, transcendentals=0),
        name=name,
    )(*args)


def like(shape, dtype):
    return jax.ShapeDtypeStruct(shape, dtype)


def exchange(arrays, pairs, tasks, collective_id, name, cost):
    na, np_, nt = len(arrays), len(pairs), len(tasks)
    side = Side(tasks)

    def kernel(*refs):
        ins, shared, side_in = refs[:na], refs[na : na + np_], refs[na + np_ : na + np_ + nt]
        refs = refs[na + np_ + nt :]
        outs, both, side_out = refs[:na], refs[na : na + np_], refs[na + np_ : na + np_ + nt]
        local, side_local, send_sem, recv_sem = refs[na + np_ + nt :]
        net = Net(send_sem, recv_sem)
        steps = [(dz, dx) for dz in range(4) for dx in range(4) if (dz, dx) != (0, 0)]
        steps.sort(key=lambda s: -(min(s[0], 4 - s[0]) * 2 + min(s[1], 4 - s[1])))

        def to(dz, dx):
            return turn(net.z, dz, 4) * 4 + turn(net.x, dx, 4)

        me = net.z * 4 + net.x
        peers = [{"wide": to(*s) * 2 + net.core} for s in steps]
        net.greet(peers + ([net.on_core()] if np_ else []) + side.peers(net))
        copies = []
        for j, s in enumerate(steps):
            for a in range(na):
                net.send(j * na + a, ins[a].at[to(*s)], outs[a].at[me], peers[j])
        for a in range(na):
            copies.append(pltpu.make_async_copy(ins[a].at[me], outs[a].at[me], local.at[a]))
        for b in range(np_):
            net.send(15 * na + b, shared[b], both[b].at[net.core], net.on_core())
            copies.append(
                pltpu.make_async_copy(shared[b], both[b].at[net.core], local.at[na + b])
            )
        for copy in copies:
            copy.start()
        extra = side.stages(net, 15 * na + max(np_, 1), side_in, side_out, side_local)
        for _ in range(3):
            for stage in extra:
                next(stage)
        for j, (dz, dx) in enumerate(steps):
            source = to((4 - dz) % 4, (4 - dx) % 4)
            for a in range(na):
                net.recv(j * na + a, outs[a].at[source])
        for b in range(np_):
            net.recv(15 * na + b, both[b].at[1 - net.core])
        drive(*extra)
        for copy in copies:
            copy.wait()
        net.finish()

    outs = [like(a.shape, a.dtype) for a in arrays] + [like((2, *p.shape), p.dtype) for p in pairs]
    return call(
        kernel,
        collective_id,
        outs + side.outs,
        [ANY] * (na + np_ + nt),
        [ANY] * (na + np_ + nt),
        [
            pltpu.SemaphoreType.DMA((na + np_,)),
            *side.local(),
            *sems(15 * na + max(np_, 1) + side.slots),
        ],
        (*arrays, *pairs, *side.arrays),
        name,
        cost,
    )


def gather_wide(shards, tasks, collective_id, name, cost):
    n, nt = len(shards), len(tasks)
    side = Side(tasks)

    def kernel(*refs):
        ins, side_in = refs[:n], refs[n : n + nt]
        outs, side_out = refs[n + nt : 2 * n + nt], refs[2 * n + nt : 2 * (n + nt)]
        local, side_local, send_sem, recv_sem = refs[2 * (n + nt) :]
        net = Net(send_sem, recv_sem)
        ones = [net.on_x(1), net.on_x(3), net.on_z(1), net.on_z(3)]
        net.greet(ones + side.peers(net))
        copies, stages = [], []

        def stage(a):
            half = ins[a].shape[0] // 2
            slot = lambda o, i, h: outs[a].at[o, i, pl.ds(h * half, half)]
            own = lambda h: ins[a].at[pl.ds(h * half, half)]
            for h in range(2):
                copy = pltpu.make_async_copy(
                    own(h), slot(net.z, net.x, h), local.at[2 * a + h]
                )
                copy.start()
                copies.append(copy)
            base = gather_slots(4) * a
            return gather_stage(net, base, own, slot, 4, net.z, net.x, net.on_z, net.on_x)

        stages = [stage(a) for a in range(n)]
        drive(*stages, *side.stages(net, gather_slots(4) * n, side_in, side_out, side_local))
        for copy in copies:
            copy.wait()
        net.finish()

    return call(
        kernel,
        collective_id,
        [like((4, 4, *shard.shape), shard.dtype) for shard in shards] + side.outs,
        [ANY] * (n + nt),
        [ANY] * (n + nt),
        [
            pltpu.SemaphoreType.DMA((2 * n,)),
            *side.local(),
            *sems(gather_slots(4) * n + side.slots),
        ],
        (*shards, *side.arrays),
        name,
        cost,
    )


def reduce_over(wide_parts, narrow_parts, tasks, dtypes, collective_id, name, cost):
    parts = [*wide_parts, *narrow_parts]
    n, split, nt = len(parts), len(wide_parts), len(tasks)
    side = Side(tasks)
    slots = split * reduce_slots(4) + (n - split) * reduce_slots(2)

    def kernel(*refs):
        ins, side_in = refs[:n], refs[n : n + nt]
        outs, side_out = refs[n + nt : 2 * n + nt], refs[2 * n + nt : 2 * (n + nt)]
        buffers, (side_local, send_sem, recv_sem) = refs[2 * (n + nt) : -3], refs[-3:]
        net = Net(send_sem, recv_sem)
        sums = [Sum(ins[a], *buffers[6 * a : 6 * a + 6]) for a in range(n)]
        stages, ends, peers = [], [], []
        if split:
            peers += [net.on_x(1), net.on_x(3), net.on_z(1), net.on_z(3)]
            stage, end = reduce_stage(net, 0, sums[:split], 4, net.z, net.x, net.on_z, net.on_x)
            stages.append(stage)
            ends += end
        if n > split:
            peers += [net.on_y(1), net.on_y(3), net.on_zl(1)]
            base = split * reduce_slots(4)
            stage, end = reduce_stage(
                net, base, sums[split:], 2, net.zl, net.y, net.on_zl, net.on_y
            )
            stages.append(stage)
            ends += end
        net.greet(peers + side.peers(net))
        extra = side.stages(net, slots, side_in, side_out, side_local)
        drive(*stages, *extra)
        for a in range(n):
            for h in range(2):
                outs[a][sums[a].h(h), :] = ends[a](h).astype(outs[a].dtype)
        net.finish()

    scratch = []
    for p in parts:
        scratch += Sum.scratch(p.shape[0], p.shape[2], p.shape[3], p.dtype)
    return call(
        kernel,
        collective_id,
        [like(p.shape[2:], d) for p, d in zip(parts, dtypes)] + side.outs,
        [VMEM] * n + [ANY] * nt,
        [VMEM] * n + [ANY] * nt,
        [*scratch, *side.local(), *sems(slots + side.slots)],
        (*parts, *side.arrays),
        name,
        cost,
    )


def softmax_narrow(logits, tasks, collective_id, name, cost):
    rows, columns = logits.shape
    side, nt = Side(tasks), len(tasks)

    def kernel(*refs):
        l_ref, side_in, p_ref, side_out = refs[0], refs[1 : 1 + nt], refs[1 + nt], refs[2 + nt : -5]
        mine, got, side_local, send_sem, recv_sem = refs[-5:]
        net = Net(send_sem, recv_sem)
        peers = [{"narrow": turn(net.narrow, k, 8)} for k in range(1, 8)]
        top = jnp.max(l_ref[...], axis=1, keepdims=True)
        mine[0] = jnp.broadcast_to(top, (rows, 128))
        mine[1] = jnp.broadcast_to(
            jnp.sum(jnp.exp(l_ref[...] - top), axis=1, keepdims=True), (rows, 128)
        )
        net.greet(peers + side.peers(net))
        for k in range(7):
            net.send(k, mine, got.at[k], peers[k])
        extra = side.stages(net, 7, side_in, side_out, side_local)
        for _ in range(2):
            for stage in extra:
                next(stage)
        for k in range(7):
            net.recv(k, got.at[k])
        largest = mine[0]
        for k in range(7):
            largest = jnp.maximum(largest, got[k, 0])
        total = mine[1] * jnp.exp(mine[0] - largest)
        for k in range(7):
            total += got[k, 1] * jnp.exp(got[k, 0] - largest)
        p_ref[...] = (jnp.exp(l_ref[...] - largest[:, :1]) / total[:, :1]).astype(BF16)
        drive(*extra)
        net.finish()

    return call(
        kernel,
        collective_id,
        [like((rows, columns), BF16)] + side.outs,
        [VMEM] + [ANY] * nt,
        [VMEM] + [ANY] * nt,
        [
            pltpu.VMEM((2, rows, 128), F32),
            pltpu.VMEM((7, 2, rows, 128), F32),
            *side.local(),
            *sems(7 + side.slots),
        ],
        (logits, *side.arrays),
        name,
        cost,
    )


def gather_back(shard, tasks, collective_id, name, cost):
    _, rows, features = shard.shape
    side, nt = Side(tasks), len(tasks)

    def kernel(*refs):
        x_ref, side_in, o_ref, side_out = refs[0], refs[1 : 1 + nt], refs[1 + nt], refs[2 + nt : -5]
        mine, local, side_local, send_sem, recv_sem = refs[-5:]
        net = Net(send_sem, recv_sem)
        net.greet([net.on_y(1), net.on_y(3), net.on_zl(1), net.on_core()] + side.peers(net))
        net.send(0, x_ref.at[1 - net.core], mine, net.on_core())
        slot = lambda o, i, h: o_ref.at[o, i, lax.rem(net.core + h, 2)]
        own = lambda h: mine if h else x_ref.at[net.core]
        net.recv(0, mine)
        copies = [
            pltpu.make_async_copy(own(h), slot(net.zl, net.y, h), local.at[h]) for h in range(2)
        ]
        for copy in copies:
            copy.start()
        drive(
            gather_stage(net, 1, own, slot, 2, net.zl, net.y, net.on_zl, net.on_y),
            *side.stages(net, 1 + gather_slots(2), side_in, side_out, side_local),
        )
        for copy in copies:
            copy.wait()
        net.finish()

    return call(
        kernel,
        collective_id,
        [like((2, 4, 2, rows, features), shard.dtype)] + side.outs,
        [ANY] * (1 + nt),
        [ANY] * (1 + nt),
        [
            pltpu.VMEM((rows, features), shard.dtype),
            pltpu.SemaphoreType.DMA((2,)),
            *side.local(),
            *sems(1 + gather_slots(2) + side.slots),
        ],
        (shard, *side.arrays),
        name,
        cost,
    )


def rotate_all(back, gate, downs, basis, thirds, inputs, collective_id, name, cost):
    tokens, depth = gate.shape
    columns = basis.shape[1]
    rows = 2 * tokens
    features = back.shape[2]
    cuts = (pl.ds(0, 896), pl.ds(896, depth - 896))

    def kernel(*refs):
        back_ref, g_ref, d_refs, basis_ref = refs[0], refs[1], refs[2:6], refs[6]
        t_refs, i_ref, o_ref, j_ref = refs[7:10], refs[10], refs[11], refs[12]
        down, bases, h_ref = refs[13:16]
        half_in, gated, other, every, part, fwd, mid, got, mine = refs[16:25]
        local, send_sem, recv_sem = refs[25:]
        net = Net(send_sem, recv_sem)
        c, z, x, zl, y = net.core, net.z, net.x, net.zl, net.y
        base_z, base_r, base_n = 8, 40, 64
        loads = [
            pltpu.make_async_copy(d_refs[k], down.at[k], local.at[10 + k]) for k in range(4)
        ]
        loads += [
            pltpu.make_async_copy(basis_ref.at[c], bases.at[0], local.at[14]),
            pltpu.make_async_copy(basis_ref.at[1 - c], bases.at[1], local.at[15]),
        ]
        third = columns // 3
        for j in range(3):
            for m in range(2):
                loads.append(
                    pltpu.make_async_copy(
                        t_refs[j].at[m],
                        bases.at[2 + m, pl.ds(j * third, third)],
                        local.at[16 + 2 * j + m],
                    )
                )
        for load in loads:
            load.start()
        ones = [net.on_x(1), net.on_x(3), net.on_z(1), net.on_z(3)]
        net.greet(ones + [net.on_y(1), net.on_y(3), net.on_zl(1), net.on_core()])
        for load in loads[:4]:
            load.wait()
        quarter = features // 4
        left = back_ref[...].reshape(2 * 4 * tokens, features)
        for j, cut in enumerate(cuts):
            total = None
            for k in range(4):
                right = down[k, :, :, cut].reshape(quarter, cut.size)
                term = jnp.dot(
                    left[:, k * quarter : (k + 1) * quarter], right, preferred_element_type=F32
                )
                total = term if total is None else total + term
            h_ref[:, :, cut] = total.reshape(2, 4 * tokens, cut.size)
            net.send((0, 7)[j], h_ref.at[1 - c, :, cut], half_in.at[:, cut], net.on_core())
        net.send(1, i_ref, j_ref, net.on_core())

        def gate_rows(s, cut):
            some = pl.ds(pl.multiple_of(s * tokens, tokens), tokens)
            value = (h_ref[c, some, cut] + half_in[some, cut]) * g_ref[:, cut].astype(F32)
            gated[s, :, cut] = value.astype(BF16)

        for j, cut in enumerate(cuts):
            net.recv((0, 7)[j], half_in.at[:, cut])
            for s in range(2):
                gate_rows(2 * zl + s, cut)

        own = lambda h: other if h else gated.at[pl.ds(2 * zl, 2)]
        slot = lambda o, i, h: every.at[o, h, i]
        zp, zm, z2 = (turn(z, s, 4) for s in (1, 3, 2))
        xp, xm, x2 = (turn(x, s, 4) for s in (1, 3, 2))
        yp, ym, y2 = (turn(y, s, 4) for s in (1, 3, 2))
        order = (z, zm, zp, z2)
        inner = lambda row: base_z + 6 + 6 * row

        def along(row, h):
            o, b = order[row], inner(row)
            src = own(h) if row == 0 else slot(o, x, h)
            net.send(b + (0, 1)[h], src, slot(o, x, h), net.on_x(1))
            net.send(b + (3, 2)[h], src, slot(o, x, h), net.on_x(3))

        def forward(row):
            o, b = order[row], inner(row)
            net.recv(b, slot(o, xm, 0))
            net.send(b + 4, slot(o, xm, 0), slot(o, xm, 0), net.on_x(1))
            net.recv(b + 2, slot(o, xp, 1))
            net.send(b + 5, slot(o, xp, 1), slot(o, xp, 1), net.on_x(3))

        def rest(row):
            o, b = order[row], inner(row)
            net.recv(b + 1, slot(o, xm, 1))
            net.recv(b + 3, slot(o, xp, 0))
            net.recv(b + 4, slot(o, x2, 0))
            net.recv(b + 5, slot(o, x2, 1))

        def multiply(row):
            o = order[row]
            for m in range(2):
                block = None
                for h in range(2):
                    left = every[o, h].reshape(4 * rows, depth)
                    term = contract_last(left, bases[2 * h + m])
                    block = term if block is None else block + term
                part[row, :, m] = block.reshape(4, rows, columns)

        def reduce_start(k):
            b = base_r + 6 * k
            net.send(b, part.at[k, y2, 0], fwd.at[k, 0], net.on_y(1))
            net.send(b + 1, part.at[k, y2, 1], fwd.at[k, 1], net.on_y(3))
            net.send(b + 2, part.at[k, yp, 1], got.at[k, 0, 1], net.on_y(1))
            net.send(b + 3, part.at[k, ym, 0], got.at[k, 1, 0], net.on_y(3))

        def reduce_middle(k):
            b = base_r + 6 * k
            net.recv(b, fwd.at[k, 0])
            mid[k, 0] = part[k, yp, 0] + fwd[k, 0]
            net.send(b + 4, mid.at[k, 0], got.at[k, 0, 0], net.on_y(1))
            net.recv(b + 1, fwd.at[k, 1])
            mid[k, 1] = part[k, ym, 1] + fwd[k, 1]
            net.send(b + 5, mid.at[k, 1], got.at[k, 1, 1], net.on_y(3))

        def reduce_end(k):
            b = base_r + 6 * k
            net.recv(b + 2, got.at[k, 0, 1])
            net.recv(b + 5, got.at[k, 1, 1])
            value = part[k, y, 1] + got[k, 0, 1] + got[k, 1, 1]
            mine[k, 1] = value.astype(BF16).reshape(2, tokens, columns)
            net.send(3 + k, mine.at[k, 1], mine.at[k, 2], net.on_core())
            net.recv(b + 3, got.at[k, 1, 0])
            net.recv(b + 4, got.at[k, 0, 0])
            value = part[k, y, 0] + got[k, 0, 0] + got[k, 1, 0]
            mine[k, 0] = value.astype(BF16).reshape(2, tokens, columns)

        last = []

        def spread(k):
            mine_k = lambda h: mine.at[k, 2 * h]
            place = lambda o, i, h: o_ref.at[order[k], o, :, h, i]
            net.recv(3 + k, mine.at[k, 2])
            for h in range(2):
                copy = pltpu.make_async_copy(mine_k(h), place(zl, y, h), local.at[2 + 2 * k + h])
                copy.start()
                last.append(copy)
            base = base_n + gather_slots(2) * k
            return gather_stage(net, base, mine_k, place, 2, zl, y, net.on_zl, net.on_y)

        net.send(base_z, own(0), slot(z, x, 0), net.on_z(1))
        net.send(base_z + 3, own(0), slot(z, x, 0), net.on_z(3))
        along(0, 0)
        for cut in cuts:
            for s in range(2):
                gate_rows(2 * (1 - zl) + s, cut)
        net.send(2, gated.at[pl.ds(2 * (1 - zl), 2)], other, net.on_zl(1))
        net.recv(2, other)
        net.send(base_z + 2, own(1), slot(z, x, 1), net.on_z(3))
        net.send(base_z + 1, own(1), slot(z, x, 1), net.on_z(1))
        along(0, 1)
        copies = [pltpu.make_async_copy(own(h), slot(z, x, h), local.at[h]) for h in range(2)]
        for copy in copies:
            copy.start()
        net.recv(base_z, slot(zm, x, 0))
        net.send(base_z + 4, slot(zm, x, 0), slot(zm, x, 0), net.on_z(1))
        net.recv(base_z + 2, slot(zp, x, 1))
        net.send(base_z + 5, slot(zp, x, 1), slot(zp, x, 1), net.on_z(3))
        forward(0)
        net.recv(base_z + 1, slot(zm, x, 1))
        for h in range(2):
            along(1, h)
        rest(0)
        for copy in copies + loads[4:]:
            copy.wait()
        multiply(0)
        reduce_start(0)
        forward(1)
        net.recv(base_z + 3, slot(zp, x, 0))
        for h in range(2):
            along(2, h)
        reduce_middle(0)
        rest(1)
        reduce_end(0)
        multiply(1)
        reduce_start(1)
        spread_0 = spread(0)
        next(spread_0)
        forward(2)
        net.recv(base_z + 4, slot(z2, x, 0))
        net.recv(base_z + 5, slot(z2, x, 1))
        for h in range(2):
            along(3, h)
        reduce_middle(1)
        next(spread_0)
        rest(2)
        reduce_end(1)
        multiply(2)
        reduce_start(2)
        spread_1 = spread(1)
        next(spread_1)
        next(spread_0)
        forward(3)
        reduce_middle(2)
        next(spread_1)
        rest(3)
        multiply(3)
        reduce_start(3)
        reduce_end(2)
        spread_2 = spread(2)
        next(spread_2)
        next(spread_1)
        reduce_middle(3)
        next(spread_2)
        reduce_end(3)
        spread_3 = spread(3)
        next(spread_3)
        next(spread_2)
        next(spread_3)
        drive(spread_0, spread_1, spread_2, spread_3)
        for copy in last:
            copy.wait()
        net.recv(1, j_ref)
        net.finish()

    return call(
        kernel,
        collective_id,
        [like((4, 2, 2, 2, 4, tokens, columns), BF16), like(inputs.shape, BF16)],
        [VMEM] * 2 + [ANY] * 9,
        [ANY, ANY],
        [
            pltpu.VMEM((4, 4, features // 16, depth), BF16),
            pltpu.VMEM((4, columns, depth), BF16),
            pltpu.VMEM((2, 4 * tokens, depth), F32),
            pltpu.VMEM((4 * tokens, depth), F32),
            pltpu.VMEM((4, tokens, depth), BF16),
            pltpu.VMEM((2, tokens, depth), BF16),
            pltpu.VMEM((4, 2, 4, 2, tokens, depth), BF16),
            pltpu.VMEM((4, 4, 2, rows, columns), F32),
            pltpu.VMEM((4, 2, rows, columns), F32),
            pltpu.VMEM((4, 2, rows, columns), F32),
            pltpu.VMEM((4, 2, 2, rows, columns), F32),
            pltpu.VMEM((4, 3, 2, tokens, columns), BF16),
            pltpu.SemaphoreType.DMA((22,)),
            *sems(64 + 4 * gather_slots(2)),
        ],
        (back, gate, *downs, basis, *thirds, inputs),
        name,
        cost,
    )


def squares(rotated, own_inputs, other_inputs):
    rows, width = rotated.shape[3], own_inputs.shape[1]
    depth = own_inputs.shape[2]

    def kernel(r_ref, a_ref, b_ref, o_ref, both, total):
        example, sample = pl.program_id(0), pl.program_id(1)

        @pl.when((example == 0) & (sample == 0))
        def _():
            total[...] = jnp.zeros_like(total)

        @pl.when(sample == 0)
        def _():
            both[:, :depth] = a_ref[0]
            both[:, depth:] = b_ref[0]

        block = jnp.dot(both[...], r_ref[0, 0], preferred_element_type=F32)
        total[...] += block * block * (1.0 / 16.0)

        @pl.when((example == 3) & (sample == 3))
        def _():
            o_ref[...] = total[...].T

    return pl.pallas_call(
        kernel,
        grid=(4, 4),
        out_shape=like((rows, width), F32),
        in_specs=[
            pl.BlockSpec((1, 1, 2 * depth, rows), lambda e, s: (e, s, 0, 0)),
            pl.BlockSpec((1, width, depth), lambda e, s: (e, 0, 0)),
            pl.BlockSpec((1, width, depth), lambda e, s: (e, 0, 0)),
        ],
        out_specs=pl.BlockSpec((rows, width), lambda e, s: (0, 0)),
        scratch_shapes=[pltpu.VMEM((width, 2 * depth), BF16), pltpu.VMEM((width, rows), F32)],
        name="squares",
    )(rotated, own_inputs, other_inputs)


def contract_last(left, right):
    return lax.dot_general(left, right, (((1,), (1,)), ((), ())), preferred_element_type=F32)


def per_device(
    resid, final_gain, unembed, labels, layer_in, gate_value, down_weight, basis_in, basis_out
):
    wide, narrow = lax.axis_index("wide"), lax.axis_index("narrow")
    core = lax.rem(wide, 2)
    tokens, width = resid.shape
    samples = labels.shape[1]
    vocab, part = unembed.shape
    hidden = down_weight.shape[0]
    columns = basis_out.shape[1]
    width_in = basis_in.shape[1]
    pair = 2 * part
    core_tokens = 16 * tokens
    few = tokens // 8

    resid_float = resid.astype(F32)
    inverse = lax.rsqrt(jnp.mean(resid_float * resid_float, axis=1) + EPSILON)
    normed = (resid_float * inverse[:, None] * final_gain).astype(BF16)

    def blocks(rows):
        return rows.reshape(tokens, 16, pair).transpose(1, 0, 2)

    down, basis = down_weight.T, basis_out.T
    normed_cols, inputs_cols, unembed_rows, basis_in_rows, basis_both, down_0 = exchange(
        [blocks(normed), blocks(layer_in)],
        [unembed.T, basis_in, basis],
        [("x", down, 0)],
        0,
        "exchange",
        30,
    )
    unembed_rows = unembed_rows.reshape(pair, vocab)
    basis_in_rows = basis_in_rows.reshape(pair, width_in)
    logits_part = jnp.dot(
        normed_cols.reshape(core_tokens, pair), unembed_rows, preferred_element_type=F32
    )
    inputs_part = jnp.dot(
        inputs_cols.reshape(core_tokens, pair), basis_in_rows, preferred_element_type=F32
    )
    mine = lax.dynamic_index_in_dim(
        labels.reshape(16, 2, 8, few, samples), core, 1, keepdims=False
    )
    shifted = mine.transpose(1, 0, 2, 3).reshape(core_tokens * samples) - narrow * vocab
    chosen = (shifted[:, None] == lax.broadcasted_iota(jnp.int32, (1, vocab), 1)).astype(BF16)
    picked = contract_last(chosen, unembed_rows).astype(BF16)
    logits, inputs_rot, picked, down_z = reduce_over(
        [logits_part.reshape(4, 4, tokens, vocab), inputs_part.reshape(4, 4, tokens, width_in)],
        [picked.reshape(2, 4, 16 * few * samples, pair)],
        [("z", down, 0)],
        [F32, BF16, BF16],
        1,
        "reduce_logits",
        60,
    )
    probs, down_1 = softmax_narrow(logits, [("x", down_z, 1)], 2, "softmax", 20)
    probs_all, inputs_all, third_0, third_1 = gather_wide(
        [probs.reshape(2, tokens // 2, vocab), inputs_rot.reshape(2, tokens // 2, width_in)],
        [("basis", basis, 0), ("basis", basis, 1)],
        3,
        "gather_probs",
        30,
    )
    inputs_all = inputs_all.reshape(4, 4 * tokens, width_in).transpose(0, 2, 1)
    common = contract_last(probs_all.reshape(core_tokens, vocab), unembed_rows)
    common = common.reshape(16, 8, few, pair).transpose(1, 0, 2, 3).reshape(2, 4, 16 * few, pair)
    common, down_2, third_2 = reduce_over(
        [], [common], [("x", down_z, 2), ("basis", basis, 2)], [F32], 4, "reduce_common", 20
    )
    grads = common.reshape(16, few, 1, pair) - picked.astype(F32).reshape(16, few, samples, pair)
    (grads,) = exchange([grads.reshape(16, few * samples, pair)], [], [], 5, "exchange_grads", 12)
    grads = grads.transpose(1, 0, 2).reshape(few, samples, width)
    resid_few = lax.dynamic_slice_in_dim(resid_float, narrow * few, few, 0)
    inverse_few = lax.dynamic_slice_in_dim(inverse, narrow * few, few, 0)
    inner = jnp.sum(final_gain * grads * resid_few[:, None, :], axis=2)
    back = (
        inverse_few[:, None, None] * final_gain * grads
        - resid_few[:, None, :] * (inverse_few**3)[:, None, None] * inner[:, :, None] / width
    )
    back = back.astype(BF16).reshape(few * samples, 4, 4, 2, part).transpose(3, 0, 1, 2, 4)
    back = lax.dynamic_slice_in_dim(
        jnp.concatenate([back, back], axis=2), lax.div(wide, 8), 4, axis=2
    )
    back, down_3 = gather_back(
        back.reshape(2, few * samples, width // 2), [("x", down_z, 3)], 6, "gather_back", 20
    )
    back = back.reshape(8, 2, few, samples, width // 2).transpose(1, 3, 0, 2, 4)
    rotated, inputs_other = rotate_all(
        back.reshape(2, samples * tokens, width // 2),
        gate_value,
        [down_0, down_1, down_2, down_3],
        basis_both,
        [third_0, third_1, third_2],
        inputs_all,
        7,
        "rotate_all",
        110,
    )
    return squares(
        rotated.reshape(4, samples, 8 * tokens, columns), inputs_all, inputs_other
    )


def solution(mesh):
    in_specs = (
        P("wide", None),
        P(),
        P("narrow", "wide"),
        P(),
        P("wide", None),
        P("wide", "narrow"),
        P("narrow", "wide"),
        P("wide", "narrow"),
        P("narrow", "wide"),
    )
    out_specs = P("wide", "narrow")
    return jax.shard_map(
        per_device, mesh=mesh, in_specs=in_specs, out_specs=out_specs, check_vma=False
    )
```

```python
import functools

import jax
import jax.numpy as jnp
from jax import lax
from jax.experimental import pallas as pl
from jax.experimental.pallas import tpu as pltpu
from jax.sharding import PartitionSpec as P

EPSILON = 1e-05
MESH = pl.DeviceIdType.MESH
F32 = jnp.float32
BF16 = jnp.bfloat16
ANY = pl.BlockSpec(memory_space=pl.ANY)
VMEM = pl.BlockSpec(memory_space=pltpu.VMEM)


class Net:
    def __init__(self, send_sem, recv_sem):
        self.send_sem, self.recv_sem = send_sem, recv_sem
        self.started = []
        wide, narrow = lax.axis_index("wide"), lax.axis_index("narrow")
        self.wide, self.narrow = wide, narrow
        self.core = lax.rem(wide, 2)
        self.x = lax.rem(lax.div(wide, 2), 4)
        self.z = lax.div(wide, 8)
        self.y = lax.rem(narrow, 4)
        self.zl = lax.div(narrow, 4)

    def on_x(self, step):
        return {"wide": self.z * 8 + lax.rem(self.x + step, 4) * 2 + self.core}

    def on_z(self, step):
        return {"wide": lax.rem(self.z + step, 4) * 8 + self.x * 2 + self.core}

    def on_y(self, step):
        return {"narrow": self.zl * 4 + lax.rem(self.y + step, 4)}

    def on_zl(self, step):
        return {"narrow": (1 - self.zl) * 4 + self.y}

    def on_core(self):
        return {"wide": self.wide + 1 - 2 * self.core}

    def greet(self, devices):
        barrier = pltpu.get_barrier_semaphore()
        for device in devices:
            pl.semaphore_signal(barrier, inc=1, device_id=device, device_id_type=MESH)
        pl.semaphore_wait(barrier, len(devices))

    def copy(self, slot, src, dst, device):
        return pltpu.make_async_remote_copy(
            src_ref=src,
            dst_ref=dst,
            send_sem=self.send_sem.at[slot],
            recv_sem=self.recv_sem.at[slot],
            device_id=device,
            device_id_type=MESH,
        )

    def send(self, slot, src, dst, device):
        copy = self.copy(slot, src, dst, device)
        copy.start()
        self.started.append(copy)

    def recv(self, slot, dst):
        self.copy(slot, dst, dst, self.on_core()).wait_recv()

    def finish(self):
        for copy in self.started:
            copy.wait_send()


def turn(place, step, size):
    return lax.rem(place + step, size)


def gather_stage(net, base, own, slot, outer_size, me_o, me_i, on_o, on_i):
    ip, im, i2 = (turn(me_i, s, 4) for s in (1, 3, 2))
    inner = lambda row: base + 6 + 6 * row

    def along(row, o, first):
        b = inner(row)
        src = own if first else (lambda h: slot(o, me_i, h))
        net.send(b, src(0), slot(o, me_i, 0), on_i(1))
        net.send(b + 2, src(1), slot(o, me_i, 1), on_i(3))
        net.send(b + 1, src(1), slot(o, me_i, 1), on_i(1))
        net.send(b + 3, src(0), slot(o, me_i, 0), on_i(3))

    def forward(row, o):
        b = inner(row)
        net.recv(b, slot(o, im, 0))
        net.send(b + 4, slot(o, im, 0), slot(o, im, 0), on_i(1))
        net.recv(b + 2, slot(o, ip, 1))
        net.send(b + 5, slot(o, ip, 1), slot(o, ip, 1), on_i(3))

    def rest(row, o):
        b = inner(row)
        net.recv(b + 1, slot(o, im, 1))
        net.recv(b + 3, slot(o, ip, 0))
        net.recv(b + 4, slot(o, i2, 0))
        net.recv(b + 5, slot(o, i2, 1))

    if outer_size == 4:
        op, om, o2 = (turn(me_o, s, 4) for s in (1, 3, 2))
        net.send(base, own(0), slot(me_o, me_i, 0), on_o(1))
        net.send(base + 2, own(1), slot(me_o, me_i, 1), on_o(3))
        net.send(base + 1, own(1), slot(me_o, me_i, 1), on_o(1))
        net.send(base + 3, own(0), slot(me_o, me_i, 0), on_o(3))
        along(0, me_o, True)
        yield
        net.recv(base, slot(om, me_i, 0))
        net.send(base + 4, slot(om, me_i, 0), slot(om, me_i, 0), on_o(1))
        net.recv(base + 2, slot(op, me_i, 1))
        net.send(base + 5, slot(op, me_i, 1), slot(op, me_i, 1), on_o(3))
        forward(0, me_o)
        net.recv(base + 1, slot(om, me_i, 1))
        along(1, om, False)
        yield
        net.recv(base + 3, slot(op, me_i, 0))
        along(2, op, False)
        forward(1, om)
        yield
        net.recv(base + 4, slot(o2, me_i, 0))
        net.recv(base + 5, slot(o2, me_i, 1))
        along(3, o2, False)
        forward(2, op)
        yield
        forward(3, o2)
        for row, o in enumerate((me_o, om, op, o2)):
            rest(row, o)
    else:
        oq = 1 - me_o
        for h in range(2):
            net.send(base + h, own(h), slot(me_o, me_i, h), on_o(1))
        along(0, me_o, True)
        yield
        forward(0, me_o)
        for h in range(2):
            net.recv(base + h, slot(oq, me_i, h))
        along(1, oq, False)
        yield
        forward(1, oq)
        yield
        rest(0, me_o)
        rest(1, oq)


def gather_slots(outer_size):
    return 6 + 6 * outer_size


class Sum:
    def __init__(self, part, fwd, mid, got, tot, zfwd, zgot):
        self.part, self.fwd, self.mid, self.got = part, fwd, mid, got
        self.tot, self.zfwd, self.zgot = tot, zfwd, zgot
        self.half = part.shape[2] // 2

    @staticmethod
    def scratch(outer, rows, columns, dtype):
        half = rows // 2
        return [
            pltpu.VMEM((outer, 2, half, columns), dtype),
            pltpu.VMEM((outer, 2, half, columns), dtype),
            pltpu.VMEM((outer, 2, rows, columns), dtype),
            pltpu.VMEM((outer, rows, columns), dtype),
            pltpu.VMEM((2, half, columns), dtype),
            pltpu.VMEM((2, rows, columns), dtype),
        ]

    def h(self, k):
        return pl.ds(k * self.half, self.half)


def reduce_slots(outer_size):
    return 6 * outer_size + 6


def reduce_stage(net, base, sums, outer_size, me_o, me_i, on_o, on_i, prepare=None):
    ip, im, i2 = (turn(me_i, s, 4) for s in (1, 3, 2))
    offsets = (2, 1, 3, 0) if outer_size == 4 else (1, 0)
    rows = [turn(me_o, off, outer_size) for off in offsets]
    count = reduce_slots(outer_size)

    def at(a, k, j):
        return base + a * count + 6 * k + j

    def start_far(k):
        for a, s in enumerate(sums):
            net.send(at(a, k, 0), s.part.at[rows[k], i2, s.h(0)], s.fwd.at[k, 0], on_i(1))
            net.send(at(a, k, 1), s.part.at[rows[k], i2, s.h(1)], s.fwd.at[k, 1], on_i(3))

    def start_near(k):
        for a, s in enumerate(sums):
            net.send(at(a, k, 2), s.part.at[rows[k], ip, s.h(1)], s.got.at[k, 0, s.h(1)], on_i(1))
            net.send(at(a, k, 3), s.part.at[rows[k], im, s.h(0)], s.got.at[k, 1, s.h(0)], on_i(3))

    def middle(k):
        for a, s in enumerate(sums):
            net.recv(at(a, k, 0), s.fwd.at[k, 0])
            s.mid[k, 0] = s.part[rows[k], ip, s.h(0)] + s.fwd[k, 0]
            net.send(at(a, k, 4), s.mid.at[k, 0], s.got.at[k, 0, s.h(0)], on_i(1))
            net.recv(at(a, k, 1), s.fwd.at[k, 1])
            s.mid[k, 1] = s.part[rows[k], im, s.h(1)] + s.fwd[k, 1]
            net.send(at(a, k, 5), s.mid.at[k, 1], s.got.at[k, 1, s.h(1)], on_i(3))

    def total(k):
        for a, s in enumerate(sums):
            z = base + a * count + 6 * outer_size
            net.recv(at(a, k, 2), s.got.at[k, 0, s.h(1)])
            net.recv(at(a, k, 3), s.got.at[k, 1, s.h(0)])
            net.recv(at(a, k, 4), s.got.at[k, 0, s.h(0)])
            net.recv(at(a, k, 5), s.got.at[k, 1, s.h(1)])
            for h in range(2):
                s.tot[k, s.h(h)] = (
                    s.part[rows[k], me_i, s.h(h)] + s.got[k, 0, s.h(h)] + s.got[k, 1, s.h(h)]
                )
            if outer_size == 2:
                if k == 0:
                    for h in range(2):
                        net.send(z + h, s.tot.at[0, s.h(h)], s.zgot.at[0, s.h(h)], on_o(1))
            elif k == 0:
                net.send(z, s.tot.at[0, s.h(0)], s.zfwd.at[0], on_o(1))
                net.send(z + 1, s.tot.at[0, s.h(1)], s.zfwd.at[1], on_o(3))
            elif k == 1:
                net.send(z + 2, s.tot.at[1, s.h(1)], s.zgot.at[0, s.h(1)], on_o(1))
                net.recv(z, s.zfwd.at[0])
                s.tot[1, s.h(0)] += s.zfwd[0]
                net.send(z + 3, s.tot.at[1, s.h(0)], s.zgot.at[0, s.h(0)], on_o(1))
            elif k == 2:
                net.send(z + 4, s.tot.at[2, s.h(0)], s.zgot.at[1, s.h(0)], on_o(3))
                net.recv(z + 1, s.zfwd.at[1])
                s.tot[2, s.h(1)] += s.zfwd[1]
                net.send(z + 5, s.tot.at[2, s.h(1)], s.zgot.at[1, s.h(1)], on_o(3))

    def ready(k):
        if prepare is not None:
            prepare(rows[k])

    def steps():
        ready(0)
        start_far(0)
        start_near(0)
        ready(1)
        start_far(1)
        yield
        for k in range(outer_size):
            middle(k)
            if k + 1 < outer_size:
                start_near(k + 1)
            if k >= 1:
                total(k - 1)
            if k + 2 < outer_size:
                ready(k + 2)
                start_far(k + 2)
            yield
        total(outer_size - 1)

    def final(a):
        s = sums[a]
        z = base + a * count + 6 * outer_size
        last = outer_size - 1

        def value(h):
            if outer_size == 2:
                net.recv(z + h, s.zgot.at[0, s.h(h)])
                return s.tot[last, s.h(h)] + s.zgot[0, s.h(h)]
            first, second = ((z + 3, z + 4), (z + 2, z + 5))[h]
            net.recv(first, s.zgot.at[0, s.h(h)])
            net.recv(second, s.zgot.at[1, s.h(h)])
            return s.tot[last, s.h(h)] + s.zgot[0, s.h(h)] + s.zgot[1, s.h(h)]

        return value

    return steps(), [final(a) for a in range(len(sums))]


def drive(*stages):
    stages = list(stages)
    while stages:
        stages = [stage for stage in stages if next(stage, 0) is None]


def ring(net, base, own, slot, me, on):
    plus, minus, far = (turn(me, s, 4) for s in (1, 3, 2))
    net.send(base, own(0), slot(me, 0), on(1))
    net.send(base + 2, own(1), slot(me, 1), on(3))
    yield
    net.send(base + 1, own(1), slot(me, 1), on(1))
    net.send(base + 3, own(0), slot(me, 0), on(3))
    yield
    net.recv(base, slot(minus, 0))
    net.send(base + 4, slot(minus, 0), slot(minus, 0), on(1))
    net.recv(base + 2, slot(plus, 1))
    net.send(base + 5, slot(plus, 1), slot(plus, 1), on(3))
    yield
    net.recv(base + 1, slot(minus, 1))
    net.recv(base + 3, slot(plus, 0))
    net.recv(base + 4, slot(far, 0))
    net.recv(base + 5, slot(far, 1))


class Side:
    def __init__(self, tasks):
        self.tasks = tasks
        self.arrays = [array for _, array, _ in tasks]
        self.outs = []
        for kind, array, _ in tasks:
            rows, depth = array.shape[-2:]
            shape = (2, rows // 3, depth) if kind == "basis" else (4, rows, depth)
            shape = (4, 4, *array.shape) if kind == "all" else shape
            self.outs.append(like(shape, array.dtype))
        self.slots = 30 * len(tasks)

    def local(self):
        return [pltpu.SemaphoreType.DMA((max(len(self.tasks), 1),))]

    def peers(self, net):
        found = []
        for kind, _, _ in self.tasks:
            if kind == "x":
                found += [net.on_x(1), net.on_x(3)]
            elif kind == "z":
                found += [net.on_z(1), net.on_z(3)]
            elif kind == "all":
                found += [net.on_x(1), net.on_x(3), net.on_z(1), net.on_z(3)]
            else:
                found += [net.on_zl(1), net.on_core()]
        return found

    def stages(self, net, base, ins, outs, local):
        return [
            self.stage(net, base + 30 * t, kind, ins[t], outs[t], step, local.at[t])
            for t, (kind, _, step) in enumerate(self.tasks)
        ]

    def stage(self, net, base, kind, src, out, step, local):
        if kind == "basis":
            rows = out.shape[1]
            net.send(base, src.at[pl.ds(rows * step, rows)], out.at[0], net.on_zl(1))
            yield
            yield
            net.recv(base, out.at[0])
            net.send(base + 1, out.at[0], out.at[1], net.on_core())
            yield
            net.recv(base + 1, out.at[1])
            return
        if kind == "all":
            copy = pltpu.make_async_copy(src, out.at[net.z, net.x], local)
            copy.start()
            slot = lambda o, i, h: out.at[o, i, h]
            own = lambda h: src.at[h]
            yield from gather_stage(net, base, own, slot, 4, net.z, net.x, net.on_z, net.on_x)
            copy.wait()
            return
        half = out.shape[1] // 2
        cut = lambda h: pl.ds(h * half, half)
        row = src if len(src.shape) == 2 else src.at[turn(net.z, step, 4)]
        own = lambda h: row.at[cut(h)]
        slot = lambda i, h: out.at[i, cut(h)]
        if kind == "z":
            yield from ring(net, base, own, slot, net.z, net.on_z)
        else:
            yield from ring(net, base, own, slot, net.x, net.on_x)


def sems(slots):
    return [pltpu.SemaphoreType.DMA((slots,)), pltpu.SemaphoreType.DMA((slots,))]


def call(kernel, collective_id, outs, in_specs, out_specs, scratch, args, name, cost):
    return pl.pallas_call(
        kernel,
        out_shape=outs,
        in_specs=in_specs,
        out_specs=out_specs,
        scratch_shapes=scratch,
        compiler_params=pltpu.CompilerParams(
            collective_id=collective_id, has_side_effects=True, vmem_limit_bytes=60 << 20
        ),
        cost_estimate=pl.CostEstimate(flops=cost * 10**9, bytes_accessed=0, transcendentals=0),
        name=name,
    )(*args)


def like(shape, dtype):
    return jax.ShapeDtypeStruct(shape, dtype)


def exchange(arrays, pairs, tasks, collective_id, name, cost):
    na, np_, nt = len(arrays), len(pairs), len(tasks)
    side = Side(tasks)

    def kernel(*refs):
        ins, shared, side_in = refs[:na], refs[na : na + np_], refs[na + np_ : na + np_ + nt]
        refs = refs[na + np_ + nt :]
        outs, both, side_out = refs[:na], refs[na : na + np_], refs[na + np_ : na + np_ + nt]
        local, side_local, send_sem, recv_sem = refs[na + np_ + nt :]
        net = Net(send_sem, recv_sem)
        steps = [(dz, dx) for dz in range(4) for dx in range(4) if (dz, dx) != (0, 0)]
        steps.sort(key=lambda s: -(min(s[0], 4 - s[0]) * 2 + min(s[1], 4 - s[1])))

        def to(dz, dx):
            return turn(net.z, dz, 4) * 4 + turn(net.x, dx, 4)

        me = net.z * 4 + net.x
        peers = [{"wide": to(*s) * 2 + net.core} for s in steps]
        net.greet(peers + ([net.on_core()] if np_ else []) + side.peers(net))
        copies = []
        for j, s in enumerate(steps):
            for a in range(na):
                net.send(j * na + a, ins[a].at[to(*s)], outs[a].at[me], peers[j])
        for a in range(na):
            copies.append(pltpu.make_async_copy(ins[a].at[me], outs[a].at[me], local.at[a]))
        for b in range(np_):
            net.send(15 * na + b, shared[b], both[b], net.on_core())
        for copy in copies:
            copy.start()
        extra = side.stages(net, 15 * na + max(np_, 1), side_in, side_out, side_local)
        for _ in range(3):
            for stage in extra:
                next(stage)
        for j, (dz, dx) in enumerate(steps):
            source = to((4 - dz) % 4, (4 - dx) % 4)
            for a in range(na):
                net.recv(j * na + a, outs[a].at[source])
        for b in range(np_):
            net.recv(15 * na + b, both[b])
        drive(*extra)
        for copy in copies:
            copy.wait()
        net.finish()

    outs = [like(a.shape, a.dtype) for a in (*arrays, *pairs)]
    return call(
        kernel,
        collective_id,
        outs + side.outs,
        [ANY] * (na + np_ + nt),
        [ANY] * (na + np_ + nt),
        [
            pltpu.SemaphoreType.DMA((na,)),
            *side.local(),
            *sems(15 * na + max(np_, 1) + side.slots),
        ],
        (*arrays, *pairs, *side.arrays),
        name,
        cost,
    )


def reduce_over(wide_parts, narrow_parts, tasks, dtypes, collective_id, name, cost):
    parts = [*wide_parts, *narrow_parts]
    n, split, nt = len(parts), len(wide_parts), len(tasks)
    side = Side(tasks)
    slots = split * reduce_slots(4) + (n - split) * reduce_slots(2)

    def kernel(*refs):
        ins, side_in = refs[:n], refs[n : n + nt]
        outs, side_out = refs[n + nt : 2 * n + nt], refs[2 * n + nt : 2 * (n + nt)]
        buffers, (side_local, send_sem, recv_sem) = refs[2 * (n + nt) : -3], refs[-3:]
        net = Net(send_sem, recv_sem)
        sums = [Sum(ins[a], *buffers[6 * a : 6 * a + 6]) for a in range(n)]
        stages, ends, peers = [], [], []
        if split:
            peers += [net.on_x(1), net.on_x(3), net.on_z(1), net.on_z(3)]
            stage, end = reduce_stage(net, 0, sums[:split], 4, net.z, net.x, net.on_z, net.on_x)
            stages.append(stage)
            ends += end
        if n > split:
            peers += [net.on_y(1), net.on_y(3), net.on_zl(1)]
            base = split * reduce_slots(4)
            stage, end = reduce_stage(
                net, base, sums[split:], 2, net.zl, net.y, net.on_zl, net.on_y
            )
            stages.append(stage)
            ends += end
        net.greet(peers + side.peers(net))
        extra = side.stages(net, slots, side_in, side_out, side_local)
        drive(*stages, *extra)
        for a in range(n):
            for h in range(2):
                outs[a][sums[a].h(h), :] = ends[a](h).astype(outs[a].dtype)
        net.finish()

    scratch = []
    for p in parts:
        scratch += Sum.scratch(p.shape[0], p.shape[2], p.shape[3], p.dtype)
    return call(
        kernel,
        collective_id,
        [like(p.shape[2:], d) for p, d in zip(parts, dtypes)] + side.outs,
        [VMEM] * n + [ANY] * nt,
        [VMEM] * n + [ANY] * nt,
        [*scratch, *side.local(), *sems(slots + side.slots)],
        (*parts, *side.arrays),
        name,
        cost,
    )


def front(normed, inputs, unembeds, bases_in, ids, down, basis, collective_id, name, cost):
    tokens, features = normed.shape[2:]
    half = features // 2
    vocab, width = unembeds[0].shape[1], bases_in[0].shape[1]
    count = ids.shape[0] // 8
    tasks = [("z", down, 0), ("x", down, 1)] + [("basis", basis, j) for j in range(3)]
    side = Side(tasks)
    base_i = reduce_slots(4)
    base_p = base_i + reduce_slots(4)
    base_s = base_p + reduce_slots(2)
    base_g = base_s + 7
    base_t = base_g + gather_slots(4)

    def kernel(*refs):
        n_ref, i_ref, id_ref, u0, u1, b0, b1, d_ref, basis_ref = refs[:9]
        common_ref, rot_ref, picked_ref, dz_ref, dx_ref, t0, t1, t2 = refs[9:17]
        unembed, basis_in, logit_part, input_part, pick_part = refs[17:22]
        sum_l, sum_i, sum_p = (refs[22 + 6 * j : 28 + 6 * j] for j in range(3))
        logits, mine, got, probs, every, local, send_sem, recv_sem = refs[40:]
        net = Net(send_sem, recv_sem)
        c = net.core
        loads = [
            pltpu.make_async_copy(u0, unembed.at[pl.ds(c * half, half)], local.at[0]),
            pltpu.make_async_copy(u1, unembed.at[pl.ds((1 - c) * half, half)], local.at[1]),
            pltpu.make_async_copy(b0, basis_in.at[pl.ds(c * half, half)], local.at[2]),
            pltpu.make_async_copy(b1, basis_in.at[pl.ds((1 - c) * half, half)], local.at[3]),
        ]
        for load in loads:
            load.start()
        ring_peers = [net.on_x(1), net.on_x(3), net.on_z(1), net.on_z(3), net.on_core()]
        narrow_peers = [{"narrow": turn(net.narrow, k, 8)} for k in range(1, 8)]
        net.greet(ring_peers + narrow_peers)
        for load in loads:
            load.wait()

        def dot_row(left, right, part):
            def run(row):
                rows = left[row].reshape(4 * tokens, features)
                value = jnp.dot(rows, right[...], preferred_element_type=F32)
                part[row] = value.reshape(4, tokens, part.shape[3])

            return run

        main, (end,) = reduce_stage(
            net, 0, [Sum(logit_part, *sum_l)], 4, net.z, net.x, net.on_z, net.on_x,
            dot_row(n_ref, unembed, logit_part),
        )
        late, (end_i,) = reduce_stage(
            net, base_i, [Sum(input_part, *sum_i)], 4, net.z, net.x, net.on_z, net.on_x,
            dot_row(i_ref, basis_in, input_part),
        )
        picks, (end_p,) = reduce_stage(
            net, base_p, [Sum(pick_part, *sum_p)], 2, net.zl, net.y, net.on_zl, net.on_y
        )

        def extra(t, out, kind, src, step):
            return side.stage(net, base_t + 30 * t, kind, src, out, step, None)

        ring_z = extra(0, dz_ref, "z", d_ref, 0)
        ring_x = extra(1, dx_ref, "x", dz_ref, 1)
        thirds = [extra(2 + j, out, "basis", basis_ref, j) for j, out in enumerate((t0, t1, t2))]

        next(main)
        next(ring_z)
        next(main)

        def pick(j, carry):
            some = id_ref[pl.ds(pl.multiple_of(j * count, count), count)]
            one = some == lax.broadcasted_iota(jnp.int32, (count, vocab), 1)
            value = contract_last(jnp.where(one, 1.0, 0.0).astype(BF16), unembed[...])
            pick_part[lax.div(j, 4), lax.rem(j, 4)] = value.astype(BF16)
            return carry

        lax.fori_loop(0, 4, pick, 0)
        next(ring_z)
        next(main)
        lax.fori_loop(4, 8, pick, 0)
        next(picks)
        next(main)
        next(ring_z)
        next(picks)
        next(main)
        next(late)
        drive(ring_z)
        next(ring_x)
        next(ring_x)
        drive(main)
        for h in range(2):
            logits[pl.ds(h * (tokens // 2), tokens // 2), :] = end(h)
        top = jnp.max(logits[...], axis=1, keepdims=True)
        mine[0] = jnp.broadcast_to(top, (tokens, 128))
        mine[1] = jnp.broadcast_to(
            jnp.sum(jnp.exp(logits[...] - top), axis=1, keepdims=True), (tokens, 128)
        )
        for k in range(7):
            net.send(base_s + k, mine, got.at[k], narrow_peers[k])
        next(late)
        next(thirds[0])
        for k in range(7):
            net.recv(base_s + k, got.at[k])
        largest = mine[0]
        for k in range(7):
            largest = jnp.maximum(largest, got[k, 0])
        total = mine[1] * jnp.exp(mine[0] - largest)
        for k in range(7):
            total += got[k, 1] * jnp.exp(got[k, 0] - largest)
        value = (jnp.exp(logits[...] - largest[:, :1]) / total[:, :1]).astype(BF16)
        probs[...] = value.reshape(2, tokens // 2, vocab)
        every[net.z, net.x] = value.reshape(2, tokens // 2, vocab)
        slot = lambda o, i, h: every.at[o, i, h]
        own = lambda h: probs.at[h]
        spread = gather_stage(
            net, base_g, own, slot, 4, net.z, net.x, net.on_z, net.on_x
        )
        next(spread)
        next(late)
        next(ring_x)
        next(spread)
        next(thirds[1])
        next(late)
        next(thirds[0])
        next(spread)
        next(thirds[2])
        next(picks)
        next(spread)
        next(late)
        drive(late)
        drive(spread)
        for h in range(2):
            rot_ref[h] = end_i(h).astype(BF16)
        drive(picks)
        for h in range(2):
            picked_ref[pl.ds(h * (count // 2), count // 2), :] = end_p(h).astype(BF16)
        for row in range(4):
            common_ref[row] = contract_last(
                every[row].reshape(4 * tokens, vocab), unembed[...]
            )
        drive(ring_x, *thirds)
        net.finish()

    return call(
        kernel,
        collective_id,
        [
            like((4, 4 * tokens, features), F32),
            like((2, tokens // 2, width), BF16),
            like((count, features), BF16),
            *side.outs,
        ],
        [VMEM] * 3 + [ANY] * 6,
        [VMEM] * 3 + [ANY] * 5,
        [
            pltpu.VMEM((features, vocab), BF16),
            pltpu.VMEM((features, width), BF16),
            pltpu.VMEM((4, 4, tokens, vocab), F32),
            pltpu.VMEM((4, 4, tokens, width), F32),
            pltpu.VMEM((2, 4, count, features), BF16),
            *Sum.scratch(4, tokens, vocab, F32),
            *Sum.scratch(4, tokens, width, F32),
            *Sum.scratch(2, count, features, BF16),
            pltpu.VMEM((tokens, vocab), F32),
            pltpu.VMEM((2, tokens, 128), F32),
            pltpu.VMEM((7, 2, tokens, 128), F32),
            pltpu.VMEM((2, tokens // 2, vocab), BF16),
            pltpu.VMEM((4, 4, 2, tokens // 2, vocab), BF16),
            pltpu.SemaphoreType.DMA((4,)),
            *sems(base_t + side.slots),
        ],
        (normed, inputs, ids, *unembeds, *bases_in, down, basis),
        name,
        cost,
    )


def gather_back(shard, tasks, collective_id, name, cost):
    _, rows, features = shard.shape
    side, nt = Side(tasks), len(tasks)

    def kernel(*refs):
        x_ref, side_in, o_ref, side_out = refs[0], refs[1 : 1 + nt], refs[1 + nt], refs[2 + nt : -5]
        mine, local, side_local, send_sem, recv_sem = refs[-5:]
        net = Net(send_sem, recv_sem)
        net.greet([net.on_y(1), net.on_y(3), net.on_zl(1), net.on_core()] + side.peers(net))
        net.send(0, x_ref.at[1 - net.core], mine, net.on_core())
        slot = lambda o, i, h: o_ref.at[o, i, lax.rem(net.core + h, 2)]
        own = lambda h: mine if h else x_ref.at[net.core]
        net.recv(0, mine)
        copies = [
            pltpu.make_async_copy(own(h), slot(net.zl, net.y, h), local.at[h]) for h in range(2)
        ]
        for copy in copies:
            copy.start()
        drive(
            gather_stage(net, 1, own, slot, 2, net.zl, net.y, net.on_zl, net.on_y),
            *side.stages(net, 1 + gather_slots(2), side_in, side_out, side_local),
        )
        for copy in copies:
            copy.wait()
        net.finish()

    return call(
        kernel,
        collective_id,
        [like((2, 4, 2, rows, features), shard.dtype)] + side.outs,
        [ANY] * (1 + nt),
        [ANY] * (1 + nt),
        [
            pltpu.VMEM((rows, features), shard.dtype),
            pltpu.SemaphoreType.DMA((2,)),
            *side.local(),
            *sems(1 + gather_slots(2) + side.slots),
        ],
        (shard, *side.arrays),
        name,
        cost,
    )


def rotate_all(back, gate, down, down_z, downs, bases, thirds, inputs, collective_id, name, cost):
    tokens, depth = gate.shape
    columns = bases[0].shape[0]
    width = inputs.shape[1]
    rows = 2 * tokens
    features = back.shape[2]
    cuts = (pl.ds(0, 896), pl.ds(896, depth - 896))

    def kernel(*refs):
        back_ref, g_ref, i_ref, own_ref, z_ref, d_refs = *refs[:5], refs[5:9]
        b_refs, t_refs, o_ref = refs[9:11], refs[11:14], refs[14]
        down, bases, h_ref, j_ref, spun, pairs, corrected = refs[15:22]
        half_in, gated, other, every, part, fwd, mid, got, mine = refs[22:31]
        local, send_sem, recv_sem = refs[31:]
        net = Net(send_sem, recv_sem)
        c, z, x, zl, y = net.core, net.z, net.x, net.zl, net.y
        base_z, base_r, base_n = 8, 40, 64
        loads = []
        for k in range(4):
            block = z_ref.at[turn(z, k, 4)] if k else own_ref
            loads.append(pltpu.make_async_copy(block, down.at[k, x], local.at[16 + 4 * k]))
            for step in range(1, 4):
                at = turn(x, step, 4)
                loads.append(
                    pltpu.make_async_copy(
                        d_refs[k].at[at], down.at[k, at], local.at[16 + 4 * k + step]
                    )
                )
        loads += [
            pltpu.make_async_copy(b_refs[m], bases.at[m], local.at[8 + m]) for m in range(2)
        ]
        third = columns // 3
        for j in range(3):
            for m in range(2):
                loads.append(
                    pltpu.make_async_copy(
                        t_refs[j].at[m],
                        bases.at[2 + m, pl.ds(j * third, third)],
                        local.at[10 + 2 * j + m],
                    )
                )
        for load in loads:
            load.start()
        ones = [net.on_x(1), net.on_x(3), net.on_z(1), net.on_z(3)]
        net.greet(ones + [net.on_y(1), net.on_y(3), net.on_zl(1), net.on_core()])
        for load in loads[:16]:
            load.wait()
        quarter = features // 4
        left = back_ref[...].reshape(2 * 4 * tokens, features)
        for j, cut in enumerate(cuts):
            total = None
            for k in range(4):
                right = down[k, :, :, cut].reshape(quarter, cut.size)
                term = jnp.dot(
                    left[:, k * quarter : (k + 1) * quarter], right, preferred_element_type=F32
                )
                total = term if total is None else total + term
            h_ref[:, :, cut] = total.reshape(2, 4 * tokens, cut.size)
            net.send((0, 7)[j], h_ref.at[1 - c, :, cut], half_in.at[:, cut], net.on_core())
        net.send(1, i_ref, j_ref, net.on_core())

        def gate_rows(s, cut):
            some = pl.ds(pl.multiple_of(s * tokens, tokens), tokens)
            value = (h_ref[c, some, cut] + half_in[some, cut]) * g_ref[:, cut].astype(F32)
            gated[s, :, cut] = value.astype(BF16)

        for j, cut in enumerate(cuts):
            net.recv((0, 7)[j], half_in.at[:, cut])
            for s in range(2):
                gate_rows(2 * zl + s, cut)

        own = lambda h: other if h else gated.at[pl.ds(2 * zl, 2)]
        slot = lambda o, i, h: every.at[o, h, i]
        zp, zm, z2 = (turn(z, s, 4) for s in (1, 3, 2))
        xp, xm, x2 = (turn(x, s, 4) for s in (1, 3, 2))
        yp, ym, y2 = (turn(y, s, 4) for s in (1, 3, 2))
        order = (z, zm, zp, z2)
        inner = lambda row: base_z + 6 + 6 * row

        def along(row, h):
            o, b = order[row], inner(row)
            src = own(h) if row == 0 else slot(o, x, h)
            net.send(b + (0, 1)[h], src, slot(o, x, h), net.on_x(1))
            net.send(b + (3, 2)[h], src, slot(o, x, h), net.on_x(3))

        def forward(row):
            o, b = order[row], inner(row)
            net.recv(b, slot(o, xm, 0))
            net.send(b + 4, slot(o, xm, 0), slot(o, xm, 0), net.on_x(1))
            net.recv(b + 2, slot(o, xp, 1))
            net.send(b + 5, slot(o, xp, 1), slot(o, xp, 1), net.on_x(3))

        def rest(row):
            o, b = order[row], inner(row)
            net.recv(b + 1, slot(o, xm, 1))
            net.recv(b + 3, slot(o, xp, 0))
            net.recv(b + 4, slot(o, x2, 0))
            net.recv(b + 5, slot(o, x2, 1))

        def multiply(row):
            o = order[row]
            for m in range(2):
                block = None
                for h in range(2):
                    left = every[o, h].reshape(4 * rows, depth)
                    term = contract_last(left, bases[2 * h + m])
                    block = term if block is None else block + term
                part[row, :, m] = block.reshape(4, rows, columns)

        def reduce_start(k):
            b = base_r + 6 * k
            net.send(b, part.at[k, y2, 0], fwd.at[k, 0], net.on_y(1))
            net.send(b + 1, part.at[k, y2, 1], fwd.at[k, 1], net.on_y(3))
            net.send(b + 2, part.at[k, yp, 1], got.at[k, 0, 1], net.on_y(1))
            net.send(b + 3, part.at[k, ym, 0], got.at[k, 1, 0], net.on_y(3))

        def reduce_middle(k):
            b = base_r + 6 * k
            net.recv(b, fwd.at[k, 0])
            mid[k, 0] = part[k, yp, 0] + fwd[k, 0]
            net.send(b + 4, mid.at[k, 0], got.at[k, 0, 0], net.on_y(1))
            net.recv(b + 1, fwd.at[k, 1])
            mid[k, 1] = part[k, ym, 1] + fwd[k, 1]
            net.send(b + 5, mid.at[k, 1], got.at[k, 1, 1], net.on_y(3))

        def reduce_end(k):
            b = base_r + 6 * k
            net.recv(b + 2, got.at[k, 0, 1])
            net.recv(b + 5, got.at[k, 1, 1])
            value = part[k, y, 1] + got[k, 0, 1] + got[k, 1, 1]
            mine[k, 1] = value.astype(BF16).reshape(2, tokens, columns)
            net.send(3 + k, mine.at[k, 1], mine.at[k, 2], net.on_core())
            net.recv(b + 3, got.at[k, 1, 0])
            net.recv(b + 4, got.at[k, 0, 0])
            value = part[k, y, 0] + got[k, 0, 0] + got[k, 1, 0]
            mine[k, 0] = value.astype(BF16).reshape(2, tokens, columns)

        def square(k, stage):
            drive(stage)
            if k == 0:
                net.recv(1, j_ref)
            e = order[k]
            pairs[:, : 4 * tokens] = i_ref[e]
            pairs[:, 4 * tokens :] = j_ref[e]

            def tile(t, carry):
                cut = pl.ds(pl.multiple_of(t * 128, 128), 128)
                total = None
                for o in range(2):
                    for s in range(2):
                        right = spun[k, o, s].reshape(8 * tokens, columns)
                        block = jnp.dot(pairs[cut], right, preferred_element_type=F32)
                        block = block * block
                        total = block if total is None else total + block
                total = total * (1.0 / 16.0)
                corrected[cut] = total if k == 0 else corrected[cut] + total
                return carry

            lax.fori_loop(0, width // 128, tile, 0)

        def spread(k):
            mine_k = lambda h: mine.at[k, 2 * h]
            place = lambda o, i, h: spun.at[k, o, :, h, i]
            net.recv(3 + k, mine.at[k, 2])
            for h in range(2):
                spun[k, zl, :, h, y] = mine[k, 2 * h]
            base = base_n + gather_slots(2) * k
            return gather_stage(net, base, mine_k, place, 2, zl, y, net.on_zl, net.on_y)

        net.send(base_z, own(0), slot(z, x, 0), net.on_z(1))
        net.send(base_z + 3, own(0), slot(z, x, 0), net.on_z(3))
        along(0, 0)
        for cut in cuts:
            for s in range(2):
                gate_rows(2 * (1 - zl) + s, cut)
        net.send(2, gated.at[pl.ds(2 * (1 - zl), 2)], other, net.on_zl(1))
        net.recv(2, other)
        net.send(base_z + 2, own(1), slot(z, x, 1), net.on_z(3))
        net.send(base_z + 1, own(1), slot(z, x, 1), net.on_z(1))
        along(0, 1)
        copies = [pltpu.make_async_copy(own(h), slot(z, x, h), local.at[h]) for h in range(2)]
        for copy in copies:
            copy.start()
        net.recv(base_z, slot(zm, x, 0))
        net.send(base_z + 4, slot(zm, x, 0), slot(zm, x, 0), net.on_z(1))
        net.recv(base_z + 2, slot(zp, x, 1))
        net.send(base_z + 5, slot(zp, x, 1), slot(zp, x, 1), net.on_z(3))
        forward(0)
        net.recv(base_z + 1, slot(zm, x, 1))
        for h in range(2):
            along(1, h)
        rest(0)
        for copy in copies + loads[16:]:
            copy.wait()
        multiply(0)
        reduce_start(0)
        forward(1)
        net.recv(base_z + 3, slot(zp, x, 0))
        for h in range(2):
            along(2, h)
        reduce_middle(0)
        rest(1)
        reduce_end(0)
        multiply(1)
        reduce_start(1)
        spread_0 = spread(0)
        next(spread_0)
        forward(2)
        net.recv(base_z + 4, slot(z2, x, 0))
        net.recv(base_z + 5, slot(z2, x, 1))
        for h in range(2):
            along(3, h)
        reduce_middle(1)
        next(spread_0)
        rest(2)
        reduce_end(1)
        multiply(2)
        reduce_start(2)
        spread_1 = spread(1)
        next(spread_1)
        next(spread_0)
        forward(3)
        reduce_middle(2)
        next(spread_1)
        rest(3)
        multiply(3)
        reduce_start(3)
        reduce_end(2)
        spread_2 = spread(2)
        next(spread_2)
        next(spread_1)
        reduce_middle(3)
        square(0, spread_0)
        next(spread_2)
        reduce_end(3)
        spread_3 = spread(3)
        next(spread_3)
        next(spread_2)
        square(1, spread_1)
        next(spread_3)
        next(spread_3)
        square(2, spread_2)
        square(3, spread_3)
        o_ref[...] = corrected[...].T
        net.finish()

    return call(
        kernel,
        collective_id,
        like((columns, width), F32),
        [VMEM] * 3 + [ANY] * 11,
        VMEM,
        [
            pltpu.VMEM((4, 4, features // 16, depth), BF16),
            pltpu.VMEM((4, columns, depth), BF16),
            pltpu.VMEM((2, 4 * tokens, depth), F32),
            pltpu.VMEM(inputs.shape, BF16),
            pltpu.VMEM((4, 2, 2, 2, 4, tokens, columns), BF16),
            pltpu.VMEM((width, 8 * tokens), BF16),
            pltpu.VMEM((width, columns), F32),
            pltpu.VMEM((4 * tokens, depth), F32),
            pltpu.VMEM((4, tokens, depth), BF16),
            pltpu.VMEM((2, tokens, depth), BF16),
            pltpu.VMEM((4, 2, 4, 2, tokens, depth), BF16),
            pltpu.VMEM((4, 4, 2, rows, columns), F32),
            pltpu.VMEM((4, 2, rows, columns), F32),
            pltpu.VMEM((4, 2, rows, columns), F32),
            pltpu.VMEM((4, 2, 2, rows, columns), F32),
            pltpu.VMEM((4, 3, 2, tokens, columns), BF16),
            pltpu.SemaphoreType.DMA((32,)),
            *sems(64 + 4 * gather_slots(2)),
        ],
        (back, gate, inputs, down, down_z, *downs, *bases, *thirds),
        name,
        cost,
    )


def contract_last(left, right):
    return lax.dot_general(left, right, (((1,), (1,)), ((), ())), preferred_element_type=F32)


def per_device(
    resid, final_gain, unembed, labels, layer_in, gate_value, down_weight, basis_in, basis_out
):
    wide, narrow = lax.axis_index("wide"), lax.axis_index("narrow")
    core = lax.rem(wide, 2)
    tokens, width = resid.shape
    samples = labels.shape[1]
    vocab, part = unembed.shape
    hidden = down_weight.shape[0]
    width_in = basis_in.shape[1]
    pair = 2 * part
    core_tokens = 16 * tokens
    few = tokens // 8

    resid_float = resid.astype(F32)
    inverse = lax.rsqrt(jnp.mean(resid_float * resid_float, axis=1) + EPSILON)
    normed = (resid_float * inverse[:, None] * final_gain).astype(BF16)

    def blocks(rows):
        return rows.reshape(tokens, 16, pair).transpose(1, 0, 2)

    down, basis = down_weight.T, basis_out.T
    normed_cols, inputs_cols, unembed_other, basis_in_other, basis_other, down_0 = exchange(
        [blocks(normed), blocks(layer_in)],
        [unembed.T, basis_in, basis],
        [("x", down, 0)],
        0,
        "exchange",
        30,
    )
    mine = lax.dynamic_index_in_dim(
        labels.reshape(16, 2, 8, few, samples), core, 1, keepdims=False
    )
    shifted = mine.transpose(1, 0, 2, 3).reshape(core_tokens * samples, 1) - narrow * vocab
    common, inputs_rot, picked, down_z, down_1, third_0, third_1, third_2 = front(
        normed_cols.reshape(4, 4, tokens, pair),
        inputs_cols.reshape(4, 4, tokens, pair),
        [unembed.T, unembed_other],
        [basis_in, basis_in_other],
        shifted,
        down,
        basis,
        1,
        "front",
        100,
    )
    common = common.reshape(16, 8, few, pair).transpose(1, 0, 2, 3).reshape(2, 4, 16 * few, pair)
    common, down_2, inputs_all = reduce_over(
        [], [common], [("x", down_z, 2), ("all", inputs_rot, 0)], [F32], 4, "reduce_common", 20
    )
    inputs_all = inputs_all.reshape(4, 4 * tokens, width_in).transpose(0, 2, 1)
    grads = common.reshape(16, few, 1, pair) - picked.astype(F32).reshape(16, few, samples, pair)
    (grads,) = exchange([grads.reshape(16, few * samples, pair)], [], [], 5, "exchange_grads", 12)
    grads = grads.transpose(1, 0, 2).reshape(few, samples, width)
    resid_few = lax.dynamic_slice_in_dim(resid_float, narrow * few, few, 0)
    inverse_few = lax.dynamic_slice_in_dim(inverse, narrow * few, few, 0)
    inner = jnp.sum(final_gain * grads * resid_few[:, None, :], axis=2)
    back = (
        inverse_few[:, None, None] * final_gain * grads
        - resid_few[:, None, :] * (inverse_few**3)[:, None, None] * inner[:, :, None] / width
    )
    back = back.astype(BF16).reshape(few * samples, 4, 4, 2, part).transpose(3, 0, 1, 2, 4)
    back = lax.dynamic_slice_in_dim(
        jnp.concatenate([back, back], axis=2), lax.div(wide, 8), 4, axis=2
    )
    back, down_3 = gather_back(
        back.reshape(2, few * samples, width // 2), [("x", down_z, 3)], 6, "gather_back", 20
    )
    back = back.reshape(8, 2, few, samples, width // 2).transpose(1, 3, 0, 2, 4)
    return rotate_all(
        back.reshape(2, samples * tokens, width // 2),
        gate_value,
        down,
        down_z,
        [down_0, down_1, down_2, down_3],
        [basis, basis_other],
        [third_0, third_1, third_2],
        inputs_all,
        7,
        "rotate_all",
        110,
    )


def solution(mesh):
    in_specs = (
        P("wide", None),
        P(),
        P("narrow", "wide"),
        P(),
        P("wide", None),
        P("wide", "narrow"),
        P("narrow", "wide"),
        P("wide", "narrow"),
        P("narrow", "wide"),
    )
    out_specs = P("wide", "narrow")
    return jax.shard_map(
        per_device, mesh=mesh, in_specs=in_specs, out_specs=out_specs, check_vma=False
    )
```

```python
import functools

import jax
import jax.numpy as jnp
from jax import lax
from jax.experimental import pallas as pl
from jax.experimental.pallas import tpu as pltpu
from jax.sharding import PartitionSpec as P

EPSILON = 1e-05
MESH = pl.DeviceIdType.MESH
F32 = jnp.float32
BF16 = jnp.bfloat16
ANY = pl.BlockSpec(memory_space=pl.ANY)
VMEM = pl.BlockSpec(memory_space=pltpu.VMEM)


class Net:
    def __init__(self, send_sem, recv_sem):
        self.send_sem, self.recv_sem = send_sem, recv_sem
        self.started = []
        wide, narrow = lax.axis_index("wide"), lax.axis_index("narrow")
        self.wide, self.narrow = wide, narrow
        self.core = lax.rem(wide, 2)
        self.x = lax.rem(lax.div(wide, 2), 4)
        self.z = lax.div(wide, 8)
        self.y = lax.rem(narrow, 4)
        self.zl = lax.div(narrow, 4)

    def on_x(self, step):
        return {"wide": self.z * 8 + lax.rem(self.x + step, 4) * 2 + self.core}

    def on_z(self, step):
        return {"wide": lax.rem(self.z + step, 4) * 8 + self.x * 2 + self.core}

    def on_y(self, step):
        return {"narrow": self.zl * 4 + lax.rem(self.y + step, 4)}

    def on_zl(self, step):
        return {"narrow": (1 - self.zl) * 4 + self.y}

    def on_core(self):
        return {"wide": self.wide + 1 - 2 * self.core}

    def call_out(self, devices):
        barrier = pltpu.get_barrier_semaphore()
        for device in devices:
            pl.semaphore_signal(barrier, inc=1, device_id=device, device_id_type=MESH)
        return lambda: pl.semaphore_wait(barrier, len(devices))

    def greet(self, devices):
        self.call_out(devices)()

    def copy(self, slot, src, dst, device):
        return pltpu.make_async_remote_copy(
            src_ref=src,
            dst_ref=dst,
            send_sem=self.send_sem.at[slot],
            recv_sem=self.recv_sem.at[slot],
            device_id=device,
            device_id_type=MESH,
        )

    def send(self, slot, src, dst, device):
        copy = self.copy(slot, src, dst, device)
        copy.start()
        self.started.append(copy)

    def recv(self, slot, dst):
        self.copy(slot, dst, dst, self.on_core()).wait_recv()

    def finish(self):
        for copy in self.started:
            copy.wait_send()


def turn(place, step, size):
    return lax.rem(place + step, size)


def gather_stage(net, base, own, slot, outer_size, me_o, me_i, on_o, on_i):
    ip, im, i2 = (turn(me_i, s, 4) for s in (1, 3, 2))
    inner = lambda row: base + 6 + 6 * row

    def along(row, o, h, first=False):
        b = inner(row)
        src = own(h) if first else slot(o, me_i, h)
        net.send(b + h, src, slot(o, me_i, h), on_i(1))
        net.send(b + 3 - h, src, slot(o, me_i, h), on_i(3))

    def forward(row, o, ways=(0, 1)):
        b = inner(row)
        if 0 in ways:
            net.recv(b, slot(o, im, 0))
            net.send(b + 4, slot(o, im, 0), slot(o, im, 0), on_i(1))
        if 1 in ways:
            net.recv(b + 2, slot(o, ip, 1))
            net.send(b + 5, slot(o, ip, 1), slot(o, ip, 1), on_i(3))

    def rest(row, o):
        b = inner(row)
        net.recv(b + 1, slot(o, im, 1))
        net.recv(b + 3, slot(o, ip, 0))
        net.recv(b + 4, slot(o, i2, 0))
        net.recv(b + 5, slot(o, i2, 1))

    if outer_size == 4:
        op, om, o2 = (turn(me_o, s, 4) for s in (1, 3, 2))
        net.send(base, own(0), slot(me_o, me_i, 0), on_o(1))
        net.send(base + 2, own(1), slot(me_o, me_i, 1), on_o(3))
        net.send(base + 1, own(1), slot(me_o, me_i, 1), on_o(1))
        net.send(base + 3, own(0), slot(me_o, me_i, 0), on_o(3))
        for h in range(2):
            along(0, me_o, h, True)
        yield
        net.recv(base, slot(om, me_i, 0))
        net.send(base + 4, slot(om, me_i, 0), slot(om, me_i, 0), on_o(1))
        net.recv(base + 2, slot(op, me_i, 1))
        net.send(base + 5, slot(op, me_i, 1), slot(op, me_i, 1), on_o(3))
        forward(0, me_o)
        along(1, om, 0)
        along(2, op, 1)
        yield
        net.recv(base + 1, slot(om, me_i, 1))
        along(1, om, 1)
        net.recv(base + 3, slot(op, me_i, 0))
        along(2, op, 0)
        forward(1, om, (0,))
        forward(2, op, (1,))
        yield
        net.recv(base + 4, slot(o2, me_i, 0))
        along(3, o2, 0)
        net.recv(base + 5, slot(o2, me_i, 1))
        along(3, o2, 1)
        forward(1, om, (1,))
        forward(2, op, (0,))
        yield
        forward(3, o2)
        for row, o in enumerate((me_o, om, op, o2)):
            rest(row, o)
    else:
        oq = 1 - me_o
        for h in range(2):
            net.send(base + h, own(h), slot(me_o, me_i, h), on_o(1))
        for h in range(2):
            along(0, me_o, h, True)
        yield
        forward(0, me_o)
        for h in range(2):
            net.recv(base + h, slot(oq, me_i, h))
            along(1, oq, h)
        yield
        forward(1, oq)
        yield
        rest(0, me_o)
        rest(1, oq)


def gather_slots(outer_size):
    return 6 + 6 * outer_size


class Sum:
    def __init__(self, part, fwd, mid, got, tot, zfwd, zgot):
        self.part, self.fwd, self.mid, self.got = part, fwd, mid, got
        self.tot, self.zfwd, self.zgot = tot, zfwd, zgot
        self.half = part.shape[2] // 2

    @staticmethod
    def scratch(outer, rows, columns, dtype):
        half = rows // 2
        return [
            pltpu.VMEM((outer, 2, half, columns), dtype),
            pltpu.VMEM((outer, 2, half, columns), dtype),
            pltpu.VMEM((outer, 2, rows, columns), dtype),
            pltpu.VMEM((outer, rows, columns), dtype),
            pltpu.VMEM((2, half, columns), dtype),
            pltpu.VMEM((2, rows, columns), dtype),
        ]

    def h(self, k):
        return pl.ds(k * self.half, self.half)


def reduce_slots(outer_size):
    return 6 * outer_size + 6


def reduce_stage(net, base, sums, outer_size, me_o, me_i, on_o, on_i, prepare=None):
    ip, im, i2 = (turn(me_i, s, 4) for s in (1, 3, 2))
    offsets = (2, 1, 3, 0) if outer_size == 4 else (1, 0)
    rows = [turn(me_o, off, outer_size) for off in offsets]
    count = reduce_slots(outer_size)

    def at(a, k, j):
        return base + a * count + 6 * k + j

    def start_far(k):
        for a, s in enumerate(sums):
            net.send(at(a, k, 0), s.part.at[rows[k], i2, s.h(0)], s.fwd.at[k, 0], on_i(1))
            net.send(at(a, k, 1), s.part.at[rows[k], i2, s.h(1)], s.fwd.at[k, 1], on_i(3))

    def start_near(k):
        for a, s in enumerate(sums):
            net.send(at(a, k, 2), s.part.at[rows[k], ip, s.h(1)], s.got.at[k, 0, s.h(1)], on_i(1))
            net.send(at(a, k, 3), s.part.at[rows[k], im, s.h(0)], s.got.at[k, 1, s.h(0)], on_i(3))

    def middle(k):
        for a, s in enumerate(sums):
            net.recv(at(a, k, 0), s.fwd.at[k, 0])
            s.mid[k, 0] = s.part[rows[k], ip, s.h(0)] + s.fwd[k, 0]
            net.send(at(a, k, 4), s.mid.at[k, 0], s.got.at[k, 0, s.h(0)], on_i(1))
            net.recv(at(a, k, 1), s.fwd.at[k, 1])
            s.mid[k, 1] = s.part[rows[k], im, s.h(1)] + s.fwd[k, 1]
            net.send(at(a, k, 5), s.mid.at[k, 1], s.got.at[k, 1, s.h(1)], on_i(3))

    def total(k):
        for a, s in enumerate(sums):
            z = base + a * count + 6 * outer_size
            net.recv(at(a, k, 2), s.got.at[k, 0, s.h(1)])
            net.recv(at(a, k, 3), s.got.at[k, 1, s.h(0)])
            net.recv(at(a, k, 4), s.got.at[k, 0, s.h(0)])
            net.recv(at(a, k, 5), s.got.at[k, 1, s.h(1)])
            for h in range(2):
                s.tot[k, s.h(h)] = (
                    s.part[rows[k], me_i, s.h(h)] + s.got[k, 0, s.h(h)] + s.got[k, 1, s.h(h)]
                )
            if outer_size == 2:
                if k == 0:
                    for h in range(2):
                        net.send(z + h, s.tot.at[0, s.h(h)], s.zgot.at[0, s.h(h)], on_o(1))
            elif k == 0:
                net.send(z, s.tot.at[0, s.h(0)], s.zfwd.at[0], on_o(1))
                net.send(z + 1, s.tot.at[0, s.h(1)], s.zfwd.at[1], on_o(3))
            elif k == 1:
                net.send(z + 2, s.tot.at[1, s.h(1)], s.zgot.at[0, s.h(1)], on_o(1))
                net.recv(z, s.zfwd.at[0])
                s.tot[1, s.h(0)] += s.zfwd[0]
                net.send(z + 3, s.tot.at[1, s.h(0)], s.zgot.at[0, s.h(0)], on_o(1))
            elif k == 2:
                net.send(z + 4, s.tot.at[2, s.h(0)], s.zgot.at[1, s.h(0)], on_o(3))
                net.recv(z + 1, s.zfwd.at[1])
                s.tot[2, s.h(1)] += s.zfwd[1]
                net.send(z + 5, s.tot.at[2, s.h(1)], s.zgot.at[1, s.h(1)], on_o(3))

    def ready(k):
        if prepare is not None:
            prepare(rows[k])

    def steps():
        ready(0)
        start_far(0)
        start_near(0)
        ready(1)
        start_far(1)
        yield
        for k in range(outer_size):
            middle(k)
            if k + 1 < outer_size:
                start_near(k + 1)
            if k >= 1:
                total(k - 1)
            if k + 2 < outer_size:
                ready(k + 2)
                start_far(k + 2)
            yield
        total(outer_size - 1)

    def final(a):
        s = sums[a]
        z = base + a * count + 6 * outer_size
        last = outer_size - 1

        def value(h):
            if outer_size == 2:
                net.recv(z + h, s.zgot.at[0, s.h(h)])
                return s.tot[last, s.h(h)] + s.zgot[0, s.h(h)]
            first, second = ((z + 3, z + 4), (z + 2, z + 5))[h]
            net.recv(first, s.zgot.at[0, s.h(h)])
            net.recv(second, s.zgot.at[1, s.h(h)])
            return s.tot[last, s.h(h)] + s.zgot[0, s.h(h)] + s.zgot[1, s.h(h)]

        return value

    return steps(), [final(a) for a in range(len(sums))]


def drive(*stages):
    stages = list(stages)
    while stages:
        stages = [stage for stage in stages if next(stage, 0) is None]


def ring(net, base, own, slot, me, on):
    plus, minus, far = (turn(me, s, 4) for s in (1, 3, 2))
    net.send(base, own(0), slot(me, 0), on(1))
    net.send(base + 2, own(1), slot(me, 1), on(3))
    yield
    net.send(base + 1, own(1), slot(me, 1), on(1))
    net.send(base + 3, own(0), slot(me, 0), on(3))
    yield
    net.recv(base, slot(minus, 0))
    net.send(base + 4, slot(minus, 0), slot(minus, 0), on(1))
    net.recv(base + 2, slot(plus, 1))
    net.send(base + 5, slot(plus, 1), slot(plus, 1), on(3))
    yield
    net.recv(base + 1, slot(minus, 1))
    net.recv(base + 3, slot(plus, 0))
    net.recv(base + 4, slot(far, 0))
    net.recv(base + 5, slot(far, 1))


class Side:
    def __init__(self, tasks):
        self.tasks = tasks
        self.arrays = [array for _, array, _ in tasks]
        self.outs = []
        for kind, array, _ in tasks:
            rows, depth = array.shape[-2:]
            shape = (2, rows // 3, depth) if kind == "basis" else (4, rows, depth)
            shape = (4, 4, *array.shape) if kind == "all" else shape
            self.outs.append(like(shape, array.dtype))
        self.slots = 30 * len(tasks)

    def local(self):
        return [pltpu.SemaphoreType.DMA((max(len(self.tasks), 1),))]

    def peers(self, net):
        found = []
        for kind, _, _ in self.tasks:
            if kind == "x":
                found += [net.on_x(1), net.on_x(3)]
            elif kind == "z":
                found += [net.on_z(1), net.on_z(3)]
            elif kind == "all":
                found += [net.on_x(1), net.on_x(3), net.on_z(1), net.on_z(3)]
            else:
                found += [net.on_zl(1), net.on_core()]
        return found

    def stages(self, net, base, ins, outs, local):
        return [
            self.stage(net, base + 30 * t, kind, ins[t], outs[t], step, local.at[t])
            for t, (kind, _, step) in enumerate(self.tasks)
        ]

    def stage(self, net, base, kind, src, out, step, local):
        if kind == "basis":
            rows = out.shape[1]
            for _ in range((0, 2, 1)[step]):
                yield
            net.send(base, src.at[pl.ds(rows * step, rows)], out.at[0], net.on_zl(1))
            yield
            yield
            net.recv(base, out.at[0])
            net.send(base + 1, out.at[0], out.at[1], net.on_core())
            yield
            net.recv(base + 1, out.at[1])
            return
        if kind == "all":
            copy = pltpu.make_async_copy(src, out.at[net.z, net.x], local)
            copy.start()
            slot = lambda o, i, h: out.at[o, i, h]
            own = lambda h: src.at[h]
            yield from gather_stage(net, base, own, slot, 4, net.z, net.x, net.on_z, net.on_x)
            copy.wait()
            return
        half = out.shape[1] // 2
        cut = lambda h: pl.ds(h * half, half)
        row = src if len(src.shape) == 2 else src.at[turn(net.z, step, 4)]
        own = lambda h: row.at[cut(h)]
        slot = lambda i, h: out.at[i, cut(h)]
        if kind == "z":
            yield from ring(net, base, own, slot, net.z, net.on_z)
        else:
            yield from ring(net, base, own, slot, net.x, net.on_x)


def sems(slots):
    return [pltpu.SemaphoreType.DMA((slots,)), pltpu.SemaphoreType.DMA((slots,))]


def call(kernel, collective_id, outs, in_specs, out_specs, scratch, args, name, cost):
    return pl.pallas_call(
        kernel,
        out_shape=outs,
        in_specs=in_specs,
        out_specs=out_specs,
        scratch_shapes=scratch,
        compiler_params=pltpu.CompilerParams(
            collective_id=collective_id, has_side_effects=True, vmem_limit_bytes=60 << 20
        ),
        cost_estimate=pl.CostEstimate(flops=cost * 10**9, bytes_accessed=0, transcendentals=0),
        name=name,
    )(*args)


def like(shape, dtype):
    return jax.ShapeDtypeStruct(shape, dtype)


def exchange(arrays, pairs, tasks, collective_id, name, cost):
    na, np_, nt = len(arrays), len(pairs), len(tasks)
    side = Side(tasks)

    def kernel(*refs):
        ins, shared, side_in = refs[:na], refs[na : na + np_], refs[na + np_ : na + np_ + nt]
        refs = refs[na + np_ + nt :]
        outs, both, side_out = refs[:na], refs[na : na + np_], refs[na + np_ : na + np_ + nt]
        local, side_local, send_sem, recv_sem = refs[na + np_ + nt :]
        net = Net(send_sem, recv_sem)
        steps = [(dz, dx) for dz in range(4) for dx in range(4) if (dz, dx) != (0, 0)]
        steps.sort(key=lambda s: -(min(s[0], 4 - s[0]) * 2 + min(s[1], 4 - s[1])))

        def to(dz, dx):
            return turn(net.z, dz, 4) * 4 + turn(net.x, dx, 4)

        me = net.z * 4 + net.x
        peers = [{"wide": to(*s) * 2 + net.core} for s in steps]
        net.greet(peers + ([net.on_core()] if np_ else []) + side.peers(net))
        copies = []
        for j, s in enumerate(steps):
            for a in range(na):
                net.send(j * na + a, ins[a].at[to(*s)], outs[a].at[me], peers[j])
        for a in range(na):
            copies.append(pltpu.make_async_copy(ins[a].at[me], outs[a].at[me], local.at[a]))
        for b in range(np_):
            net.send(15 * na + b, shared[b], both[b], net.on_core())
        for copy in copies:
            copy.start()
        extra = side.stages(net, 15 * na + max(np_, 1), side_in, side_out, side_local)
        for _ in range(3):
            for stage in extra:
                next(stage)
        for j, (dz, dx) in enumerate(steps):
            source = to((4 - dz) % 4, (4 - dx) % 4)
            for a in range(na):
                net.recv(j * na + a, outs[a].at[source])
        for b in range(np_):
            net.recv(15 * na + b, both[b])
        drive(*extra)
        for copy in copies:
            copy.wait()
        net.finish()

    outs = [like(a.shape, a.dtype) for a in (*arrays, *pairs)]
    return call(
        kernel,
        collective_id,
        outs + side.outs,
        [ANY] * (na + np_ + nt),
        [ANY] * (na + np_ + nt),
        [
            pltpu.SemaphoreType.DMA((na,)),
            *side.local(),
            *sems(15 * na + max(np_, 1) + side.slots),
        ],
        (*arrays, *pairs, *side.arrays),
        name,
        cost,
    )


def reduce_over(wide_parts, narrow_parts, tasks, dtypes, collective_id, name, cost):
    parts = [*wide_parts, *narrow_parts]
    n, split, nt = len(parts), len(wide_parts), len(tasks)
    side = Side(tasks)
    slots = split * reduce_slots(4) + (n - split) * reduce_slots(2)

    def kernel(*refs):
        ins, side_in = refs[:n], refs[n : n + nt]
        outs, side_out = refs[n + nt : 2 * n + nt], refs[2 * n + nt : 2 * (n + nt)]
        buffers, (side_local, send_sem, recv_sem) = refs[2 * (n + nt) : -3], refs[-3:]
        net = Net(send_sem, recv_sem)
        sums = [Sum(ins[a], *buffers[6 * a : 6 * a + 6]) for a in range(n)]
        stages, ends, peers = [], [], []
        if split:
            peers += [net.on_x(1), net.on_x(3), net.on_z(1), net.on_z(3)]
            stage, end = reduce_stage(net, 0, sums[:split], 4, net.z, net.x, net.on_z, net.on_x)
            stages.append(stage)
            ends += end
        if n > split:
            peers += [net.on_y(1), net.on_y(3), net.on_zl(1)]
            base = split * reduce_slots(4)
            stage, end = reduce_stage(
                net, base, sums[split:], 2, net.zl, net.y, net.on_zl, net.on_y
            )
            stages.append(stage)
            ends += end
        net.greet(peers + side.peers(net))
        extra = side.stages(net, slots, side_in, side_out, side_local)
        drive(*stages, *extra)
        for a in range(n):
            for h in range(2):
                outs[a][sums[a].h(h), :] = ends[a](h).astype(outs[a].dtype)
        net.finish()

    scratch = []
    for p in parts:
        scratch += Sum.scratch(p.shape[0], p.shape[2], p.shape[3], p.dtype)
    return call(
        kernel,
        collective_id,
        [like(p.shape[2:], d) for p, d in zip(parts, dtypes)] + side.outs,
        [VMEM] * n + [ANY] * nt,
        [VMEM] * n + [ANY] * nt,
        [*scratch, *side.local(), *sems(slots + side.slots)],
        (*parts, *side.arrays),
        name,
        cost,
    )


def front(normed, inputs, unembeds, bases_in, ids, down, collective_id, name, cost):
    tokens, features = normed.shape[2:]
    half = features // 2
    vocab, width = unembeds[0].shape[1], bases_in[0].shape[1]
    count = ids.shape[0] // 8
    side = Side([("z", down, 0), ("x", down, 0)])
    base_i = reduce_slots(4)
    base_p = base_i + reduce_slots(4)
    base_s = base_p + reduce_slots(2)
    base_g = base_s + 7
    base_t = base_g + gather_slots(4)

    def kernel(*refs):
        n_ref, i_ref, id_ref, u0, u1, b0, b1, d_ref = refs[:8]
        common_ref, rot_ref, picked_ref, dz_ref, dx_ref = refs[8:13]
        unembed, basis_in, logit_part, input_part, pick_part = refs[13:18]
        sum_l, sum_i, sum_p = (refs[18 + 6 * j : 24 + 6 * j] for j in range(3))
        logits, mine, got, probs, every, local, send_sem, recv_sem = refs[36:]
        net = Net(send_sem, recv_sem)
        c = net.core
        loads = [
            pltpu.make_async_copy(u0, unembed.at[pl.ds(c * half, half)], local.at[0]),
            pltpu.make_async_copy(u1, unembed.at[pl.ds((1 - c) * half, half)], local.at[1]),
            pltpu.make_async_copy(b0, basis_in.at[pl.ds(c * half, half)], local.at[2]),
            pltpu.make_async_copy(b1, basis_in.at[pl.ds((1 - c) * half, half)], local.at[3]),
        ]
        for load in loads:
            load.start()
        ring_peers = [net.on_x(1), net.on_x(3), net.on_z(1), net.on_z(3), net.on_core()]
        narrow_peers = [{"narrow": turn(net.narrow, k, 8)} for k in range(1, 8)]
        net.greet(ring_peers + narrow_peers)
        for load in loads:
            load.wait()

        def dot_row(left, right, part):
            def run(row):
                rows = left[row].reshape(4 * tokens, features)
                value = jnp.dot(rows, right[...], preferred_element_type=F32)
                part[row] = value.reshape(4, tokens, part.shape[3])

            return run

        main, (end,) = reduce_stage(
            net, 0, [Sum(logit_part, *sum_l)], 4, net.z, net.x, net.on_z, net.on_x,
            dot_row(n_ref, unembed, logit_part),
        )
        late, (end_i,) = reduce_stage(
            net, base_i, [Sum(input_part, *sum_i)], 4, net.z, net.x, net.on_z, net.on_x,
            dot_row(i_ref, basis_in, input_part),
        )
        picks, (end_p,) = reduce_stage(
            net, base_p, [Sum(pick_part, *sum_p)], 2, net.zl, net.y, net.on_zl, net.on_y
        )

        def extra(t, out, kind, src, step):
            return side.stage(net, base_t + 30 * t, kind, src, out, step, None)

        ring_z = extra(0, dz_ref, "z", d_ref, 0)
        ring_x = extra(1, dx_ref, "x", d_ref, 0)

        def pick(j, carry):
            some = id_ref[pl.ds(pl.multiple_of(j * count, count), count)]
            one = some == lax.broadcasted_iota(jnp.int32, (count, vocab), 1)
            value = contract_last(jnp.where(one, 1.0, 0.0).astype(BF16), unembed[...])
            pick_part[lax.div(j, 4), lax.rem(j, 4)] = value.astype(BF16)
            return carry

        next(main)
        next(ring_z)
        for j in range(4):
            lax.fori_loop(2 * j, 2 * j + 2, pick, 0)
            if j == 3:
                next(picks)
            next(main)
        next(late)
        next(ring_x)
        next(ring_x)
        next(picks)
        drive(main)
        next(ring_z)
        for h in range(2):
            logits[pl.ds(h * (tokens // 2), tokens // 2), :] = end(h)
        top = jnp.max(logits[...], axis=1, keepdims=True)
        mine[0] = jnp.broadcast_to(top, (tokens, 128))
        mine[1] = jnp.broadcast_to(
            jnp.sum(jnp.exp(logits[...] - top), axis=1, keepdims=True), (tokens, 128)
        )
        for k in range(7):
            net.send(base_s + k, mine, got.at[k], narrow_peers[k])
        next(late)
        for k in range(7):
            net.recv(base_s + k, got.at[k])
        largest = mine[0]
        for k in range(7):
            largest = jnp.maximum(largest, got[k, 0])
        total = mine[1] * jnp.exp(mine[0] - largest)
        for k in range(7):
            total += got[k, 1] * jnp.exp(got[k, 0] - largest)
        value = (jnp.exp(logits[...] - largest[:, :1]) / total[:, :1]).astype(BF16)
        probs[...] = value.reshape(2, tokens // 2, vocab)
        every[net.z, net.x] = value.reshape(2, tokens // 2, vocab)
        slot = lambda o, i, h: every.at[o, i, h]
        own = lambda h: probs.at[h]
        spread = gather_stage(
            net, base_g, own, slot, 4, net.z, net.x, net.on_z, net.on_x
        )
        next(spread)
        next(ring_x)
        next(late)
        next(ring_z)
        next(spread)
        next(late)
        next(picks)
        next(spread)
        next(late)
        next(spread)
        drive(late)
        drive(spread)
        for h in range(2):
            rot_ref[h] = end_i(h).astype(BF16)
        drive(picks)
        for h in range(2):
            picked_ref[pl.ds(h * (count // 2), count // 2), :] = end_p(h).astype(BF16)
        for row in range(4):
            common_ref[row] = contract_last(
                every[row].reshape(4 * tokens, vocab), unembed[...]
            )
        drive(ring_x, ring_z)
        net.finish()

    return call(
        kernel,
        collective_id,
        [
            like((4, 4 * tokens, features), F32),
            like((2, tokens // 2, width), BF16),
            like((count, features), BF16),
            *side.outs,
        ],
        [VMEM] * 3 + [ANY] * 5,
        [VMEM] * 3 + [ANY] * 2,
        [
            pltpu.VMEM((features, vocab), BF16),
            pltpu.VMEM((features, width), BF16),
            pltpu.VMEM((4, 4, tokens, vocab), F32),
            pltpu.VMEM((4, 4, tokens, width), F32),
            pltpu.VMEM((2, 4, count, features), BF16),
            *Sum.scratch(4, tokens, vocab, F32),
            *Sum.scratch(4, tokens, width, F32),
            *Sum.scratch(2, count, features, BF16),
            pltpu.VMEM((tokens, vocab), F32),
            pltpu.VMEM((2, tokens, 128), F32),
            pltpu.VMEM((7, 2, tokens, 128), F32),
            pltpu.VMEM((2, tokens // 2, vocab), BF16),
            pltpu.VMEM((4, 4, 2, tokens // 2, vocab), BF16),
            pltpu.SemaphoreType.DMA((4,)),
            *sems(base_t + side.slots),
        ],
        (normed, inputs, ids, *unembeds, *bases_in, down),
        name,
        cost,
    )


def gather_back(shard, tasks, collective_id, name, cost):
    _, rows, features = shard.shape
    side, nt = Side(tasks), len(tasks)

    def kernel(*refs):
        x_ref, side_in, o_ref, side_out = refs[0], refs[1 : 1 + nt], refs[1 + nt], refs[2 + nt : -5]
        mine, local, side_local, send_sem, recv_sem = refs[-5:]
        net = Net(send_sem, recv_sem)
        net.greet([net.on_y(1), net.on_y(3), net.on_zl(1), net.on_core()] + side.peers(net))
        net.send(0, x_ref.at[1 - net.core], mine, net.on_core())
        slot = lambda o, i, h: o_ref.at[o, i, lax.rem(net.core + h, 2)]
        own = lambda h: mine if h else x_ref.at[net.core]
        net.recv(0, mine)
        copies = [
            pltpu.make_async_copy(own(h), slot(net.zl, net.y, h), local.at[h]) for h in range(2)
        ]
        for copy in copies:
            copy.start()
        drive(
            gather_stage(net, 1, own, slot, 2, net.zl, net.y, net.on_zl, net.on_y),
            *side.stages(net, 1 + gather_slots(2), side_in, side_out, side_local),
        )
        for copy in copies:
            copy.wait()
        net.finish()

    return call(
        kernel,
        collective_id,
        [like((2, 4, 2, rows, features), shard.dtype)] + side.outs,
        [ANY] * (1 + nt),
        [ANY] * (1 + nt),
        [
            pltpu.VMEM((rows, features), shard.dtype),
            pltpu.SemaphoreType.DMA((2,)),
            *side.local(),
            *sems(1 + gather_slots(2) + side.slots),
        ],
        (shard, *side.arrays),
        name,
        cost,
    )


def rotate_all(back, gate, down, down_z, downs, bases, thirds, inputs, collective_id, name, cost):
    tokens, depth = gate.shape
    columns = bases[0].shape[0]
    width = inputs.shape[2]
    rows = 2 * tokens
    features = back.shape[2]
    cuts = (pl.ds(0, 896), pl.ds(896, depth - 896))

    def kernel(*refs):
        back_ref, g_ref, i_ref, own_ref, z_ref, d_refs = *refs[:5], refs[5:9]
        b_refs, t_refs, o_ref = refs[9:11], refs[11:14], refs[14]
        down, bases, h_ref, ours_in, j_ref, spun, pairs, corrected = refs[15:23]
        half_in, gated, other, every, part, fwd, mid, got, mine = refs[23:32]
        local, send_sem, recv_sem = refs[32:]
        net = Net(send_sem, recv_sem)
        c, z, x, zl, y = net.core, net.z, net.x, net.zl, net.y
        base_z, base_r, base_n, base_i = 8, 40, 64, 136
        loads = []
        for k in range(4):
            block = z_ref.at[turn(z, k, 4)] if k else own_ref
            loads.append(pltpu.make_async_copy(block, down.at[k, x], local.at[16 + 4 * k]))
            for step in range(1, 4):
                at = turn(x, step, 4)
                loads.append(
                    pltpu.make_async_copy(
                        d_refs[k].at[at], down.at[k, at], local.at[16 + 4 * k + step]
                    )
                )
        loads += [
            pltpu.make_async_copy(b_refs[m], bases.at[m], local.at[8 + m]) for m in range(2)
        ]
        third = columns // 3
        for j in range(3):
            for m in range(2):
                loads.append(
                    pltpu.make_async_copy(
                        t_refs[j].at[m],
                        bases.at[2 + m, pl.ds(j * third, third)],
                        local.at[10 + 2 * j + m],
                    )
                )
        ones = [net.on_x(1), net.on_x(3), net.on_z(1), net.on_z(3)]
        all_here = net.call_out(ones + [net.on_y(1), net.on_y(3), net.on_zl(1), net.on_core()])
        for load in loads[:16]:
            load.start()
        quarter = features // 4
        left = back_ref[...].reshape(2 * 4 * tokens, features)
        for j, cut in enumerate(cuts):
            total = None
            for k in range(4):
                if j == 0:
                    for load in loads[4 * k : 4 * k + 4]:
                        load.wait()
                right = down[k, :, :, cut].reshape(quarter, cut.size)
                term = jnp.dot(
                    left[:, k * quarter : (k + 1) * quarter], right, preferred_element_type=F32
                )
                total = term if total is None else total + term
            h_ref[:, :, cut] = total.reshape(2, 4 * tokens, cut.size)
        for load in loads[16:]:
            load.start()
        all_here()
        theirs, ours = (
            pl.ds(pl.multiple_of(2 * tokens * o, 2 * tokens), 2 * tokens) for o in (1 - zl, zl)
        )
        net.send(0, h_ref.at[1 - c, theirs], half_in.at[theirs], net.on_core())
        net.send(7, h_ref.at[1 - c, ours], half_in.at[ours], net.on_core())
        ours_in[z, x] = i_ref[...]
        inputs_stage = gather_stage(
            net, base_i, lambda h: i_ref.at[h], lambda o, i, h: ours_in.at[o, i, h],
            4, z, x, net.on_z, net.on_x,
        )
        next(inputs_stage)

        def gate_rows(s):
            some = pl.ds(pl.multiple_of(s * tokens, tokens), tokens)
            value = (h_ref[c, some] + half_in[some]) * g_ref[...].astype(F32)
            gated[s] = value.astype(BF16)

        net.recv(0, half_in.at[theirs])
        for s in range(2):
            gate_rows(2 * (1 - zl) + s)
        net.send(2, gated.at[pl.ds(2 * (1 - zl), 2)], other, net.on_zl(1))
        next(inputs_stage)
        net.recv(7, half_in.at[ours])
        for s in range(2):
            gate_rows(2 * zl + s)

        own = lambda h: other if h else gated.at[pl.ds(2 * zl, 2)]
        slot = lambda o, i, h: every.at[o, h, i]
        zp, zm, z2 = (turn(z, s, 4) for s in (1, 3, 2))
        xp, xm, x2 = (turn(x, s, 4) for s in (1, 3, 2))
        yp, ym, y2 = (turn(y, s, 4) for s in (1, 3, 2))
        order = (z, zm, zp, z2)
        inner = lambda row: base_z + 6 + 6 * row

        def along(row, h):
            o, b = order[row], inner(row)
            src = own(h) if row == 0 else slot(o, x, h)
            net.send(b + h, src, slot(o, x, h), net.on_x(1))
            net.send(b + 3 - h, src, slot(o, x, h), net.on_x(3))

        def forward(row, ways=(0, 1)):
            o, b = order[row], inner(row)
            if 0 in ways:
                net.recv(b, slot(o, xm, 0))
                net.send(b + 4, slot(o, xm, 0), slot(o, xm, 0), net.on_x(1))
            if 1 in ways:
                net.recv(b + 2, slot(o, xp, 1))
                net.send(b + 5, slot(o, xp, 1), slot(o, xp, 1), net.on_x(3))

        def rest(row):
            o, b = order[row], inner(row)
            net.recv(b + 1, slot(o, xm, 1))
            net.recv(b + 3, slot(o, xp, 0))
            net.recv(b + 4, slot(o, x2, 0))
            net.recv(b + 5, slot(o, x2, 1))

        def multiply(row):
            o = order[row]
            for m in range(2):
                block = None
                for h in range(2):
                    left = every[o, h].reshape(4 * rows, depth)
                    term = contract_last(left, bases[2 * h + m])
                    block = term if block is None else block + term
                part[row, :, m] = block.reshape(4, rows, columns)

        def reduce_start(k):
            b = base_r + 6 * k
            net.send(b, part.at[k, y2, 0], fwd.at[k, 0], net.on_y(1))
            net.send(b + 1, part.at[k, y2, 1], fwd.at[k, 1], net.on_y(3))
            net.send(b + 2, part.at[k, yp, 1], got.at[k, 0, 1], net.on_y(1))
            net.send(b + 3, part.at[k, ym, 0], got.at[k, 1, 0], net.on_y(3))

        def reduce_middle(k):
            b = base_r + 6 * k
            net.recv(b, fwd.at[k, 0])
            mid[k, 0] = part[k, yp, 0] + fwd[k, 0]
            net.send(b + 4, mid.at[k, 0], got.at[k, 0, 0], net.on_y(1))
            net.recv(b + 1, fwd.at[k, 1])
            mid[k, 1] = part[k, ym, 1] + fwd[k, 1]
            net.send(b + 5, mid.at[k, 1], got.at[k, 1, 1], net.on_y(3))

        def reduce_end(k):
            b = base_r + 6 * k
            net.recv(b + 2, got.at[k, 0, 1])
            net.recv(b + 5, got.at[k, 1, 1])
            value = part[k, y, 1] + got[k, 0, 1] + got[k, 1, 1]
            mine[k, 1] = value.astype(BF16).reshape(2, tokens, columns)
            net.send(3 + k, mine.at[k, 1], mine.at[k, 2], net.on_core())
            net.recv(b + 3, got.at[k, 1, 0])
            net.recv(b + 4, got.at[k, 0, 0])
            value = part[k, y, 0] + got[k, 0, 0] + got[k, 1, 0]
            mine[k, 0] = value.astype(BF16).reshape(2, tokens, columns)

        def square(k, stage):
            drive(stage)
            if k == 0:
                net.recv(1, j_ref)
            e = order[k]
            pairs[:, : 4 * tokens] = ours_in[e].reshape(4 * tokens, width).T
            pairs[:, 4 * tokens :] = j_ref[e].reshape(4 * tokens, width).T

            def tile(t, carry):
                cut = pl.ds(pl.multiple_of(t * 128, 128), 128)
                total = None
                for o in range(2):
                    for s in range(2):
                        right = spun[k, o, s].reshape(8 * tokens, columns)
                        block = jnp.dot(pairs[cut], right, preferred_element_type=F32)
                        block = block * block
                        total = block if total is None else total + block
                total = total * (1.0 / 16.0)
                corrected[cut] = total if k == 0 else corrected[cut] + total
                return carry

            lax.fori_loop(0, width // 128, tile, 0)

        def spread(k):
            mine_k = lambda h: mine.at[k, 2 * h]
            place = lambda o, i, h: spun.at[k, o, :, h, i]
            net.recv(3 + k, mine.at[k, 2])
            for h in range(2):
                spun[k, zl, :, h, y] = mine[k, 2 * h]
            base = base_n + gather_slots(2) * k
            return gather_stage(net, base, mine_k, place, 2, zl, y, net.on_zl, net.on_y)

        net.send(base_z, own(0), slot(z, x, 0), net.on_z(1))
        net.send(base_z + 3, own(0), slot(z, x, 0), net.on_z(3))
        along(0, 0)
        next(inputs_stage)
        net.recv(2, other)
        net.send(base_z + 2, own(1), slot(z, x, 1), net.on_z(3))
        net.send(base_z + 1, own(1), slot(z, x, 1), net.on_z(1))
        along(0, 1)
        copies = [pltpu.make_async_copy(own(h), slot(z, x, h), local.at[h]) for h in range(2)]
        for copy in copies:
            copy.start()
        drive(inputs_stage)
        net.send(1, ours_in, j_ref, net.on_core())
        net.recv(base_z, slot(zm, x, 0))
        net.send(base_z + 4, slot(zm, x, 0), slot(zm, x, 0), net.on_z(1))
        net.recv(base_z + 2, slot(zp, x, 1))
        net.send(base_z + 5, slot(zp, x, 1), slot(zp, x, 1), net.on_z(3))
        forward(0)
        along(1, 0)
        net.recv(base_z + 1, slot(zm, x, 1))
        along(1, 1)
        rest(0)
        for copy in copies + loads[16:]:
            copy.wait()
        multiply(0)
        reduce_start(0)
        forward(1)
        along(2, 1)
        net.recv(base_z + 3, slot(zp, x, 0))
        along(2, 0)
        reduce_middle(0)
        rest(1)
        last = inner(3)
        net.send(last + 1, slot(zm, xp, 1), slot(zm, xp, 1), net.on_z(1))
        net.send(last + 2, slot(zm, xm, 1), slot(zm, xm, 1), net.on_z(1))
        reduce_end(0)
        multiply(1)
        reduce_start(1)
        spread_0 = spread(0)
        next(spread_0)
        forward(2)
        net.recv(base_z + 4, slot(z2, x, 0))
        along(3, 0)
        reduce_middle(1)
        next(spread_0)
        rest(2)
        net.send(last + 5, slot(zp, x2, 1), slot(zp, x2, 1), net.on_z(3))
        reduce_end(1)
        multiply(2)
        reduce_start(2)
        spread_1 = spread(1)
        next(spread_1)
        next(spread_0)
        forward(3, (0,))
        reduce_middle(2)
        next(spread_1)
        net.recv(base_z + 5, slot(z2, x, 1))
        net.recv(last + 3, slot(z2, xp, 0))
        net.recv(last + 4, slot(z2, x2, 0))
        net.recv(last + 1, slot(z2, xp, 1))
        net.recv(last + 2, slot(z2, xm, 1))
        net.recv(last + 5, slot(z2, x2, 1))
        multiply(3)
        reduce_start(3)
        reduce_end(2)
        spread_2 = spread(2)
        next(spread_2)
        next(spread_1)
        reduce_middle(3)
        square(0, spread_0)
        next(spread_2)
        reduce_end(3)
        spread_3 = spread(3)
        next(spread_3)
        next(spread_2)
        square(1, spread_1)
        next(spread_3)
        next(spread_3)
        square(2, spread_2)
        square(3, spread_3)
        o_ref[...] = corrected[...].T
        net.finish()

    return call(
        kernel,
        collective_id,
        like((columns, width), F32),
        [VMEM] * 3 + [ANY] * 11,
        VMEM,
        [
            pltpu.VMEM((4, 4, features // 16, depth), BF16),
            pltpu.VMEM((4, columns, depth), BF16),
            pltpu.VMEM((2, 4 * tokens, depth), F32),
            pltpu.VMEM((4, 4, *inputs.shape), BF16),
            pltpu.VMEM((4, 4, *inputs.shape), BF16),
            pltpu.VMEM((4, 2, 2, 2, 4, tokens, columns), BF16),
            pltpu.VMEM((width, 8 * tokens), BF16),
            pltpu.VMEM((width, columns), F32),
            pltpu.VMEM((4 * tokens, depth), F32),
            pltpu.VMEM((4, tokens, depth), BF16),
            pltpu.VMEM((2, tokens, depth), BF16),
            pltpu.VMEM((4, 2, 4, 2, tokens, depth), BF16),
            pltpu.VMEM((4, 4, 2, rows, columns), F32),
            pltpu.VMEM((4, 2, rows, columns), F32),
            pltpu.VMEM((4, 2, rows, columns), F32),
            pltpu.VMEM((4, 2, 2, rows, columns), F32),
            pltpu.VMEM((4, 3, 2, tokens, columns), BF16),
            pltpu.SemaphoreType.DMA((32,)),
            *sems(64 + 4 * gather_slots(2) + gather_slots(4)),
        ],
        (back, gate, inputs, down, down_z, *downs, *bases, *thirds),
        name,
        cost,
    )


def contract_last(left, right):
    return lax.dot_general(left, right, (((1,), (1,)), ((), ())), preferred_element_type=F32)


def per_device(
    resid, final_gain, unembed, labels, layer_in, gate_value, down_weight, basis_in, basis_out
):
    wide, narrow = lax.axis_index("wide"), lax.axis_index("narrow")
    core = lax.rem(wide, 2)
    tokens, width = resid.shape
    samples = labels.shape[1]
    vocab, part = unembed.shape
    hidden = down_weight.shape[0]
    width_in = basis_in.shape[1]
    pair = 2 * part
    core_tokens = 16 * tokens
    few = tokens // 8

    resid_float = resid.astype(F32)
    inverse = lax.rsqrt(jnp.mean(resid_float * resid_float, axis=1) + EPSILON)
    normed = (resid_float * inverse[:, None] * final_gain).astype(BF16)

    def blocks(rows):
        return rows.reshape(tokens, 16, pair).transpose(1, 0, 2)

    down, basis = down_weight.T, basis_out.T
    normed_cols, inputs_cols, unembed_other, basis_in_other, basis_other = exchange(
        [blocks(normed), blocks(layer_in)],
        [unembed.T, basis_in, basis],
        [],
        0,
        "exchange",
        30,
    )
    mine = lax.dynamic_index_in_dim(
        labels.reshape(16, 2, 8, few, samples), core, 1, keepdims=False
    )
    shifted = mine.transpose(1, 0, 2, 3).reshape(core_tokens * samples, 1) - narrow * vocab
    common, inputs_rot, picked, down_z, down_0 = front(
        normed_cols.reshape(4, 4, tokens, pair),
        inputs_cols.reshape(4, 4, tokens, pair),
        [unembed.T, unembed_other],
        [basis_in, basis_in_other],
        shifted,
        down,
        1,
        "front",
        100,
    )
    common = common.reshape(16, 8, few, pair).transpose(1, 0, 2, 3).reshape(2, 4, 16 * few, pair)
    common, down_1, third_0, third_1 = reduce_over(
        [],
        [common],
        [("x", down_z, 1), ("basis", basis, 0), ("basis", basis, 1)],
        [F32],
        4,
        "reduce_common",
        30,
    )
    grads = common.reshape(16, few, 1, pair) - picked.astype(F32).reshape(16, few, samples, pair)
    grads, down_2 = exchange(
        [grads.reshape(16, few * samples, pair)],
        [],
        [("x", down_z, 2)],
        5,
        "exchange_grads",
        20,
    )
    grads = grads.transpose(1, 0, 2).reshape(few, samples, width)
    resid_few = lax.dynamic_slice_in_dim(resid_float, narrow * few, few, 0)
    inverse_few = lax.dynamic_slice_in_dim(inverse, narrow * few, few, 0)
    inner = jnp.sum(final_gain * grads * resid_few[:, None, :], axis=2)
    back = (
        inverse_few[:, None, None] * final_gain * grads
        - resid_few[:, None, :] * (inverse_few**3)[:, None, None] * inner[:, :, None] / width
    )
    back = back.astype(BF16).reshape(few * samples, 4, 4, 2, part).transpose(3, 0, 1, 2, 4)
    back = lax.dynamic_slice_in_dim(
        jnp.concatenate([back, back], axis=2), lax.div(wide, 8), 4, axis=2
    )
    back, down_3, third_2 = gather_back(
        back.reshape(2, few * samples, width // 2),
        [("x", down_z, 3), ("basis", basis, 2)],
        6,
        "gather_back",
        20,
    )
    back = back.reshape(8, 2, few, samples, width // 2).transpose(1, 3, 0, 2, 4)
    return rotate_all(
        back.reshape(2, samples * tokens, width // 2),
        gate_value,
        down,
        down_z,
        [down_0, down_1, down_2, down_3],
        [basis, basis_other],
        [third_0, third_1, third_2],
        inputs_rot,
        7,
        "rotate_all",
        110,
    )


def solution(mesh):
    in_specs = (
        P("wide", None),
        P(),
        P("narrow", "wide"),
        P(),
        P("wide", None),
        P("wide", "narrow"),
        P("narrow", "wide"),
        P("wide", "narrow"),
        P("narrow", "wide"),
    )
    out_specs = P("wide", "narrow")
    return jax.shard_map(
        per_device, mesh=mesh, in_specs=in_specs, out_specs=out_specs, check_vma=False
    )
```

```python
import functools

import jax
import jax.numpy as jnp
from jax import lax
from jax.experimental import pallas as pl
from jax.experimental.pallas import tpu as pltpu
from jax.sharding import PartitionSpec as P

EPSILON = 1e-05
MESH = pl.DeviceIdType.MESH
F32 = jnp.float32
BF16 = jnp.bfloat16
ANY = pl.BlockSpec(memory_space=pl.ANY)
VMEM = pl.BlockSpec(memory_space=pltpu.VMEM)


class Net:
    def __init__(self, send_sem, recv_sem):
        self.send_sem, self.recv_sem = send_sem, recv_sem
        self.started = []
        wide, narrow = lax.axis_index("wide"), lax.axis_index("narrow")
        self.wide, self.narrow = wide, narrow
        self.core = lax.rem(wide, 2)
        self.x = lax.rem(lax.div(wide, 2), 4)
        self.z = lax.div(wide, 8)
        self.y = lax.rem(narrow, 4)
        self.zl = lax.div(narrow, 4)

    def on_x(self, step):
        return {"wide": self.z * 8 + lax.rem(self.x + step, 4) * 2 + self.core}

    def on_z(self, step):
        return {"wide": lax.rem(self.z + step, 4) * 8 + self.x * 2 + self.core}

    def on_y(self, step):
        return {"narrow": self.zl * 4 + lax.rem(self.y + step, 4)}

    def on_zl(self, step):
        return {"narrow": (1 - self.zl) * 4 + self.y}

    def on_core(self):
        return {"wide": self.wide + 1 - 2 * self.core}

    def call_out(self, devices):
        barrier = pltpu.get_barrier_semaphore()
        for device in devices:
            pl.semaphore_signal(barrier, inc=1, device_id=device, device_id_type=MESH)
        return lambda: pl.semaphore_wait(barrier, len(devices))

    def greet(self, devices):
        self.call_out(devices)()

    def copy(self, slot, src, dst, device):
        return pltpu.make_async_remote_copy(
            src_ref=src,
            dst_ref=dst,
            send_sem=self.send_sem.at[slot],
            recv_sem=self.recv_sem.at[slot],
            device_id=device,
            device_id_type=MESH,
        )

    def send(self, slot, src, dst, device):
        copy = self.copy(slot, src, dst, device)
        copy.start()
        self.started.append(copy)

    def recv(self, slot, dst):
        self.copy(slot, dst, dst, self.on_core()).wait_recv()

    def finish(self):
        for copy in self.started:
            copy.wait_send()


def turn(place, step, size):
    return lax.rem(place + step, size)


def gather_stage(net, base, own, slot, outer_size, me_o, me_i, on_o, on_i):
    ip, im, i2 = (turn(me_i, s, 4) for s in (1, 3, 2))
    inner = lambda row: base + 6 + 6 * row

    def along(row, o, h, first=False):
        b = inner(row)
        src = own(h) if first else slot(o, me_i, h)
        net.send(b + h, src, slot(o, me_i, h), on_i(1))
        net.send(b + 3 - h, src, slot(o, me_i, h), on_i(3))

    def forward(row, o, ways=(0, 1)):
        b = inner(row)
        if 0 in ways:
            net.recv(b, slot(o, im, 0))
            net.send(b + 4, slot(o, im, 0), slot(o, im, 0), on_i(1))
        if 1 in ways:
            net.recv(b + 2, slot(o, ip, 1))
            net.send(b + 5, slot(o, ip, 1), slot(o, ip, 1), on_i(3))

    def rest(row, o):
        b = inner(row)
        net.recv(b + 1, slot(o, im, 1))
        net.recv(b + 3, slot(o, ip, 0))
        net.recv(b + 4, slot(o, i2, 0))
        net.recv(b + 5, slot(o, i2, 1))

    if outer_size == 4:
        op, om, o2 = (turn(me_o, s, 4) for s in (1, 3, 2))
        net.send(base, own(0), slot(me_o, me_i, 0), on_o(1))
        net.send(base + 2, own(1), slot(me_o, me_i, 1), on_o(3))
        net.send(base + 1, own(1), slot(me_o, me_i, 1), on_o(1))
        net.send(base + 3, own(0), slot(me_o, me_i, 0), on_o(3))
        for h in range(2):
            along(0, me_o, h, True)
        yield
        net.recv(base, slot(om, me_i, 0))
        net.send(base + 4, slot(om, me_i, 0), slot(om, me_i, 0), on_o(1))
        net.recv(base + 2, slot(op, me_i, 1))
        net.send(base + 5, slot(op, me_i, 1), slot(op, me_i, 1), on_o(3))
        forward(0, me_o)
        along(1, om, 0)
        along(2, op, 1)
        yield
        net.recv(base + 1, slot(om, me_i, 1))
        along(1, om, 1)
        net.recv(base + 3, slot(op, me_i, 0))
        along(2, op, 0)
        forward(1, om, (0,))
        forward(2, op, (1,))
        yield
        net.recv(base + 4, slot(o2, me_i, 0))
        along(3, o2, 0)
        net.recv(base + 5, slot(o2, me_i, 1))
        along(3, o2, 1)
        forward(1, om, (1,))
        forward(2, op, (0,))
        yield
        forward(3, o2)
        for row, o in enumerate((me_o, om, op, o2)):
            rest(row, o)
            yield
    else:
        oq = 1 - me_o
        for h in range(2):
            net.send(base + h, own(h), slot(me_o, me_i, h), on_o(1))
        for h in range(2):
            along(0, me_o, h, True)
        yield
        forward(0, me_o)
        for h in range(2):
            net.recv(base + h, slot(oq, me_i, h))
            along(1, oq, h)
        yield
        forward(1, oq)
        yield
        rest(0, me_o)
        rest(1, oq)


def gather_slots(outer_size):
    return 6 + 6 * outer_size


class Sum:
    def __init__(self, part, fwd, mid, got, tot, zfwd, zgot):
        self.part, self.fwd, self.mid, self.got = part, fwd, mid, got
        self.tot, self.zfwd, self.zgot = tot, zfwd, zgot
        self.half = part.shape[2] // 2

    @staticmethod
    def scratch(outer, rows, columns, dtype):
        half = rows // 2
        return [
            pltpu.VMEM((outer, 2, half, columns), dtype),
            pltpu.VMEM((outer, 2, half, columns), dtype),
            pltpu.VMEM((outer, 2, rows, columns), dtype),
            pltpu.VMEM((outer, rows, columns), dtype),
            pltpu.VMEM((2, half, columns), dtype),
            pltpu.VMEM((2, rows, columns), dtype),
        ]

    def h(self, k):
        return pl.ds(k * self.half, self.half)


def reduce_slots(outer_size):
    return 6 * outer_size + 6


def reduce_stage(net, base, sums, outer_size, me_o, me_i, on_o, on_i, prepare=None):
    ip, im, i2 = (turn(me_i, s, 4) for s in (1, 3, 2))
    offsets = (2, 1, 3, 0) if outer_size == 4 else (1, 0)
    rows = [turn(me_o, off, outer_size) for off in offsets]
    count = reduce_slots(outer_size)

    def at(a, k, j):
        return base + a * count + 6 * k + j

    def start_far(k):
        for a, s in enumerate(sums):
            net.send(at(a, k, 0), s.part.at[rows[k], i2, s.h(0)], s.fwd.at[k, 0], on_i(1))
            net.send(at(a, k, 1), s.part.at[rows[k], i2, s.h(1)], s.fwd.at[k, 1], on_i(3))

    def start_near(k):
        for a, s in enumerate(sums):
            net.send(at(a, k, 2), s.part.at[rows[k], ip, s.h(1)], s.got.at[k, 0, s.h(1)], on_i(1))
            net.send(at(a, k, 3), s.part.at[rows[k], im, s.h(0)], s.got.at[k, 1, s.h(0)], on_i(3))

    def middle(k):
        for a, s in enumerate(sums):
            net.recv(at(a, k, 0), s.fwd.at[k, 0])
            s.mid[k, 0] = s.part[rows[k], ip, s.h(0)] + s.fwd[k, 0]
            net.send(at(a, k, 4), s.mid.at[k, 0], s.got.at[k, 0, s.h(0)], on_i(1))
            net.recv(at(a, k, 1), s.fwd.at[k, 1])
            s.mid[k, 1] = s.part[rows[k], im, s.h(1)] + s.fwd[k, 1]
            net.send(at(a, k, 5), s.mid.at[k, 1], s.got.at[k, 1, s.h(1)], on_i(3))

    def total(k):
        for a, s in enumerate(sums):
            z = base + a * count + 6 * outer_size
            net.recv(at(a, k, 2), s.got.at[k, 0, s.h(1)])
            net.recv(at(a, k, 3), s.got.at[k, 1, s.h(0)])
            net.recv(at(a, k, 4), s.got.at[k, 0, s.h(0)])
            net.recv(at(a, k, 5), s.got.at[k, 1, s.h(1)])
            for h in range(2):
                s.tot[k, s.h(h)] = (
                    s.part[rows[k], me_i, s.h(h)] + s.got[k, 0, s.h(h)] + s.got[k, 1, s.h(h)]
                )
            if outer_size == 2:
                if k == 0:
                    for h in range(2):
                        net.send(z + h, s.tot.at[0, s.h(h)], s.zgot.at[0, s.h(h)], on_o(1))
            elif k == 0:
                net.send(z, s.tot.at[0, s.h(0)], s.zfwd.at[0], on_o(1))
                net.send(z + 1, s.tot.at[0, s.h(1)], s.zfwd.at[1], on_o(3))
            elif k == 1:
                net.send(z + 2, s.tot.at[1, s.h(1)], s.zgot.at[0, s.h(1)], on_o(1))
                net.recv(z, s.zfwd.at[0])
                s.tot[1, s.h(0)] += s.zfwd[0]
                net.send(z + 3, s.tot.at[1, s.h(0)], s.zgot.at[0, s.h(0)], on_o(1))
            elif k == 2:
                net.send(z + 4, s.tot.at[2, s.h(0)], s.zgot.at[1, s.h(0)], on_o(3))
                net.recv(z + 1, s.zfwd.at[1])
                s.tot[2, s.h(1)] += s.zfwd[1]
                net.send(z + 5, s.tot.at[2, s.h(1)], s.zgot.at[1, s.h(1)], on_o(3))

    def ready(k):
        if prepare is not None:
            prepare(rows[k])

    def steps():
        ready(0)
        start_far(0)
        start_near(0)
        ready(1)
        start_far(1)
        yield
        for k in range(outer_size):
            middle(k)
            if k + 1 < outer_size:
                start_near(k + 1)
            if k >= 1:
                total(k - 1)
            if k + 2 < outer_size:
                ready(k + 2)
                start_far(k + 2)
            yield
        total(outer_size - 1)

    def final(a):
        s = sums[a]
        z = base + a * count + 6 * outer_size
        last = outer_size - 1

        def value(h):
            if outer_size == 2:
                net.recv(z + h, s.zgot.at[0, s.h(h)])
                return s.tot[last, s.h(h)] + s.zgot[0, s.h(h)]
            first, second = ((z + 3, z + 4), (z + 2, z + 5))[h]
            net.recv(first, s.zgot.at[0, s.h(h)])
            net.recv(second, s.zgot.at[1, s.h(h)])
            return s.tot[last, s.h(h)] + s.zgot[0, s.h(h)] + s.zgot[1, s.h(h)]

        return value

    return steps(), [final(a) for a in range(len(sums))]


def drive(*stages):
    stages = list(stages)
    while stages:
        stages = [stage for stage in stages if next(stage, 0) is None]


def ring(net, base, own, slot, me, on):
    plus, minus, far = (turn(me, s, 4) for s in (1, 3, 2))
    net.send(base, own(0), slot(me, 0), on(1))
    net.send(base + 2, own(1), slot(me, 1), on(3))
    yield
    net.send(base + 1, own(1), slot(me, 1), on(1))
    net.send(base + 3, own(0), slot(me, 0), on(3))
    yield
    net.recv(base, slot(minus, 0))
    net.send(base + 4, slot(minus, 0), slot(minus, 0), on(1))
    net.recv(base + 2, slot(plus, 1))
    net.send(base + 5, slot(plus, 1), slot(plus, 1), on(3))
    yield
    net.recv(base + 1, slot(minus, 1))
    net.recv(base + 3, slot(plus, 0))
    net.recv(base + 4, slot(far, 0))
    net.recv(base + 5, slot(far, 1))


class Side:
    def __init__(self, tasks):
        self.tasks = tasks
        self.arrays = [array for _, array, _ in tasks]
        self.outs = []
        for kind, array, _ in tasks:
            rows, depth = array.shape[-2:]
            shape = (2, rows // 3, depth) if kind == "basis" else (4, rows, depth)
            shape = (4, 4, *array.shape) if kind == "all" else shape
            self.outs.append(like(shape, array.dtype))
        self.slots = 30 * len(tasks)

    def local(self):
        return [pltpu.SemaphoreType.DMA((max(len(self.tasks), 1),))]

    def peers(self, net):
        found = []
        for kind, _, _ in self.tasks:
            if kind == "x":
                found += [net.on_x(1), net.on_x(3)]
            elif kind == "z":
                found += [net.on_z(1), net.on_z(3)]
            elif kind == "all":
                found += [net.on_x(1), net.on_x(3), net.on_z(1), net.on_z(3)]
            else:
                found += [net.on_zl(1), net.on_core()]
        return found

    def stages(self, net, base, ins, outs, local):
        return [
            self.stage(net, base + 30 * t, kind, ins[t], outs[t], step, local.at[t])
            for t, (kind, _, step) in enumerate(self.tasks)
        ]

    def stage(self, net, base, kind, src, out, step, local):
        if kind == "basis":
            rows = out.shape[1]
            for _ in range((0, 2, 1)[step]):
                yield
            net.send(base, src.at[pl.ds(rows * step, rows)], out.at[0], net.on_zl(1))
            yield
            yield
            net.recv(base, out.at[0])
            net.send(base + 1, out.at[0], out.at[1], net.on_core())
            yield
            net.recv(base + 1, out.at[1])
            return
        if kind == "all":
            copy = pltpu.make_async_copy(src, out.at[net.z, net.x], local)
            copy.start()
            slot = lambda o, i, h: out.at[o, i, h]
            own = lambda h: src.at[h]
            yield from gather_stage(net, base, own, slot, 4, net.z, net.x, net.on_z, net.on_x)
            copy.wait()
            return
        half = out.shape[1] // 2
        cut = lambda h: pl.ds(h * half, half)
        row = src if len(src.shape) == 2 else src.at[turn(net.z, step, 4)]
        own = lambda h: row.at[cut(h)]
        slot = lambda i, h: out.at[i, cut(h)]
        if kind == "z":
            yield from ring(net, base, own, slot, net.z, net.on_z)
        else:
            yield from ring(net, base, own, slot, net.x, net.on_x)


def sems(slots):
    return [pltpu.SemaphoreType.DMA((slots,)), pltpu.SemaphoreType.DMA((slots,))]


def call(kernel, collective_id, outs, in_specs, out_specs, scratch, args, name, cost):
    return pl.pallas_call(
        kernel,
        out_shape=outs,
        in_specs=in_specs,
        out_specs=out_specs,
        scratch_shapes=scratch,
        compiler_params=pltpu.CompilerParams(
            collective_id=collective_id, has_side_effects=True, vmem_limit_bytes=60 << 20
        ),
        cost_estimate=pl.CostEstimate(flops=cost * 10**9, bytes_accessed=0, transcendentals=0),
        name=name,
    )(*args)


def like(shape, dtype):
    return jax.ShapeDtypeStruct(shape, dtype)


def exchange(arrays, pairs, tasks, collective_id, name, cost):
    na, np_, nt = len(arrays), len(pairs), len(tasks)
    side = Side(tasks)

    def kernel(*refs):
        ins, shared, side_in = refs[:na], refs[na : na + np_], refs[na + np_ : na + np_ + nt]
        refs = refs[na + np_ + nt :]
        outs, both, side_out = refs[:na], refs[na : na + np_], refs[na + np_ : na + np_ + nt]
        local, side_local, send_sem, recv_sem = refs[na + np_ + nt :]
        net = Net(send_sem, recv_sem)
        steps = [(dz, dx) for dz in range(4) for dx in range(4) if (dz, dx) != (0, 0)]
        steps.sort(key=lambda s: -(min(s[0], 4 - s[0]) * 2 + min(s[1], 4 - s[1])))

        def to(dz, dx):
            return turn(net.z, dz, 4) * 4 + turn(net.x, dx, 4)

        me = net.z * 4 + net.x
        peers = [{"wide": to(*s) * 2 + net.core} for s in steps]
        net.greet(peers + ([net.on_core()] if np_ else []) + side.peers(net))
        copies = []
        for j, s in enumerate(steps):
            for a in range(na):
                net.send(j * na + a, ins[a].at[to(*s)], outs[a].at[me], peers[j])
        for a in range(na):
            copies.append(pltpu.make_async_copy(ins[a].at[me], outs[a].at[me], local.at[a]))
        for b in range(np_):
            net.send(15 * na + b, shared[b], both[b], net.on_core())
        for copy in copies:
            copy.start()
        extra = side.stages(net, 15 * na + max(np_, 1), side_in, side_out, side_local)
        for _ in range(3):
            for stage in extra:
                next(stage)
        for j, (dz, dx) in enumerate(steps):
            source = to((4 - dz) % 4, (4 - dx) % 4)
            for a in range(na):
                net.recv(j * na + a, outs[a].at[source])
        for b in range(np_):
            net.recv(15 * na + b, both[b])
        drive(*extra)
        for copy in copies:
            copy.wait()
        net.finish()

    outs = [like(a.shape, a.dtype) for a in (*arrays, *pairs)]
    return call(
        kernel,
        collective_id,
        outs + side.outs,
        [ANY] * (na + np_ + nt),
        [ANY] * (na + np_ + nt),
        [
            pltpu.SemaphoreType.DMA((na,)),
            *side.local(),
            *sems(15 * na + max(np_, 1) + side.slots),
        ],
        (*arrays, *pairs, *side.arrays),
        name,
        cost,
    )


def reduce_over(wide_parts, narrow_parts, tasks, dtypes, collective_id, name, cost):
    parts = [*wide_parts, *narrow_parts]
    n, split, nt = len(parts), len(wide_parts), len(tasks)
    side = Side(tasks)
    slots = split * reduce_slots(4) + (n - split) * reduce_slots(2)

    def kernel(*refs):
        ins, side_in = refs[:n], refs[n : n + nt]
        outs, side_out = refs[n + nt : 2 * n + nt], refs[2 * n + nt : 2 * (n + nt)]
        buffers, (side_local, send_sem, recv_sem) = refs[2 * (n + nt) : -3], refs[-3:]
        net = Net(send_sem, recv_sem)
        sums = [Sum(ins[a], *buffers[6 * a : 6 * a + 6]) for a in range(n)]
        stages, ends, peers = [], [], []
        if split:
            peers += [net.on_x(1), net.on_x(3), net.on_z(1), net.on_z(3)]
            stage, end = reduce_stage(net, 0, sums[:split], 4, net.z, net.x, net.on_z, net.on_x)
            stages.append(stage)
            ends += end
        if n > split:
            peers += [net.on_y(1), net.on_y(3), net.on_zl(1)]
            base = split * reduce_slots(4)
            stage, end = reduce_stage(
                net, base, sums[split:], 2, net.zl, net.y, net.on_zl, net.on_y
            )
            stages.append(stage)
            ends += end
        net.greet(peers + side.peers(net))
        extra = side.stages(net, slots, side_in, side_out, side_local)
        drive(*stages, *extra)
        for a in range(n):
            for h in range(2):
                outs[a][sums[a].h(h), :] = ends[a](h).astype(outs[a].dtype)
        net.finish()

    scratch = []
    for p in parts:
        scratch += Sum.scratch(p.shape[0], p.shape[2], p.shape[3], p.dtype)
    return call(
        kernel,
        collective_id,
        [like(p.shape[2:], d) for p, d in zip(parts, dtypes)] + side.outs,
        [VMEM] * n + [ANY] * nt,
        [VMEM] * n + [ANY] * nt,
        [*scratch, *side.local(), *sems(slots + side.slots)],
        (*parts, *side.arrays),
        name,
        cost,
    )


def front(normed, inputs, unembed_own, basis_in_own, basis_own, ids, down, collective_id, name, cost):
    tokens, features = normed.shape[1:]
    half = features // 2
    vocab, width = unembed_own.shape[1], basis_in_own.shape[1]
    count = ids.shape[0] // 8
    side = Side([("z", down, 0), ("x", down, 0)])
    base_i = reduce_slots(4)
    base_p = base_i + reduce_slots(4)
    base_s = base_p + reduce_slots(2)
    base_g = base_s + 7
    base_t = base_g + gather_slots(4)
    base_x = base_t + side.slots

    def kernel(*refs):
        id_ref, nb_ref, ib_ref, u_ref, b_ref, basis_ref, d_ref = refs[:7]
        common_ref, rot_ref, picked_ref, other_ref, dz_ref, dx_ref = refs[7:13]
        n_ref, i_ref, unembed, basis_in, logit_part, input_part, pick_part = refs[13:20]
        sum_l, sum_i, sum_p = (refs[20 + 6 * j : 26 + 6 * j] for j in range(3))
        logits, mine, got, probs, every, local, send_sem, recv_sem = refs[38:]
        net = Net(send_sem, recv_sem)
        c, z, x = net.core, net.z, net.x
        my_rows, its_rows = (
            pl.ds(pl.multiple_of(o * half, half), half) for o in (c, 1 - c)
        )
        steps = [(dz, dx) for dz in range(4) for dx in range(4) if (dz, dx) != (0, 0)]
        steps.sort(key=lambda s: -(min(s[0], 4 - s[0]) * 2 + min(s[1], 4 - s[1])))
        peers = [
            {"wide": turn(z, dz, 4) * 8 + turn(x, dx, 4) * 2 + c} for dz, dx in steps
        ]
        narrow_peers = [{"narrow": turn(net.narrow, k, 8)} for k in range(1, 8)]
        all_here = net.call_out(peers + [net.on_core()] + narrow_peers)
        keeps = [
            pltpu.make_async_copy(nb_ref.at[z * 4 + x], n_ref.at[z, x], local.at[0]),
            pltpu.make_async_copy(ib_ref.at[z * 4 + x], i_ref.at[z, x], local.at[1]),
            pltpu.make_async_copy(u_ref, unembed.at[my_rows], local.at[2]),
            pltpu.make_async_copy(b_ref, basis_in.at[my_rows], local.at[3]),
        ]
        for keep in keeps:
            keep.start()
        all_here()

        def scatter(base, src, dst):
            for j, (dz, dx) in enumerate(steps):
                target = turn(z, dz, 4) * 4 + turn(x, dx, 4)
                net.send(base + j, src.at[target], dst.at[z, x], peers[j])

        scatter(base_x, nb_ref, n_ref)
        net.send(base_x + 30, u_ref, unembed.at[my_rows], net.on_core())
        scatter(base_x + 15, ib_ref, i_ref)
        net.send(base_x + 31, b_ref, basis_in.at[my_rows], net.on_core())
        net.send(base_x + 32, basis_ref, other_ref, net.on_core())

        def dot_row(base, left, keep, right, part):
            offsets = iter((2, 1, 3, 0))

            def run(row):
                offset = next(offsets)
                for j, (dz, dx) in enumerate(steps):
                    if (4 - dz) % 4 == offset:
                        net.recv(base + j, left.at[row, turn(x, (4 - dx) % 4, 4)])
                if offset == 0:
                    keep.wait()
                rows = left[row].reshape(4 * tokens, features)
                value = jnp.dot(rows, right[...], preferred_element_type=F32)
                part[row] = value.reshape(4, tokens, part.shape[3])

            return run

        keeps[2].wait()
        net.recv(base_x + 30, unembed.at[its_rows])
        main, (end,) = reduce_stage(
            net, 0, [Sum(logit_part, *sum_l)], 4, net.z, net.x, net.on_z, net.on_x,
            dot_row(base_x, n_ref, keeps[0], unembed, logit_part),
        )
        late, (end_i,) = reduce_stage(
            net, base_i, [Sum(input_part, *sum_i)], 4, net.z, net.x, net.on_z, net.on_x,
            dot_row(base_x + 15, i_ref, keeps[1], basis_in, input_part),
        )
        picks, (end_p,) = reduce_stage(
            net, base_p, [Sum(pick_part, *sum_p)], 2, net.zl, net.y, net.on_zl, net.on_y
        )

        def extra(t, out, kind, src, step):
            return side.stage(net, base_t + 30 * t, kind, src, out, step, None)

        ring_z = extra(0, dz_ref, "z", d_ref, 0)
        ring_x = extra(1, dx_ref, "x", d_ref, 0)

        def pick(j, carry):
            some = id_ref[pl.ds(pl.multiple_of(j * count, count), count)]
            one = some == lax.broadcasted_iota(jnp.int32, (count, vocab), 1)
            value = contract_last(jnp.where(one, 1.0, 0.0).astype(BF16), unembed[...])
            pick_part[lax.div(j, 4), lax.rem(j, 4)] = value.astype(BF16)
            return carry

        next(main)
        next(ring_z)
        for j in range(4):
            lax.fori_loop(2 * j, 2 * j + 2, pick, 0)
            if j == 3:
                next(picks)
            next(main)
        keeps[3].wait()
        net.recv(base_x + 31, basis_in.at[its_rows])
        next(late)
        next(ring_x)
        next(ring_x)
        next(picks)
        drive(main)
        next(ring_z)
        for h in range(2):
            logits[pl.ds(h * (tokens // 2), tokens // 2), :] = end(h)
        top = jnp.max(logits[...], axis=1, keepdims=True)
        mine[0] = jnp.broadcast_to(top, (tokens, 128))
        mine[1] = jnp.broadcast_to(
            jnp.sum(jnp.exp(logits[...] - top), axis=1, keepdims=True), (tokens, 128)
        )
        for k in range(7):
            net.send(base_s + k, mine, got.at[k], narrow_peers[k])
        next(late)
        for k in range(7):
            net.recv(base_s + k, got.at[k])
        largest = mine[0]
        for k in range(7):
            largest = jnp.maximum(largest, got[k, 0])
        total = mine[1] * jnp.exp(mine[0] - largest)
        for k in range(7):
            total += got[k, 1] * jnp.exp(got[k, 0] - largest)
        value = (jnp.exp(logits[...] - largest[:, :1]) / total[:, :1]).astype(BF16)
        probs[...] = value.reshape(2, tokens // 2, vocab)
        every[net.z, net.x] = value.reshape(2, tokens // 2, vocab)
        slot = lambda o, i, h: every.at[o, i, h]
        own = lambda h: probs.at[h]
        spread = gather_stage(
            net, base_g, own, slot, 4, net.z, net.x, net.on_z, net.on_x
        )
        next(spread)
        next(ring_x)
        next(late)
        next(ring_z)
        next(spread)
        next(late)
        next(picks)
        next(spread)
        next(late)
        next(spread)
        for step in (0, 3, 1, 2):
            next(spread)
            row = turn(net.z, step, 4)
            common_ref[row] = contract_last(every[row].reshape(4 * tokens, vocab), unembed[...])
        drive(late)
        drive(spread)
        for h in range(2):
            rot_ref[h] = end_i(h).astype(BF16)
        drive(picks)
        for h in range(2):
            picked_ref[pl.ds(h * (count // 2), count // 2), :] = end_p(h).astype(BF16)
        drive(ring_x, ring_z)
        net.recv(base_x + 32, other_ref)
        net.finish()

    return call(
        kernel,
        collective_id,
        [
            like((4, 4 * tokens, features), F32),
            like((2, tokens // 2, width), BF16),
            like((count, features), BF16),
            like(basis_own.shape, BF16),
            *side.outs,
        ],
        [VMEM] + [ANY] * 6,
        [VMEM] * 3 + [ANY] * 3,
        [
            pltpu.VMEM((4, 4, tokens, features), BF16),
            pltpu.VMEM((4, 4, tokens, features), BF16),
            pltpu.VMEM((features, vocab), BF16),
            pltpu.VMEM((features, width), BF16),
            pltpu.VMEM((4, 4, tokens, vocab), F32),
            pltpu.VMEM((4, 4, tokens, width), F32),
            pltpu.VMEM((2, 4, count, features), BF16),
            *Sum.scratch(4, tokens, vocab, F32),
            *Sum.scratch(4, tokens, width, F32),
            *Sum.scratch(2, count, features, BF16),
            pltpu.VMEM((tokens, vocab), F32),
            pltpu.VMEM((2, tokens, 128), F32),
            pltpu.VMEM((7, 2, tokens, 128), F32),
            pltpu.VMEM((2, tokens // 2, vocab), BF16),
            pltpu.VMEM((4, 4, 2, tokens // 2, vocab), BF16),
            pltpu.SemaphoreType.DMA((4,)),
            *sems(base_x + 33),
        ],
        (ids, normed, inputs, unembed_own, basis_in_own, basis_own, down),
        name,
        cost,
    )


def gather_back(shard, tasks, collective_id, name, cost):
    _, rows, features = shard.shape
    side, nt = Side(tasks), len(tasks)

    def kernel(*refs):
        x_ref, side_in, o_ref, side_out = refs[0], refs[1 : 1 + nt], refs[1 + nt], refs[2 + nt : -5]
        mine, local, side_local, send_sem, recv_sem = refs[-5:]
        net = Net(send_sem, recv_sem)
        net.greet([net.on_y(1), net.on_y(3), net.on_zl(1), net.on_core()] + side.peers(net))
        net.send(0, x_ref.at[1 - net.core], mine, net.on_core())
        slot = lambda o, i, h: o_ref.at[o, i, lax.rem(net.core + h, 2)]
        own = lambda h: mine if h else x_ref.at[net.core]
        net.recv(0, mine)
        copies = [
            pltpu.make_async_copy(own(h), slot(net.zl, net.y, h), local.at[h]) for h in range(2)
        ]
        for copy in copies:
            copy.start()
        drive(
            gather_stage(net, 1, own, slot, 2, net.zl, net.y, net.on_zl, net.on_y),
            *side.stages(net, 1 + gather_slots(2), side_in, side_out, side_local),
        )
        for copy in copies:
            copy.wait()
        net.finish()

    return call(
        kernel,
        collective_id,
        [like((2, 4, 2, rows, features), shard.dtype)] + side.outs,
        [ANY] * (1 + nt),
        [ANY] * (1 + nt),
        [
            pltpu.VMEM((rows, features), shard.dtype),
            pltpu.SemaphoreType.DMA((2,)),
            *side.local(),
            *sems(1 + gather_slots(2) + side.slots),
        ],
        (shard, *side.arrays),
        name,
        cost,
    )


def rotate_all(back, gate, down, down_z, downs, bases, thirds, inputs, collective_id, name, cost):
    tokens, depth = gate.shape
    columns = bases[0].shape[0]
    width = inputs.shape[2]
    rows = 2 * tokens
    features = back.shape[2]
    cuts = (pl.ds(0, 896), pl.ds(896, depth - 896))

    def kernel(*refs):
        back_ref, g_ref, i_ref, own_ref, z_ref, d_refs = *refs[:5], refs[5:9]
        b_refs, t_refs, o_ref = refs[9:11], refs[11:14], refs[14]
        down, bases, h_ref, ours_in, j_ref, spun, pairs, corrected = refs[15:23]
        half_in, gated, other, every, part, fwd, mid, got, mine = refs[23:32]
        local, send_sem, recv_sem = refs[32:]
        net = Net(send_sem, recv_sem)
        c, z, x, zl, y = net.core, net.z, net.x, net.zl, net.y
        base_z, base_r, base_n, base_i = 8, 40, 64, 136
        loads = []
        for k in range(4):
            block = z_ref.at[turn(z, k, 4)] if k else own_ref
            loads.append(pltpu.make_async_copy(block, down.at[k, x], local.at[16 + 4 * k]))
            for step in range(1, 4):
                at = turn(x, step, 4)
                loads.append(
                    pltpu.make_async_copy(
                        d_refs[k].at[at], down.at[k, at], local.at[16 + 4 * k + step]
                    )
                )
        loads += [
            pltpu.make_async_copy(b_refs[m], bases.at[m], local.at[8 + m]) for m in range(2)
        ]
        third = columns // 3
        for j in range(3):
            for m in range(2):
                loads.append(
                    pltpu.make_async_copy(
                        t_refs[j].at[m],
                        bases.at[2 + m, pl.ds(j * third, third)],
                        local.at[10 + 2 * j + m],
                    )
                )
        ones = [net.on_x(1), net.on_x(3), net.on_z(1), net.on_z(3)]
        all_here = net.call_out(ones + [net.on_y(1), net.on_y(3), net.on_zl(1), net.on_core()])
        for load in loads[:16]:
            load.start()
        quarter = features // 4
        left = back_ref[...].reshape(2 * 4 * tokens, features)
        for j, cut in enumerate(cuts):
            total = None
            for k in range(4):
                if j == 0:
                    for load in loads[4 * k : 4 * k + 4]:
                        load.wait()
                right = down[k, :, :, cut].reshape(quarter, cut.size)
                term = jnp.dot(
                    left[:, k * quarter : (k + 1) * quarter], right, preferred_element_type=F32
                )
                total = term if total is None else total + term
            h_ref[:, :, cut] = total.reshape(2, 4 * tokens, cut.size)
        for load in loads[16:]:
            load.start()
        all_here()
        theirs, ours = (
            pl.ds(pl.multiple_of(2 * tokens * o, 2 * tokens), 2 * tokens) for o in (1 - zl, zl)
        )
        net.send(0, h_ref.at[1 - c, theirs], half_in.at[theirs], net.on_core())
        net.send(7, h_ref.at[1 - c, ours], half_in.at[ours], net.on_core())
        ours_in[z, x] = i_ref[...]
        inputs_stage = gather_stage(
            net, base_i, lambda h: i_ref.at[h], lambda o, i, h: ours_in.at[o, i, h],
            4, z, x, net.on_z, net.on_x,
        )
        next(inputs_stage)

        def gate_rows(s):
            some = pl.ds(pl.multiple_of(s * tokens, tokens), tokens)
            value = (h_ref[c, some] + half_in[some]) * g_ref[...].astype(F32)
            gated[s] = value.astype(BF16)

        net.recv(0, half_in.at[theirs])
        for s in range(2):
            gate_rows(2 * (1 - zl) + s)
        net.send(2, gated.at[pl.ds(2 * (1 - zl), 2)], other, net.on_zl(1))
        next(inputs_stage)
        net.recv(7, half_in.at[ours])
        for s in range(2):
            gate_rows(2 * zl + s)

        own = lambda h: other if h else gated.at[pl.ds(2 * zl, 2)]
        slot = lambda o, i, h: every.at[o, h, i]
        zp, zm, z2 = (turn(z, s, 4) for s in (1, 3, 2))
        xp, xm, x2 = (turn(x, s, 4) for s in (1, 3, 2))
        yp, ym, y2 = (turn(y, s, 4) for s in (1, 3, 2))
        order = (z, zm, zp, z2)
        inner = lambda row: base_z + 6 + 6 * row

        def along(row, h):
            o, b = order[row], inner(row)
            src = own(h) if row == 0 else slot(o, x, h)
            net.send(b + h, src, slot(o, x, h), net.on_x(1))
            net.send(b + 3 - h, src, slot(o, x, h), net.on_x(3))

        def forward(row, ways=(0, 1)):
            o, b = order[row], inner(row)
            if 0 in ways:
                net.recv(b, slot(o, xm, 0))
                net.send(b + 4, slot(o, xm, 0), slot(o, xm, 0), net.on_x(1))
            if 1 in ways:
                net.recv(b + 2, slot(o, xp, 1))
                net.send(b + 5, slot(o, xp, 1), slot(o, xp, 1), net.on_x(3))

        def rest(row):
            o, b = order[row], inner(row)
            net.recv(b + 1, slot(o, xm, 1))
            net.recv(b + 3, slot(o, xp, 0))
            net.recv(b + 4, slot(o, x2, 0))
            net.recv(b + 5, slot(o, x2, 1))

        def multiply(row):
            o = order[row]
            for m in range(2):
                block = None
                for h in range(2):
                    left = every[o, h].reshape(4 * rows, depth)
                    term = contract_last(left, bases[2 * h + m])
                    block = term if block is None else block + term
                part[row, :, m] = block.reshape(4, rows, columns)

        def reduce_start(k):
            b = base_r + 6 * k
            net.send(b, part.at[k, y2, 0], fwd.at[k, 0], net.on_y(1))
            net.send(b + 1, part.at[k, y2, 1], fwd.at[k, 1], net.on_y(3))
            net.send(b + 2, part.at[k, yp, 1], got.at[k, 0, 1], net.on_y(1))
            net.send(b + 3, part.at[k, ym, 0], got.at[k, 1, 0], net.on_y(3))

        def reduce_middle(k):
            b = base_r + 6 * k
            net.recv(b, fwd.at[k, 0])
            mid[k, 0] = part[k, yp, 0] + fwd[k, 0]
            net.send(b + 4, mid.at[k, 0], got.at[k, 0, 0], net.on_y(1))
            net.recv(b + 1, fwd.at[k, 1])
            mid[k, 1] = part[k, ym, 1] + fwd[k, 1]
            net.send(b + 5, mid.at[k, 1], got.at[k, 1, 1], net.on_y(3))

        def reduce_end(k):
            b = base_r + 6 * k
            net.recv(b + 2, got.at[k, 0, 1])
            net.recv(b + 5, got.at[k, 1, 1])
            value = part[k, y, 1] + got[k, 0, 1] + got[k, 1, 1]
            mine[k, 1] = value.astype(BF16).reshape(2, tokens, columns)
            net.send(3 + k, mine.at[k, 1], mine.at[k, 2], net.on_core())
            net.recv(b + 3, got.at[k, 1, 0])
            net.recv(b + 4, got.at[k, 0, 0])
            value = part[k, y, 0] + got[k, 0, 0] + got[k, 1, 0]
            mine[k, 0] = value.astype(BF16).reshape(2, tokens, columns)

        def square(k, stage):
            drive(stage)
            if k == 0:
                net.recv(1, j_ref)
            e = order[k]
            pairs[:, : 4 * tokens] = ours_in[e].reshape(4 * tokens, width).T
            pairs[:, 4 * tokens :] = j_ref[e].reshape(4 * tokens, width).T

            def tile(t, carry):
                cut = pl.ds(pl.multiple_of(t * 128, 128), 128)
                total = None
                for o in range(2):
                    for s in range(2):
                        right = spun[k, o, s].reshape(8 * tokens, columns)
                        block = jnp.dot(pairs[cut], right, preferred_element_type=F32)
                        block = block * block
                        total = block if total is None else total + block
                total = total * (1.0 / 16.0)
                corrected[cut] = total if k == 0 else corrected[cut] + total
                return carry

            lax.fori_loop(0, width // 128, tile, 0)

        def spread(k):
            mine_k = lambda h: mine.at[k, 2 * h]
            place = lambda o, i, h: spun.at[k, o, :, h, i]
            net.recv(3 + k, mine.at[k, 2])
            for h in range(2):
                spun[k, zl, :, h, y] = mine[k, 2 * h]
            base = base_n + gather_slots(2) * k
            return gather_stage(net, base, mine_k, place, 2, zl, y, net.on_zl, net.on_y)

        net.send(base_z, own(0), slot(z, x, 0), net.on_z(1))
        net.send(base_z + 3, own(0), slot(z, x, 0), net.on_z(3))
        along(0, 0)
        next(inputs_stage)
        net.recv(2, other)
        net.send(base_z + 2, own(1), slot(z, x, 1), net.on_z(3))
        net.send(base_z + 1, own(1), slot(z, x, 1), net.on_z(1))
        along(0, 1)
        copies = [pltpu.make_async_copy(own(h), slot(z, x, h), local.at[h]) for h in range(2)]
        for copy in copies:
            copy.start()
        drive(inputs_stage)
        net.send(1, ours_in, j_ref, net.on_core())
        net.recv(base_z, slot(zm, x, 0))
        net.send(base_z + 4, slot(zm, x, 0), slot(zm, x, 0), net.on_z(1))
        net.recv(base_z + 2, slot(zp, x, 1))
        net.send(base_z + 5, slot(zp, x, 1), slot(zp, x, 1), net.on_z(3))
        forward(0)
        along(1, 0)
        net.recv(base_z + 1, slot(zm, x, 1))
        along(1, 1)
        rest(0)
        for copy in copies + loads[16:]:
            copy.wait()
        multiply(0)
        reduce_start(0)
        forward(1)
        along(2, 1)
        net.recv(base_z + 3, slot(zp, x, 0))
        along(2, 0)
        reduce_middle(0)
        rest(1)
        last = inner(3)
        net.send(last + 1, slot(zm, xp, 1), slot(zm, xp, 1), net.on_z(1))
        net.send(last + 2, slot(zm, xm, 1), slot(zm, xm, 1), net.on_z(1))
        reduce_end(0)
        multiply(1)
        reduce_start(1)
        spread_0 = spread(0)
        next(spread_0)
        forward(2)
        net.recv(base_z + 4, slot(z2, x, 0))
        along(3, 0)
        reduce_middle(1)
        next(spread_0)
        rest(2)
        net.send(last + 5, slot(zp, x2, 1), slot(zp, x2, 1), net.on_z(3))
        reduce_end(1)
        multiply(2)
        reduce_start(2)
        spread_1 = spread(1)
        next(spread_1)
        next(spread_0)
        forward(3, (0,))
        reduce_middle(2)
        next(spread_1)
        net.recv(base_z + 5, slot(z2, x, 1))
        net.recv(last + 3, slot(z2, xp, 0))
        net.recv(last + 4, slot(z2, x2, 0))
        net.recv(last + 1, slot(z2, xp, 1))
        net.recv(last + 2, slot(z2, xm, 1))
        net.recv(last + 5, slot(z2, x2, 1))
        multiply(3)
        reduce_start(3)
        reduce_end(2)
        spread_2 = spread(2)
        next(spread_2)
        next(spread_1)
        reduce_middle(3)
        square(0, spread_0)
        next(spread_2)
        reduce_end(3)
        spread_3 = spread(3)
        next(spread_3)
        next(spread_2)
        square(1, spread_1)
        next(spread_3)
        next(spread_3)
        square(2, spread_2)
        square(3, spread_3)
        o_ref[...] = corrected[...].T
        net.finish()

    return call(
        kernel,
        collective_id,
        like((columns, width), F32),
        [VMEM] * 3 + [ANY] * 11,
        VMEM,
        [
            pltpu.VMEM((4, 4, features // 16, depth), BF16),
            pltpu.VMEM((4, columns, depth), BF16),
            pltpu.VMEM((2, 4 * tokens, depth), F32),
            pltpu.VMEM((4, 4, *inputs.shape), BF16),
            pltpu.VMEM((4, 4, *inputs.shape), BF16),
            pltpu.VMEM((4, 2, 2, 2, 4, tokens, columns), BF16),
            pltpu.VMEM((width, 8 * tokens), BF16),
            pltpu.VMEM((width, columns), F32),
            pltpu.VMEM((4 * tokens, depth), F32),
            pltpu.VMEM((4, tokens, depth), BF16),
            pltpu.VMEM((2, tokens, depth), BF16),
            pltpu.VMEM((4, 2, 4, 2, tokens, depth), BF16),
            pltpu.VMEM((4, 4, 2, rows, columns), F32),
            pltpu.VMEM((4, 2, rows, columns), F32),
            pltpu.VMEM((4, 2, rows, columns), F32),
            pltpu.VMEM((4, 2, 2, rows, columns), F32),
            pltpu.VMEM((4, 3, 2, tokens, columns), BF16),
            pltpu.SemaphoreType.DMA((32,)),
            *sems(64 + 4 * gather_slots(2) + gather_slots(4)),
        ],
        (back, gate, inputs, down, down_z, *downs, *bases, *thirds),
        name,
        cost,
    )


def contract_last(left, right):
    return lax.dot_general(left, right, (((1,), (1,)), ((), ())), preferred_element_type=F32)


def per_device(
    resid, final_gain, unembed, labels, layer_in, gate_value, down_weight, basis_in, basis_out
):
    wide, narrow = lax.axis_index("wide"), lax.axis_index("narrow")
    core = lax.rem(wide, 2)
    tokens, width = resid.shape
    samples = labels.shape[1]
    vocab, part = unembed.shape
    hidden = down_weight.shape[0]
    width_in = basis_in.shape[1]
    pair = 2 * part
    core_tokens = 16 * tokens
    few = tokens // 8

    resid_float = resid.astype(F32)
    inverse = lax.rsqrt(jnp.mean(resid_float * resid_float, axis=1) + EPSILON)
    normed = (resid_float * inverse[:, None] * final_gain).astype(BF16)

    def blocks(rows):
        return rows.reshape(tokens, 16, pair).transpose(1, 0, 2)

    down, basis = down_weight.T, basis_out.T
    mine = lax.dynamic_index_in_dim(
        labels.reshape(16, 2, 8, few, samples), core, 1, keepdims=False
    )
    shifted = mine.transpose(1, 0, 2, 3).reshape(core_tokens * samples, 1) - narrow * vocab
    common, inputs_rot, picked, basis_other, down_z, down_0 = front(
        blocks(normed),
        blocks(layer_in),
        unembed.T,
        basis_in,
        basis,
        shifted,
        down,
        1,
        "front",
        120,
    )
    common = common.reshape(16, 8, few, pair).transpose(1, 0, 2, 3).reshape(2, 4, 16 * few, pair)
    common, down_1, third_0, third_1 = reduce_over(
        [],
        [common],
        [("x", down_z, 1), ("basis", basis, 0), ("basis", basis, 1)],
        [F32],
        4,
        "reduce_common",
        30,
    )
    grads = common.reshape(16, few, 1, pair) - picked.astype(F32).reshape(16, few, samples, pair)
    grads, down_2 = exchange(
        [grads.reshape(16, few * samples, pair)],
        [],
        [("x", down_z, 2)],
        5,
        "exchange_grads",
        20,
    )
    grads = grads.transpose(1, 0, 2).reshape(few, samples, width)
    resid_few = lax.dynamic_slice_in_dim(resid_float, narrow * few, few, 0)
    inverse_few = lax.dynamic_slice_in_dim(inverse, narrow * few, few, 0)
    inner = jnp.sum(final_gain * grads * resid_few[:, None, :], axis=2)
    back = (
        inverse_few[:, None, None] * final_gain * grads
        - resid_few[:, None, :] * (inverse_few**3)[:, None, None] * inner[:, :, None] / width
    )
    back = back.astype(BF16).reshape(few * samples, 4, 4, 2, part).transpose(3, 0, 1, 2, 4)
    back = lax.dynamic_slice_in_dim(
        jnp.concatenate([back, back], axis=2), lax.div(wide, 8), 4, axis=2
    )
    back, down_3, third_2 = gather_back(
        back.reshape(2, few * samples, width // 2),
        [("x", down_z, 3), ("basis", basis, 2)],
        6,
        "gather_back",
        20,
    )
    back = back.reshape(8, 2, few, samples, width // 2).transpose(1, 3, 0, 2, 4)
    return rotate_all(
        back.reshape(2, samples * tokens, width // 2),
        gate_value,
        down,
        down_z,
        [down_0, down_1, down_2, down_3],
        [basis, basis_other],
        [third_0, third_1, third_2],
        inputs_rot,
        7,
        "rotate_all",
        110,
    )


def solution(mesh):
    in_specs = (
        P("wide", None),
        P(),
        P("narrow", "wide"),
        P(),
        P("wide", None),
        P("wide", "narrow"),
        P("narrow", "wide"),
        P("wide", "narrow"),
        P("narrow", "wide"),
    )
    out_specs = P("wide", "narrow")
    return jax.shard_map(
        per_device, mesh=mesh, in_specs=in_specs, out_specs=out_specs, check_vma=False
    )
```
